512 devices in a mesh: seq: 64 (over z_hi, y, x, core), chan: 8 (over z_lo).
Axes of the slice: x: 4, y: 4, z: 16 (z_hi: 2, z_lo: 8; z = z_hi * 8 + z_lo), core: 2. Of those that a mesh axis runs over, the one named last changes fastest.
Arguments:
- query_in: bfloat16 [2048, 8192], P('chan', 'seq'), may hold values from -6 to 6
- key_in: bfloat16 [2048, 8192], P('chan', 'seq'), may hold values from -6 to 6
- value_in: bfloat16 [2048, 8192], P('chan', 'seq'), may hold values from -6 to 6
- short_weight: float32 [3, 7, 2048], P(None, None, 'chan'), may hold values from -2 to 2
- residue: float32 [2048, 16], P(('chan', 'seq')), may hold values from -1.5 to 1.5
- log_rate: float32 [2048, 16], P(('chan', 'seq')), may hold values from -13 to -3.2
- grad_out: bfloat16 [2048, 8192], P('chan', 'seq'), may hold values from -6 to 6
Outputs:
- output: bfloat16 [2048, 8192], P('chan', 'seq')
- grad_query: bfloat16 [2048, 8192], P('chan', 'seq')
- grad_key: bfloat16 [2048, 8192], P('chan', 'seq')
- grad_value: bfloat16 [2048, 8192], P('chan', 'seq')
- grad_short: float32 [3, 7, 2048], P(None, None, 'chan')
- grad_residue: float32 [2048, 16], P(('chan', 'seq'))
- grad_log_rate: float32 [2048, 16], P(('chan', 'seq'))
The draws below stay inside these ranges and needn't reach their ends.
All inputs are finite; a program needn't handle non-finite values.
Results may differ from the reference program's by a relative error of at most 0.008.
Values may be sent and summed in bfloat16 or wider, within the bound.
No kernel may reach another device: no remote copies, remote signals or barrier semaphores. Data moves between devices by JAX's collectives and lax.ppermute only.
A program may use at most 64 MiB of HBM per device.

```python
import math
import jax
import jax.numpy as jnp
from jax import lax

D = 2048
MODES = 16
LENGTH = 8192


def levels(own_key, extent, pieces, least, top_value):
    level, own = 1.0, jax.random.fold_in(own_key, 6)
    for position, blocks in pieces:
        heights = jnp.exp(jax.random.uniform(jax.random.fold_in(own, position), (blocks,), jnp.float32, least / len(pieces), top_value / len(pieces)))
        level = level * jnp.repeat(heights, extent[position] // blocks).reshape([-1 if axis == position else 1 for axis in range(len(extent))])
    return level


def scatter_about(own_key, shape, spread, bound, split=(), held_as=jnp.bfloat16):
    values = jax.random.normal(own_key, shape, jnp.float32) * spread
    if len(split) > 0:
        values = levels(own_key, shape, split, -0.22, 0.18) * values
    return jnp.clip(values, min=-bound, max=bound).astype(held_as)


def setup_inputs(seed: int = 0) -> dict:
    seeds = jax.random.split(jax.random.key(seed), 8)
    return {
        "query_in": scatter_about(seeds[0], (D, LENGTH), 1.0, 6.0, ((0, 8), (1, 64))),
        "key_in": scatter_about(seeds[1], (D, LENGTH), 1.0, 6.0, ((0, 8), (1, 64))),
        "value_in": scatter_about(seeds[2], (D, LENGTH), 1.0, 6.0, ((0, 8), (1, 64))),
        "short_weight": scatter_about(seeds[3], (3, 7, D), 7 ** -0.5, 2.0, ((2, 8),), jnp.float32),
        "residue": scatter_about(seeds[4], (D, MODES), MODES ** -0.5, 1.5, ((0, 512),), jnp.float32),
        "log_rate": jnp.clip(-13.0 + 9.8 * jax.random.uniform(seeds[5], (D, MODES), jnp.float32) ** levels(seeds[5], (D, MODES), ((0, 512),), -0.2, 0.2), -13.0, -3.2),
        "grad_out": scatter_about(seeds[6], (D, LENGTH), 1.0, 6.0, ((0, 8), (1, 64))),
    }


def causal_taps(signal, taps):
    length = signal.shape[1]
    padded = jnp.pad(signal, ((0, 0), (6, 0)))
    total = jnp.zeros_like(signal)
    for offset in range(7):
        total = total + taps[offset][:, None] * padded[:, 6 - offset:6 - offset + length]
    return total

def causal_taps_back(gradient, taps):
    length = gradient.shape[1]
    padded = jnp.pad(gradient, ((0, 0), (0, 6)))
    total = jnp.zeros_like(gradient)
    for offset in range(7):
        total = total + taps[offset][:, None] * padded[:, offset:offset + length]
    return total

def taps_gradient(gradient, signal):
    length = signal.shape[1]
    padded = jnp.pad(signal, ((0, 0), (6, 0)))
    rows_out = [lax.optimization_barrier(jnp.sum(gradient * padded[:, 6 - offset:6 - offset + length], axis=1)) for offset in range(7)]
    return jnp.stack(rows_out, axis=0)

def modal_filter(residue, log_rate, length):
    decay_rate = jnp.exp(log_rate)
    offsets = jnp.arange(length).astype(residue.dtype)
    filt = jnp.zeros((residue.shape[0], length), residue.dtype)
    for mode_index in range(residue.shape[1]):
        factor = residue[:, mode_index] * jnp.sqrt(2.0 * decay_rate[:, mode_index])
        filt = filt + factor[:, None] * jnp.exp(-decay_rate[:, mode_index][:, None] * offsets)
    return filt

def modal_grads(filt_grad, residue, log_rate):
    decay_rate = jnp.exp(log_rate)
    offsets = jnp.arange(filt_grad.shape[1]).astype(residue.dtype)
    res_terms = []
    log_terms = []
    for mode_index in range(residue.shape[1]):
        rate_col = decay_rate[:, mode_index][:, None]
        basis = jnp.sqrt(2.0 * rate_col) * jnp.exp(-rate_col * offsets)
        weighted = filt_grad * basis
        res_terms.append(lax.optimization_barrier(jnp.sum(weighted, axis=1)))
        log_terms.append(residue[:, mode_index] * lax.optimization_barrier(jnp.sum(weighted * (0.5 - rate_col * offsets), axis=1)))
    return (jnp.stack(res_terms, axis=1), jnp.stack(log_terms, axis=1))

def long_block(items):
    mixed_blk, grad_blk, residue_blk, rate_blk = items
    length = mixed_blk.shape[1]
    fft_len = 2 * length
    filt = modal_filter(residue_blk, rate_blk, length)
    spec_mixed = jnp.fft.rfft(mixed_blk, n=fft_len, axis=1)
    spec_filter = jnp.fft.rfft(filt, n=fft_len, axis=1)
    spec_grad = jnp.fft.rfft(grad_blk, n=fft_len, axis=1)
    long_out = jnp.fft.irfft(spec_mixed * spec_filter, n=fft_len, axis=1)[:, :length]
    long_grad = jnp.fft.irfft(spec_grad * jnp.conj(spec_filter), n=fft_len, axis=1)[:, :length]
    filt_grad = jnp.fft.irfft(spec_grad * jnp.conj(spec_mixed), n=fft_len, axis=1)[:, :length]
    grad_res, grad_log = modal_grads(filt_grad, residue_blk, rate_blk)
    return (long_out.astype(jnp.bfloat16), long_grad.astype(jnp.bfloat16), grad_res, grad_log)

def reference(query_in, key_in, value_in, short_weight, residue, log_rate, grad_out):
    width, length = query_in.shape
    query_wide = query_in.astype(jnp.float32)
    key_wide = key_in.astype(jnp.float32)
    value_wide = value_in.astype(jnp.float32)
    query_hat = causal_taps(query_wide, short_weight[0])
    key_hat = causal_taps(key_wide, short_weight[1])
    value_hat = causal_taps(value_wide, short_weight[2])
    mixed = (key_hat * value_hat).astype(jnp.bfloat16)
    grad_up = grad_out.astype(jnp.float32)
    grad_mixed = (grad_up * query_hat).astype(jnp.bfloat16)
    blocks = 16
    per_block = width // blocks
    long_out, long_grad, grad_res, grad_log = lax.map(long_block, (mixed.astype(jnp.float32).reshape(blocks, per_block, length), grad_mixed.astype(jnp.float32).reshape(blocks, per_block, length), residue.reshape(blocks, per_block, residue.shape[1]), log_rate.reshape(blocks, per_block, residue.shape[1])))
    long_out = long_out.reshape(width, length).astype(jnp.float32)
    long_grad = long_grad.reshape(width, length).astype(jnp.float32)
    scale = 1.0 / math.sqrt(length)
    grad_residue = grad_res.reshape(width, -1) * scale
    grad_log_rate = grad_log.reshape(width, -1) * scale
    output = (query_hat * long_out).astype(jnp.bfloat16)
    grad_q = grad_up * long_out
    grad_k = long_grad * value_hat
    grad_v = long_grad * key_hat
    grad_query = causal_taps_back(grad_q, short_weight[0]).astype(jnp.bfloat16)
    grad_key = causal_taps_back(grad_k, short_weight[1]).astype(jnp.bfloat16)
    grad_value = causal_taps_back(grad_v, short_weight[2]).astype(jnp.bfloat16)
    grad_short = jnp.stack([taps_gradient(grad_q, query_wide), taps_gradient(grad_k, key_wide), taps_gradient(grad_v, value_wide)], axis=0) * scale
    return (output, grad_query, grad_key, grad_value, grad_short, grad_residue, grad_log_rate)
```

```python
import math

import jax
import jax.numpy as jnp
from jax import lax
from jax.experimental import pallas as pl
from jax.experimental.pallas import tpu as pltpu
from jax.sharding import PartitionSpec as P

TAPS = 7
MODES = 16
PAD = 8
ROWS_IN = 16
ROWS_OUT = 24
VMEM_LIMIT = 40 * 1024 * 1024


def pack_kernel(query_ref, key_ref, value_ref, grad_ref, send_ref, wide, mixed_rows):
    owners = send_ref.shape[0]
    for stream, ref in enumerate((query_ref, key_ref, value_ref, grad_ref)):
        wide[...] = ref[...].astype(jnp.float32)
        for chan in range(4):
            mixed_rows[pl.ds(stream * 4 + chan, owners, stride=ROWS_IN), :] = wide[
                pl.ds(chan, owners, stride=4), :
            ]
    send_ref[...] = mixed_rows[...].reshape(send_ref.shape).astype(jnp.bfloat16)


def unpack_kernel(recv_ref, out_ref, gq_ref, gk_ref, gv_ref, short_ref, rows, wide):
    owners = recv_ref.shape[0]
    rows[...] = recv_ref[...].reshape(rows.shape).astype(jnp.float32)
    for stream, ref in enumerate((out_ref, gq_ref, gk_ref, gv_ref)):
        for chan in range(4):
            wide[pl.ds(chan, owners, stride=4), :] = rows[
                pl.ds(stream * 4 + chan, owners, stride=ROWS_OUT), :
            ]
        ref[...] = wide[...].astype(jnp.bfloat16)
    for chan in range(4):
        wide[pl.ds(chan, owners, stride=4), :] = (
            rows[pl.ds(16 + chan, owners, stride=ROWS_OUT), :]
            + rows[pl.ds(20 + chan, owners, stride=ROWS_OUT), :]
        )
    short_ref[...] = wide[...].T[: short_ref.shape[0], :]


def main_kernel(
    recv_ref,
    prm_ref,
    send_ref,
    modal_ref,
    raw,
    xt,
    hat,
    mixed,
    gmixed,
    part_y,
    part_z,
    states,
    grads,
    sums,
    out_rows,
):
    chunks = recv_ref.shape[0]
    toks = recv_ref.shape[2]
    lanes = 4 * chunks
    scale = 1.0 / math.sqrt(chunks * toks)
    f32 = jnp.float32
    lane_chunk = lax.broadcasted_iota(jnp.int32, (8, lanes), 1) % chunks

    raw[...] = recv_ref[...].reshape(raw.shape).astype(f32)
    for stream in range(4):
        for pair in range(2):
            first = stream * 4 + 2 * pair
            tile = jnp.concatenate(
                [
                    raw[pl.ds(first, chunks, stride=ROWS_IN), :],
                    raw[pl.ds(first + 1, chunks, stride=ROWS_IN), :],
                ],
                axis=0,
            )
            xt[stream, PAD : PAD + toks, pair * 2 * chunks : (pair + 1) * 2 * chunks] = tile.T
    for stream in range(3):
        tail = pltpu.roll(xt[stream, toks : toks + PAD, :], 1, 1)
        xt[stream, 0:PAD, :] = jnp.where(lane_chunk >= 1, tail, 0.0)

    block = 32
    for start in range(0, toks, block):
        filtered = []
        for stream in range(3):
            total = None
            for tap in range(TAPS):
                row = prm_ref[stream * TAPS + tap : stream * TAPS + tap + 1, :]
                lo = PAD - tap + start
                term = row * xt[stream, lo : lo + block, :]
                total = term if total is None else total + term
            filtered.append(total)
            hat[stream, start : start + block, :] = total
        mixed[start : start + block, :] = (
            (filtered[1] * filtered[2]).astype(jnp.bfloat16).astype(f32)
        )
        gmixed[start : start + block, :] = (
            (xt[3, PAD + start : PAD + start + block, :] * filtered[0])
            .astype(jnp.bfloat16)
            .astype(f32)
        )

    rates = [jnp.exp(prm_ref[24 + 8 * i : 32 + 8 * i, :]) for i in range(2)]
    resid = [prm_ref[40 + 8 * i : 48 + 8 * i, :] for i in range(2)]
    decay = [jnp.exp(-r) for r in rates]
    root = [jnp.sqrt(2.0 * r) for r in rates]
    amp = [resid[i] * root[i] for i in range(2)]

    zero = jnp.zeros((8, lanes), f32)

    def row_of(ref, tok):
        return jnp.broadcast_to(ref[pl.ds(tok, 1), :], (8, lanes))

    def local_body(tok, carry):
        e0, e1, f0, f1 = carry
        xb = row_of(mixed, tok)
        gb = row_of(gmixed, toks - 1 - tok)
        return (
            decay[0] * e0 + xb,
            decay[1] * e1 + xb,
            decay[0] * f0 + gb,
            decay[1] * f1 + gb,
        )

    e0, e1, f0, f1 = lax.fori_loop(0, toks, local_body, (zero,) * 4, unroll=16)

    ends = [e0, e1]
    heads = [f0, f1]
    step = 1
    while step < chunks:
        for i in range(2):
            power = jnp.exp(rates[i] * (-1.0 * toks * step))
            moved = jnp.where(lane_chunk >= step, pltpu.roll(ends[i], step, 1), 0.0)
            ends[i] = ends[i] + power * moved
            moved = jnp.where(
                lane_chunk < chunks - step, pltpu.roll(heads[i], lanes - step, 1), 0.0
            )
            heads[i] = heads[i] + power * moved
        step *= 2
    start_h = [jnp.where(lane_chunk >= 1, pltpu.roll(e, 1, 1), 0.0) for e in ends]
    start_p = [
        jnp.where(lane_chunk < chunks - 1, pltpu.roll(f, lanes - 1, 1), 0.0) for f in heads
    ]

    def keep(ref, tok, value):
        for half in range(2):
            ref[half, pl.ds(pl.multiple_of(8 * tok, 8), 8), :] = value[
                :, half * toks : (half + 1) * toks
            ]

    def forward_body(tok, carry):
        h0, h1, r0, r1 = carry
        xb = row_of(mixed, tok)
        gb = row_of(gmixed, tok)
        h0 = decay[0] * h0 + xb
        h1 = decay[1] * h1 + xb
        keep(part_y, tok, amp[0] * h0 + amp[1] * h1)
        states[pl.ds(pl.multiple_of(16 * tok, 8), 8), :] = h0
        states[pl.ds(pl.multiple_of(16 * tok + 8, 8), 8), :] = h1
        return (h0, h1, r0 + gb * h0, r1 + gb * h1)

    _, _, r0, r1 = lax.fori_loop(
        0, toks, forward_body, (start_h[0], start_h[1], zero, zero), unroll=16
    )

    def backward_body(step_index, carry):
        p0, p1, k0, k1 = carry
        tok = toks - 1 - step_index
        gb = row_of(gmixed, tok)
        q0 = decay[0] * p0
        q1 = decay[1] * p1
        k0 = k0 + states[pl.ds(pl.multiple_of(16 * tok, 8), 8), :] * q0
        k1 = k1 + states[pl.ds(pl.multiple_of(16 * tok + 8, 8), 8), :] * q1
        p0 = q0 + gb
        p1 = q1 + gb
        keep(part_z, tok, amp[0] * p0 + amp[1] * p1)
        return (p0, p1, k0, k1)

    _, _, k0, k1 = lax.fori_loop(
        0, toks, backward_body, (start_p[0], start_p[1], zero, zero), unroll=16
    )

    def folded(ref, first, count):
        halves = []
        for half in range(2):
            total = None
            for sub in range(8):
                term = ref[half, pl.ds(first + sub, count, stride=8), :]
                total = term if total is None else total + term
            halves.append(total)
        return jnp.concatenate(halves, axis=1)

    def gathered(ref, start):
        return folded(ref, 8 * start, block).astype(jnp.bfloat16).astype(f32)

    def put(stream, start, value):
        hat[stream, start : start + block, :] = value

    for start in range(0, toks, block):
        rows = slice(start, start + block)
        conv = gathered(part_y, start)
        back = gathered(part_z, start)
        grads[0, rows, :] = xt[3, PAD + start : PAD + start + block, :] * conv
        grads[1, rows, :] = back * hat[2, rows, :]
        grads[2, rows, :] = back * hat[1, rows, :]
        mixed[rows, :] = hat[0, rows, :] * conv
    for stream in range(3):
        head = pltpu.roll(grads[stream, 0:PAD, :], lanes - 1, 1)
        grads[stream, toks : toks + PAD, :] = jnp.where(lane_chunk < chunks - 1, head, 0.0)
    for stream in range(3):
        tap_sums = [zero for _ in range(TAPS)]
        for start in range(0, toks, block):
            own = grads[stream, start : start + block, :]
            total = None
            for tap in range(TAPS):
                row = prm_ref[stream * TAPS + tap : stream * TAPS + tap + 1, :]
                term = row * grads[stream, start + tap : start + tap + block, :]
                total = term if total is None else total + term
                lo = PAD - tap + start
                prod = own * xt[stream, lo : lo + block, :]
                for sub in range(0, block, 8):
                    tap_sums[tap] = tap_sums[tap] + prod[sub : sub + 8, :]
            put(stream, start, total)
        for tap in range(TAPS):
            index = stream * TAPS + tap
            keep(sums, index, tap_sums[tap])
    for index in range(21, 24):
        keep(sums, index, zero)
    short_rows = folded(sums, 0, 24)
    modal_rows = [root[0] * r0, root[1] * r1] + [
        amp[i] * (0.5 * (r0, r1)[i] - rates[i] * (k0, k1)[i]) for i in range(2)
    ]
    every = jnp.concatenate([short_rows] + modal_rows, axis=0)
    owner = lax.broadcasted_iota(jnp.int32, (8, lanes), 1) // chunks
    pick = (owner == lax.broadcasted_iota(jnp.int32, (8, lanes), 0)).astype(f32)
    totals = (
        lax.dot_general(
            pick,
            every,
            (((1,), (1,)), ((), ())),
            precision=lax.Precision.HIGHEST,
            preferred_element_type=f32,
        )
        * scale
    )
    modal_ref[...] = totals[:, 24:56]

    for stream in range(4):
        for pair in range(2):
            cols = slice(pair * 2 * chunks, (pair + 1) * 2 * chunks)
            tile = (mixed[:, cols] if stream == 0 else hat[stream - 1, :, cols]).T
            first = stream * 4 + 2 * pair
            out_rows[pl.ds(first, chunks, stride=ROWS_OUT), :] = tile[:chunks]
            out_rows[pl.ds(first + 1, chunks, stride=ROWS_OUT), :] = tile[chunks:]
    short = jnp.concatenate([totals[0:4, 0:24], jnp.zeros((4, toks - 24), f32)], axis=1)
    upper = short.astype(jnp.bfloat16).astype(f32)
    for chan in range(4):
        out_rows[pl.ds(16 + chan, chunks, stride=ROWS_OUT), :] = jnp.broadcast_to(
            upper[chan : chan + 1, :], (chunks, toks)
        )
        out_rows[pl.ds(20 + chan, chunks, stride=ROWS_OUT), :] = jnp.broadcast_to(
            (short - upper)[chan : chan + 1, :], (chunks, toks)
        )
    send_ref[...] = out_rows[...].reshape(send_ref.shape).astype(jnp.bfloat16)


def run_pack(query_in, key_in, value_in, grad_out):
    chans, toks = query_in.shape
    owners = chans // 4
    return pl.pallas_call(
        pack_kernel,
        out_shape=jax.ShapeDtypeStruct((owners, ROWS_IN, toks), jnp.bfloat16),
        scratch_shapes=[
            pltpu.VMEM((chans, toks), jnp.float32),
            pltpu.VMEM((owners * ROWS_IN, toks), jnp.float32),
        ],
        compiler_params=pltpu.CompilerParams(vmem_limit_bytes=VMEM_LIMIT),
    )(query_in, key_in, value_in, grad_out)


def run_main(recv, prm):
    chunks, _, toks = recv.shape
    lanes = 4 * chunks
    f32 = jnp.float32
    return pl.pallas_call(
        main_kernel,
        out_shape=(
            jax.ShapeDtypeStruct((chunks, ROWS_OUT, toks), jnp.bfloat16),
            jax.ShapeDtypeStruct((8, 2 * MODES), f32),
        ),
        scratch_shapes=[
            pltpu.VMEM((chunks * ROWS_IN, toks), f32),
            pltpu.VMEM((4, PAD + toks, lanes), f32),
            pltpu.VMEM((3, toks, lanes), f32),
            pltpu.VMEM((toks, lanes), f32),
            pltpu.VMEM((toks, lanes), f32),
            pltpu.VMEM((2, 8 * toks, lanes // 2), f32),
            pltpu.VMEM((2, 8 * toks, lanes // 2), f32),
            pltpu.VMEM((16 * toks, lanes), f32),
            pltpu.VMEM((3, toks + PAD, lanes), f32),
            pltpu.VMEM((2, 8 * 24, lanes // 2), f32),
            pltpu.VMEM((chunks * ROWS_OUT, toks), f32),
        ],
        compiler_params=pltpu.CompilerParams(vmem_limit_bytes=VMEM_LIMIT),
    )(recv, prm)


def run_unpack(recv):
    owners, _, toks = recv.shape
    chans = 4 * owners
    whole = jax.ShapeDtypeStruct((chans, toks), jnp.bfloat16)
    return pl.pallas_call(
        unpack_kernel,
        out_shape=(whole, whole, whole, whole, jax.ShapeDtypeStruct((3 * TAPS, chans), jnp.float32)),
        scratch_shapes=[
            pltpu.VMEM((owners * ROWS_OUT, toks), jnp.float32),
            pltpu.VMEM((chans, toks), jnp.float32),
        ],
        compiler_params=pltpu.CompilerParams(vmem_limit_bytes=VMEM_LIMIT),
    )(recv)


def parameter_rows(weights, residue, log_rate, chunks):
    rows = jnp.concatenate(
        [
            weights.reshape(3 * TAPS, 4),
            jnp.zeros((3, 4), jnp.float32),
            log_rate.T,
            residue.T,
        ],
        axis=0,
    )
    return jnp.repeat(rows, chunks, axis=1)


def local(query_in, key_in, value_in, short_weight, residue, log_rate, grad_out):
    chunks = lax.axis_size("seq")
    chans = query_in.shape[0]
    owned = chans // chunks
    weights = lax.dynamic_slice(
        short_weight, (0, 0, owned * lax.axis_index("seq")), (3, TAPS, owned)
    )
    prm = parameter_rows(weights, residue, log_rate, chunks)
    send = run_pack(query_in, key_in, value_in, grad_out)
    recv = lax.all_to_all(send, "seq", 0, 0, tiled=True)
    back, modal = run_main(recv, prm)
    final = lax.all_to_all(back, "seq", 0, 0, tiled=True)
    output, grad_query, grad_key, grad_value, short = run_unpack(final)
    grad_short = short.reshape(3, TAPS, chans)
    return (
        output,
        grad_query,
        grad_key,
        grad_value,
        grad_short,
        modal[:owned, :MODES],
        modal[:owned, MODES:],
    )


def solution(mesh):
    return jax.shard_map(
        local,
        mesh=mesh,
        in_specs=(
            P("chan", "seq"),
            P("chan", "seq"),
            P("chan", "seq"),
            P(None, None, "chan"),
            P(("chan", "seq"), None),
            P(("chan", "seq"), None),
            P("chan", "seq"),
        ),
        out_specs=(
            P("chan", "seq"),
            P("chan", "seq"),
            P("chan", "seq"),
            P("chan", "seq"),
            P(None, None, "chan"),
            P(("chan", "seq"), None),
            P(("chan", "seq"), None),
        ),
        check_vma=False,
    )
```

```python
import math

import jax
import jax.numpy as jnp
from jax import lax
from jax.experimental import pallas as pl
from jax.experimental.pallas import tpu as pltpu
from jax.sharding import PartitionSpec as P

TAPS = 7
MODES = 16
PAD = 8
ROWS_IN = 16
ROWS_OUT = 18
VMEM_LIMIT = 40 * 1024 * 1024


def pack_kernel(query_ref, key_ref, value_ref, grad_ref, send_ref, held, wide, mixed_rows, sems):
    owners = send_ref.shape[0]
    copies = [
        pltpu.make_async_copy(ref, held.at[stream], sems.at[stream])
        for stream, ref in enumerate((query_ref, key_ref, value_ref, grad_ref))
    ]
    for copy in copies:
        copy.start()
    for stream, copy in enumerate(copies):
        copy.wait()
        wide[stream] = held[stream].astype(jnp.float32)
        for chan in range(4):
            mixed_rows[pl.ds(stream * 4 + chan, owners, stride=ROWS_IN), :] = wide[
                stream, pl.ds(chan, owners, stride=4), :
            ]
    send_ref[...] = mixed_rows[...].reshape(send_ref.shape).astype(jnp.bfloat16)


def unpack_kernel(recv_ref, out_ref, gq_ref, gk_ref, gv_ref, short_ref, rows, wide):
    owners = recv_ref.shape[0] // ROWS_OUT
    rows[...] = recv_ref[...].astype(jnp.float32)
    for stream, ref in enumerate((out_ref, gq_ref, gk_ref, gv_ref)):
        for chan in range(4):
            wide[stream, pl.ds(chan, owners, stride=4), :] = rows[
                pl.ds(stream * 4 + chan, owners, stride=ROWS_OUT), :
            ]
        ref[...] = wide[stream].astype(jnp.bfloat16)
    short = (
        rows[pl.ds(16, owners, stride=ROWS_OUT), :] + rows[pl.ds(17, owners, stride=ROWS_OUT), :]
    )
    for chan in range(4):
        wide[4, pl.ds(chan, owners, stride=4), :] = pltpu.roll(short, (128 - 32 * chan) % 128, 1)
    turned = wide[4].T
    for stream in range(3):
        short_ref[stream] = turned[stream * TAPS : (stream + 1) * TAPS, :]


def main_kernel(
    recv_ref,
    prm_ref,
    send_ref,
    modal_ref,
    raw,
    xt,
    hat,
    mixed,
    gmixed,
    part_y,
    part_z,
    states,
    grads,
    sums,
    out_rows,
):
    chunks = recv_ref.shape[0]
    toks = recv_ref.shape[2]
    lanes = 4 * chunks
    scale = 1.0 / math.sqrt(chunks * toks)
    f32 = jnp.float32
    lane_chunk = lax.broadcasted_iota(jnp.int32, (8, lanes), 1) % chunks

    raw[...] = recv_ref[...].reshape(raw.shape).astype(f32)
    for stream in range(4):
        for pair in range(2):
            first = stream * 4 + 2 * pair
            tile = jnp.concatenate(
                [
                    raw[pl.ds(first, chunks, stride=ROWS_IN), :],
                    raw[pl.ds(first + 1, chunks, stride=ROWS_IN), :],
                ],
                axis=0,
            )
            xt[stream, PAD : PAD + toks, pair * 2 * chunks : (pair + 1) * 2 * chunks] = tile.T
    for stream in range(3):
        tail = pltpu.roll(xt[stream, toks : toks + PAD, :], 1, 1)
        xt[stream, 0:PAD, :] = jnp.where(lane_chunk >= 1, tail, 0.0)

    block = 32
    for start in range(0, toks, block):
        filtered = []
        for stream in range(3):
            total = None
            for tap in range(TAPS):
                row = prm_ref[stream * TAPS + tap : stream * TAPS + tap + 1, :]
                lo = PAD - tap + start
                term = row * xt[stream, lo : lo + block, :]
                total = term if total is None else total + term
            filtered.append(total)
            hat[stream, start : start + block, :] = total
        mixed[start : start + block, :] = (
            (filtered[1] * filtered[2]).astype(jnp.bfloat16).astype(f32)
        )
        gmixed[start : start + block, :] = (
            (xt[3, PAD + start : PAD + start + block, :] * filtered[0])
            .astype(jnp.bfloat16)
            .astype(f32)
        )

    rates = [jnp.exp(prm_ref[24 + 8 * i : 32 + 8 * i, :]) for i in range(2)]
    resid = [prm_ref[40 + 8 * i : 48 + 8 * i, :] for i in range(2)]
    decay = [jnp.exp(-r) for r in rates]
    root = [jnp.sqrt(2.0 * r) for r in rates]
    amp = [resid[i] * root[i] for i in range(2)]

    zero = jnp.zeros((8, lanes), f32)

    def row_of(ref, tok):
        return jnp.broadcast_to(ref[pl.ds(tok, 1), :], (8, lanes))

    def local_body(tok, carry):
        e0, e1, f0, f1 = carry
        xb = row_of(mixed, tok)
        gb = row_of(gmixed, toks - 1 - tok)
        return (
            decay[0] * e0 + xb,
            decay[1] * e1 + xb,
            decay[0] * f0 + gb,
            decay[1] * f1 + gb,
        )

    e0, e1, f0, f1 = lax.fori_loop(0, toks, local_body, (zero,) * 4, unroll=16)

    ends = [e0, e1]
    heads = [f0, f1]
    step = 1
    while step < chunks:
        for i in range(2):
            power = jnp.exp(rates[i] * (-1.0 * toks * step))
            moved = jnp.where(lane_chunk >= step, pltpu.roll(ends[i], step, 1), 0.0)
            ends[i] = ends[i] + power * moved
            moved = jnp.where(
                lane_chunk < chunks - step, pltpu.roll(heads[i], lanes - step, 1), 0.0
            )
            heads[i] = heads[i] + power * moved
        step *= 2
    start_h = [jnp.where(lane_chunk >= 1, pltpu.roll(e, 1, 1), 0.0) for e in ends]
    start_p = [
        jnp.where(lane_chunk < chunks - 1, pltpu.roll(f, lanes - 1, 1), 0.0) for f in heads
    ]

    def keep(ref, tok, value):
        for half in range(2):
            ref[half, pl.ds(pl.multiple_of(8 * tok, 8), 8), :] = value[
                :, half * toks : (half + 1) * toks
            ]

    def forward_body(tok, carry):
        h0, h1, r0, r1 = carry
        xb = row_of(mixed, tok)
        gb = row_of(gmixed, tok)
        h0 = decay[0] * h0 + xb
        h1 = decay[1] * h1 + xb
        keep(part_y, tok, amp[0] * h0 + amp[1] * h1)
        states[pl.ds(pl.multiple_of(16 * tok, 8), 8), :] = h0
        states[pl.ds(pl.multiple_of(16 * tok + 8, 8), 8), :] = h1
        return (h0, h1, r0 + gb * h0, r1 + gb * h1)

    _, _, r0, r1 = lax.fori_loop(
        0, toks, forward_body, (start_h[0], start_h[1], zero, zero), unroll=16
    )

    def backward_body(step_index, carry):
        p0, p1, k0, k1 = carry
        tok = toks - 1 - step_index
        gb = row_of(gmixed, tok)
        q0 = decay[0] * p0
        q1 = decay[1] * p1
        k0 = k0 + states[pl.ds(pl.multiple_of(16 * tok, 8), 8), :] * q0
        k1 = k1 + states[pl.ds(pl.multiple_of(16 * tok + 8, 8), 8), :] * q1
        p0 = q0 + gb
        p1 = q1 + gb
        keep(part_z, tok, amp[0] * p0 + amp[1] * p1)
        return (p0, p1, k0, k1)

    _, _, k0, k1 = lax.fori_loop(
        0, toks, backward_body, (start_p[0], start_p[1], zero, zero), unroll=16
    )

    def folded(ref, first, count):
        halves = []
        for half in range(2):
            total = None
            for sub in range(8):
                term = ref[half, pl.ds(first + sub, count, stride=8), :]
                total = term if total is None else total + term
            halves.append(total)
        return jnp.concatenate(halves, axis=1)

    def gathered(ref, start):
        return folded(ref, 8 * start, block).astype(jnp.bfloat16).astype(f32)

    def put(stream, start, value):
        hat[stream, start : start + block, :] = value

    for start in range(0, toks, block):
        rows = slice(start, start + block)
        conv = gathered(part_y, start)
        back = gathered(part_z, start)
        grads[0, rows, :] = xt[3, PAD + start : PAD + start + block, :] * conv
        grads[1, rows, :] = back * hat[2, rows, :]
        grads[2, rows, :] = back * hat[1, rows, :]
        mixed[rows, :] = hat[0, rows, :] * conv
    for stream in range(3):
        head = pltpu.roll(grads[stream, 0:PAD, :], lanes - 1, 1)
        grads[stream, toks : toks + PAD, :] = jnp.where(lane_chunk < chunks - 1, head, 0.0)
    for stream in range(3):
        tap_sums = [zero for _ in range(TAPS)]
        for start in range(0, toks, block):
            own = grads[stream, start : start + block, :]
            total = None
            for tap in range(TAPS):
                row = prm_ref[stream * TAPS + tap : stream * TAPS + tap + 1, :]
                term = row * grads[stream, start + tap : start + tap + block, :]
                total = term if total is None else total + term
                lo = PAD - tap + start
                prod = own * xt[stream, lo : lo + block, :]
                for sub in range(0, block, 8):
                    tap_sums[tap] = tap_sums[tap] + prod[sub : sub + 8, :]
            put(stream, start, total)
        for tap in range(TAPS):
            index = stream * TAPS + tap
            keep(sums, index, tap_sums[tap])
    for index in range(21, 24):
        keep(sums, index, zero)
    short_rows = folded(sums, 0, 24)
    modal_rows = [root[0] * r0, root[1] * r1] + [
        amp[i] * (0.5 * (r0, r1)[i] - rates[i] * (k0, k1)[i]) for i in range(2)
    ]
    every = jnp.concatenate([short_rows] + modal_rows, axis=0)
    owner = lax.broadcasted_iota(jnp.int32, (8, lanes), 1) // chunks
    pick = (owner == lax.broadcasted_iota(jnp.int32, (8, lanes), 0)).astype(f32)
    totals = (
        lax.dot_general(
            pick,
            every,
            (((1,), (1,)), ((), ())),
            precision=lax.Precision.HIGHEST,
            preferred_element_type=f32,
        )
        * scale
    )
    modal_ref[...] = totals[:, 24:56]

    for stream in range(4):
        for pair in range(2):
            cols = slice(pair * 2 * chunks, (pair + 1) * 2 * chunks)
            tile = (mixed[:, cols] if stream == 0 else hat[stream - 1, :, cols]).T
            first = stream * 4 + 2 * pair
            out_rows[pl.ds(first, chunks, stride=ROWS_OUT), :] = tile[:chunks]
            out_rows[pl.ds(first + 1, chunks, stride=ROWS_OUT), :] = tile[chunks:]
    short = jnp.concatenate([totals[:, 0:24], jnp.zeros((8, toks - 24), f32)], axis=1)
    line = short[0:1, :]
    for chan in range(1, 4):
        line = line + pltpu.roll(short, 32 * chan, 1)[chan : chan + 1, :]
    upper = line.astype(jnp.bfloat16).astype(f32)
    out_rows[pl.ds(16, chunks, stride=ROWS_OUT), :] = jnp.broadcast_to(upper, (chunks, toks))
    out_rows[pl.ds(17, chunks, stride=ROWS_OUT), :] = jnp.broadcast_to(line - upper, (chunks, toks))
    send_ref[...] = out_rows[...].astype(jnp.bfloat16)


def run_pack(query_in, key_in, value_in, grad_out):
    chans, toks = query_in.shape
    owners = chans // 4
    return pl.pallas_call(
        pack_kernel,
        in_specs=[pl.BlockSpec(memory_space=pltpu.HBM)] * 4,
        out_shape=jax.ShapeDtypeStruct((owners, ROWS_IN, toks), jnp.bfloat16),
        scratch_shapes=[
            pltpu.VMEM((4, chans, toks), jnp.bfloat16),
            pltpu.VMEM((4, chans, toks), jnp.float32),
            pltpu.VMEM((owners * ROWS_IN, toks), jnp.float32),
            pltpu.SemaphoreType.DMA((4,)),
        ],
        compiler_params=pltpu.CompilerParams(vmem_limit_bytes=VMEM_LIMIT),
    )(query_in, key_in, value_in, grad_out)


def run_main(recv, prm):
    chunks, _, toks = recv.shape
    lanes = 4 * chunks
    f32 = jnp.float32
    return pl.pallas_call(
        main_kernel,
        out_shape=(
            jax.ShapeDtypeStruct((chunks * ROWS_OUT, toks), jnp.bfloat16),
            jax.ShapeDtypeStruct((8, 2 * MODES), f32),
        ),
        scratch_shapes=[
            pltpu.VMEM((chunks * ROWS_IN, toks), f32),
            pltpu.VMEM((4, PAD + toks, lanes), f32),
            pltpu.VMEM((3, toks, lanes), f32),
            pltpu.VMEM((toks, lanes), f32),
            pltpu.VMEM((toks, lanes), f32),
            pltpu.VMEM((2, 8 * toks, lanes // 2), f32),
            pltpu.VMEM((2, 8 * toks, lanes // 2), f32),
            pltpu.VMEM((16 * toks, lanes), f32),
            pltpu.VMEM((3, toks + PAD, lanes), f32),
            pltpu.VMEM((2, 8 * 24, lanes // 2), f32),
            pltpu.VMEM((chunks * ROWS_OUT, toks), f32),
        ],
        compiler_params=pltpu.CompilerParams(vmem_limit_bytes=VMEM_LIMIT),
    )(recv, prm)


def run_unpack(recv):
    rows, toks = recv.shape
    owners = rows // ROWS_OUT
    chans = 4 * owners
    whole = jax.ShapeDtypeStruct((chans, toks), jnp.bfloat16)
    return pl.pallas_call(
        unpack_kernel,
        out_shape=(whole,) * 4 + (jax.ShapeDtypeStruct((3, TAPS, chans), jnp.float32),),
        scratch_shapes=[
            pltpu.VMEM((owners * ROWS_OUT, toks), jnp.float32),
            pltpu.VMEM((5, chans, toks), jnp.float32),
        ],
        compiler_params=pltpu.CompilerParams(vmem_limit_bytes=VMEM_LIMIT),
    )(recv)


def parameter_rows(weights, residue, log_rate, chunks):
    rows = jnp.concatenate(
        [
            weights.reshape(3 * TAPS, 4),
            jnp.zeros((3, 4), jnp.float32),
            log_rate.T,
            residue.T,
        ],
        axis=0,
    )
    return jnp.repeat(rows, chunks, axis=1)


def local(query_in, key_in, value_in, short_weight, residue, log_rate, grad_out):
    chunks = lax.axis_size("seq")
    chans = query_in.shape[0]
    owned = chans // chunks
    weights = lax.dynamic_slice(
        short_weight, (0, 0, owned * lax.axis_index("seq")), (3, TAPS, owned)
    )
    prm = parameter_rows(weights, residue, log_rate, chunks)
    send = run_pack(query_in, key_in, value_in, grad_out)
    recv = lax.all_to_all(send, "seq", 0, 0, tiled=True)
    back, modal = run_main(recv, prm)
    paired = back.reshape(chunks, ROWS_OUT // 2, 2, back.shape[1])
    final = lax.all_to_all(paired, "seq", 0, 0, tiled=True)
    output, grad_query, grad_key, grad_value, grad_short = run_unpack(final.reshape(back.shape))
    return (
        output,
        grad_query,
        grad_key,
        grad_value,
        grad_short,
        modal[:owned, :MODES],
        modal[:owned, MODES:],
    )


def solution(mesh):
    return jax.shard_map(
        local,
        mesh=mesh,
        in_specs=(
            P("chan", "seq"),
            P("chan", "seq"),
            P("chan", "seq"),
            P(None, None, "chan"),
            P(("chan", "seq"), None),
            P(("chan", "seq"), None),
            P("chan", "seq"),
        ),
        out_specs=(
            P("chan", "seq"),
            P("chan", "seq"),
            P("chan", "seq"),
            P("chan", "seq"),
            P(None, None, "chan"),
            P(("chan", "seq"), None),
            P(("chan", "seq"), None),
        ),
        check_vma=False,
    )
```

```python
import math

import jax
import jax.numpy as jnp
from jax import lax
from jax.experimental import pallas as pl
from jax.experimental.pallas import tpu as pltpu
from jax.sharding import PartitionSpec as P

TAPS = 7
MODES = 16
PAD = 8
OWNED = 8
ROWS_IN = 4 * OWNED
ROWS_OUT = 40
VMEM_LIMIT = 40 * 1024 * 1024

STATE, DERIV, RSUM, KSUM, EDGE, SHORT, RESPONSE, MESSAGE = 0, 16, 32, 48, 64, 96, 128, 384


def first_row(chan, chans):
    return chan if chan < 4 else chans // 2 + chan - 4


def pack_kernel(query_ref, key_ref, value_ref, grad_ref, send_ref, held, wide, mixed_rows, sems):
    owners = send_ref.shape[0]
    chans = query_ref.shape[0]
    copies = [
        pltpu.make_async_copy(ref, held.at[stream], sems.at[stream])
        for stream, ref in enumerate((query_ref, key_ref, value_ref, grad_ref))
    ]
    for copy in copies:
        copy.start()
    for stream, copy in enumerate(copies):
        copy.wait()
        wide[stream] = held[stream].astype(jnp.float32)
        for chan in range(OWNED):
            mixed_rows[pl.ds(stream * OWNED + chan, owners, stride=ROWS_IN), :] = wide[
                stream, pl.ds(first_row(chan, chans), owners, stride=4), :
            ]
    send_ref[...] = mixed_rows[...].reshape(send_ref.shape).astype(jnp.bfloat16)


def unpack_kernel(recv_ref, out_ref, gq_ref, gk_ref, gv_ref, short_ref, rows, wide):
    owners = recv_ref.shape[0]
    chans = out_ref.shape[0]
    rows[...] = recv_ref[...].reshape(rows.shape).astype(jnp.float32)
    for stream, ref in enumerate((out_ref, gq_ref, gk_ref, gv_ref)):
        for chan in range(OWNED):
            wide[stream, pl.ds(first_row(chan, chans), owners, stride=4), :] = rows[
                pl.ds(stream * OWNED + chan, owners, stride=ROWS_OUT), :
            ]
        ref[...] = wide[stream].astype(jnp.bfloat16)
    for group in range(2):
        short = (
            rows[pl.ds(32 + group, owners, stride=ROWS_OUT), :]
            + rows[pl.ds(34 + group, owners, stride=ROWS_OUT), :]
        )
        for chan in range(4):
            wide[4, pl.ds(first_row(4 * group + chan, chans), owners, stride=4), :] = pltpu.roll(
                short, (128 - 32 * chan) % 128, 1
            )
    turned = wide[4].T
    for stream in range(3):
        short_ref[stream] = turned[stream * TAPS : (stream + 1) * TAPS, :]


def lane_ids(chunks, rows):
    lane = lax.broadcasted_iota(jnp.int32, (rows, OWNED * chunks), 1)
    return lane % chunks, lane // chunks


def owner_pick(chunks):
    owner = lane_ids(chunks, OWNED)[1]
    return (owner == lax.broadcasted_iota(jnp.int32, owner.shape, 0)).astype(jnp.float32)


def exact_dot(left, right, dims):
    return lax.dot_general(
        left,
        right,
        (dims, ((), ())),
        precision=lax.Precision.HIGHEST,
        preferred_element_type=jnp.float32,
    )


def modal_rows(prm_ref):
    rates = [jnp.exp(prm_ref[24 + 8 * i : 32 + 8 * i, :]) for i in range(2)]
    resid = [prm_ref[40 + 8 * i : 48 + 8 * i, :] for i in range(2)]
    decay = [jnp.exp(-r) for r in rates]
    root = [jnp.sqrt(2.0 * r) for r in rates]
    amp = [resid[i] * root[i] for i in range(2)]
    return rates, decay, root, amp


def keep(ref, tok, value):
    lanes = ref.shape[2]
    for half in range(2):
        ref[half, pl.ds(pl.multiple_of(8 * tok, 8), 8), :] = value[
            :, half * lanes : (half + 1) * lanes
        ]


def folded(ref, first, count):
    halves = []
    for half in range(2):
        total = None
        for sub in range(8):
            term = ref[half, pl.ds(first + sub, count, stride=8), :]
            total = term if total is None else total + term
        halves.append(total)
    return jnp.concatenate(halves, axis=1)


def tap_row(prm_ref, stream, tap):
    index = stream * TAPS + tap
    return prm_ref[index : index + 1, :]


def rounded(value):
    return value.astype(jnp.bfloat16).astype(jnp.float32)


def first_kernel(
    half_ref,
    recv_ref,
    prm_ref,
    grad_ref,
    hat_ref,
    fwd_ref,
    bwd_ref,
    msg_ref,
    raw,
    xt,
    mixed,
    gmixed,
    base,
    part_y,
    part_z,
    states,
    weighted,
    sums,
    rows,
):
    chunks = recv_ref.shape[0]
    toks = recv_ref.shape[2]
    lanes = OWNED * chunks
    f32 = jnp.float32
    chunk_of, _ = lane_ids(chunks, 8)
    half = half_ref[0]
    late = half.astype(f32)
    early = 1.0 - late
    zero = jnp.zeros((8, lanes), f32)
    block = 32

    raw[...] = recv_ref[...].reshape(raw.shape).astype(f32)
    per_tile = toks // chunks
    for stream in range(4):
        for group in range(OWNED // per_tile):
            tile = jnp.concatenate(
                [
                    raw[
                        pl.ds(stream * OWNED + group * per_tile + c, chunks, stride=ROWS_IN), :
                    ]
                    for c in range(per_tile)
                ],
                axis=0,
            )
            xt[stream, PAD : PAD + toks, group * toks : (group + 1) * toks] = tile.T
    for stream in range(3):
        tail = pltpu.roll(xt[stream, toks : toks + PAD, :], 1, 1)
        xt[stream, 0:PAD, :] = jnp.where(chunk_of >= 1, tail, 0.0)

    fringe = (lax.broadcasted_iota(jnp.int32, (8, lanes), 0) < TAPS - 1) & (chunk_of == 0)
    kept = 1.0 - jnp.where(fringe, late, 0.0)
    for start in range(0, toks, block):
        filtered = []
        for stream in range(3):
            total = None
            for tap in range(TAPS):
                lo = PAD - tap + start
                term = tap_row(prm_ref, stream, tap) * xt[stream, lo : lo + block, :]
                total = term if total is None else total + term
            filtered.append(total)
            hat_ref[stream, start : start + block, :] = total
        grad = xt[3, PAD + start : PAD + start + block, :]
        mixed[start : start + block, :] = rounded(filtered[1] * filtered[2])
        gmixed[start : start + block, :] = rounded(grad * filtered[0])
        grad_ref[start : start + block, :] = grad
        base[0, start : start + block, :] = grad
        base[1, start : start + block, :] = filtered[2]
        base[2, start : start + block, :] = filtered[1]
    mixed[0:8, :] = mixed[0:8, :] * kept
    gmixed[0:8, :] = gmixed[0:8, :] * kept
    for stream in range(3):
        base[stream, 0:8, :] = base[stream, 0:8, :] * kept

    rates, decay, _, amp = modal_rows(prm_ref)

    def row_of(ref, tok):
        return jnp.broadcast_to(ref[pl.ds(tok, 1), :], (8, lanes))

    def local_body(tok, carry):
        e0, e1, f0, f1 = carry
        xb = row_of(mixed, tok)
        gb = row_of(gmixed, toks - 1 - tok)
        return (
            decay[0] * e0 + xb,
            decay[1] * e1 + xb,
            decay[0] * f0 + gb,
            decay[1] * f1 + gb,
        )

    e0, e1, f0, f1 = lax.fori_loop(0, toks, local_body, (zero,) * 4, unroll=16)
    ends = [e0, e1]
    heads = [f0, f1]
    step = 1
    while step < chunks:
        for i in range(2):
            power = jnp.exp(rates[i] * (-1.0 * toks * step))
            moved = jnp.where(chunk_of >= step, pltpu.roll(ends[i], step, 1), 0.0)
            ends[i] = ends[i] + power * moved
            moved = jnp.where(chunk_of < chunks - step, pltpu.roll(heads[i], lanes - step, 1), 0.0)
            heads[i] = heads[i] + power * moved
        step *= 2
    start_h = [jnp.where(chunk_of >= 1, pltpu.roll(e, 1, 1), 0.0) for e in ends]
    start_p = [jnp.where(chunk_of < chunks - 1, pltpu.roll(f, lanes - 1, 1), 0.0) for f in heads]

    def forward_body(tok, carry):
        h0, h1, r0, r1, d0, d1 = carry
        xb = row_of(mixed, tok)
        gb = row_of(gmixed, tok)
        h0 = decay[0] * h0 + xb
        h1 = decay[1] * h1 + xb
        keep(part_y, tok, amp[0] * h0 + amp[1] * h1)
        states[pl.ds(pl.multiple_of(16 * tok, 8), 8), :] = h0
        states[pl.ds(pl.multiple_of(16 * tok + 8, 8), 8), :] = h1
        return (
            h0,
            h1,
            r0 + gb * h0,
            r1 + gb * h1,
            decay[0] * d0 + h0,
            decay[1] * d1 + h1,
        )

    _, _, r0, r1, d0, d1 = lax.fori_loop(
        0, toks, forward_body, (start_h[0], start_h[1]) + (zero,) * 4, unroll=16
    )

    def backward_body(step_index, carry):
        p0, p1, k0, k1, c0, c1 = carry
        tok = toks - 1 - step_index
        gb = row_of(gmixed, tok)
        q0 = decay[0] * p0
        q1 = decay[1] * p1
        k0 = k0 + states[pl.ds(pl.multiple_of(16 * tok, 8), 8), :] * q0
        k1 = k1 + states[pl.ds(pl.multiple_of(16 * tok + 8, 8), 8), :] * q1
        p0 = q0 + gb
        p1 = q1 + gb
        keep(part_z, tok, amp[0] * p0 + amp[1] * p1)
        return (p0, p1, k0, k1, decay[0] * c0 + p0, decay[1] * c1 + p1)

    _, _, k0, k1, c0, c1 = lax.fori_loop(
        0, toks, backward_body, (start_p[0], start_p[1]) + (zero,) * 4, unroll=16
    )

    for start in range(0, toks, block):
        fwd_ref[start : start + block, :] = folded(part_y, 8 * start, block)
        bwd_ref[start : start + block, :] = folded(part_z, 8 * start, block)

    for stream in range(3):
        tap_sums = [zero for _ in range(TAPS)]
        for start in range(0, toks, block):
            conv = (fwd_ref if stream == 0 else bwd_ref)[start : start + block, :]
            own = conv * base[stream, start : start + block, :]
            for tap in range(TAPS):
                lo = PAD - tap + start
                prod = own * xt[stream, lo : lo + block, :]
                for sub in range(0, block, 8):
                    tap_sums[tap] = tap_sums[tap] + prod[sub : sub + 8, :]
        for tap in range(TAPS):
            keep(sums, stream * TAPS + tap, tap_sums[tap])
    for index in range(3 * TAPS, 24):
        keep(sums, index, zero)
    rows[SHORT : SHORT + 24, :] = folded(sums, 0, 24)
    rows[SHORT + 24 : RESPONSE, :] = zero

    def fill(slot, stream):
        for tap in range(TAPS):
            for start in range(0, toks, block):
                lo = PAD - tap + start
                weighted[slot + tap, start : start + block, :] = (
                    base[stream, start : start + block, :] * xt[stream, lo : lo + block, :]
                )

    span_c = chunk_of.astype(f32)
    power_early = [jnp.exp(-r * (toks * (chunks - 1.0 - span_c) + 1.0)) for r in rates]
    power_late = [jnp.exp(-r * (toks * span_c - (TAPS - 2.0))) for r in rates]

    def respond(slot, powers, reverse):
        def body(step_index, carry):
            tok = toks - 1 - step_index if reverse else step_index
            out = []
            for tap in range(TAPS):
                wb = row_of(weighted.at[slot + tap], tok)
                for i in range(2):
                    out.append(decay[i] * carry[2 * tap + i] + wb)
            return tuple(out)

        total = lax.fori_loop(0, toks, body, (zero,) * (2 * TAPS), unroll=8)
        for tap in range(TAPS):
            for i in range(2):
                lo = RESPONSE + 16 * (slot + tap) + 8 * i
                rows[lo : lo + 8, :] = total[2 * tap + i] * powers[i]

    @pl.when(half == 0)
    def _():
        fill(0, 1)
        fill(TAPS, 2)
        respond(0, power_early, False)
        respond(TAPS, power_early, False)
        for stream in range(4):
            lo = EDGE + 8 * stream
            rows[lo : lo + 8, :] = jnp.where(
                chunk_of == chunks - 1, xt[stream, toks : toks + PAD, :], 0.0
            )
        for i in range(2):
            weight = jnp.exp(-rates[i] * (toks * (chunks - 1.0 - span_c)))
            rows[STATE + 8 * i : STATE + 8 * i + 8, :] = jnp.where(
                chunk_of == chunks - 1, ends[i], 0.0
            )
            rows[DERIV + 8 * i : DERIV + 8 * i + 8, :] = (d0, d1)[i] * weight

    @pl.when(half != 0)
    def _():
        fill(0, 0)
        respond(0, power_late, True)
        for lo in range(RESPONSE + 16 * TAPS, RESPONSE + 32 * TAPS, 8):
            rows[lo : lo + 8, :] = zero
        for stream in range(4):
            lo = EDGE + 8 * stream
            rows[lo : lo + 8, :] = jnp.where(chunk_of == 0, xt[stream, PAD : 2 * PAD, :], 0.0)
        for i in range(2):
            grow = jnp.exp(rates[i] * (TAPS - 1.0))
            weight = jnp.exp(-rates[i] * (toks * span_c))
            first = jnp.where(chunk_of == 0, heads[i], 0.0)
            rows[STATE + 8 * i : STATE + 8 * i + 8, :] = first * grow
            rows[DERIV + 8 * i : DERIV + 8 * i + 8, :] = (
                (c0, c1)[i] * weight - (TAPS - 1.0) * first
            ) * grow

    for i in range(2):
        rows[RSUM + 8 * i : RSUM + 8 * i + 8, :] = (r0, r1)[i]
        rows[KSUM + 8 * i : KSUM + 8 * i + 8, :] = (k0, k1)[i]
    for lo in range(RESPONSE + 32 * TAPS, MESSAGE, 8):
        rows[lo : lo + 8, :] = zero
    msg_ref[...] = exact_dot(owner_pick(chunks), rows[...], ((1,), (1,)))


def second_kernel(
    half_ref,
    own_ref,
    other_ref,
    prm_ref,
    grad_ref,
    hat_ref,
    fwd_ref,
    bwd_ref,
    send_ref,
    modal_ref,
    edge0,
    edge1,
    edges,
    part,
    outs,
    grads,
    out_rows,
):
    toks, lanes = grad_ref.shape
    chunks = lanes // OWNED
    f32 = jnp.float32
    chunk_of, _ = lane_ids(chunks, 8)
    scale = 1.0 / math.sqrt(2 * chunks * toks)
    half = half_ref[0]
    late = half.astype(f32)
    early = 1.0 - late
    rates, decay, root, amp = modal_rows(prm_ref)
    pick = owner_pick(chunks)
    fringe = TAPS - 1
    zero = jnp.zeros((8, lanes), f32)

    own = own_ref[...]
    other = other_ref[...]
    edge0[...] = exact_dot(own * early + other * late, pick, ((0,), (0,)))
    edge1[...] = exact_dot(own * late + other * early, pick, ((0,), (0,)))

    def pair(ref, first):
        return [ref[first + 8 * i : first + 8 * i + 8, :] for i in range(2)]

    row_id = lax.broadcasted_iota(jnp.int32, (8, lanes), 0)
    live = jnp.where(row_id < fringe, 1.0, 0.0)
    hats = []
    for stream in range(3):
        edges[stream, 0:8, :] = edge0[EDGE + 8 * stream : EDGE + 8 * stream + 8, :]
        edges[stream, 8:16, :] = edge1[EDGE + 8 * stream : EDGE + 8 * stream + 8, :]
        total = None
        for tap in range(TAPS):
            term = tap_row(prm_ref, stream, tap) * edges[stream, 8 - tap : 16 - tap, :]
            total = term if total is None else total + term
        hats.append(total)
    grad_edge = edge1[EDGE + 24 : EDGE + 32, :]
    x_edge = rounded(hats[1] * hats[2])
    g_edge = rounded(grad_edge * hats[0])

    state = pair(edge0, STATE)
    passed = []
    y_edge = zero
    for tok in range(fringe):
        xb = jnp.broadcast_to(x_edge[tok : tok + 1, :], (8, lanes))
        state = [decay[i] * state[i] + xb for i in range(2)]
        passed.append(state)
        line = jnp.sum(amp[0] * state[0] + amp[1] * state[1], axis=0, keepdims=True)
        y_edge = jnp.where(row_id == tok, line, y_edge)
    after = state
    back = pair(edge1, STATE)
    r_edge = [zero, zero]
    k_edge = [zero, zero]
    z_edge = zero
    adjoint = back
    for tok in range(fringe - 1, -1, -1):
        gb = jnp.broadcast_to(g_edge[tok : tok + 1, :], (8, lanes))
        moved = [decay[i] * adjoint[i] for i in range(2)]
        k_edge = [k_edge[i] + passed[tok][i] * moved[i] for i in range(2)]
        r_edge = [r_edge[i] + gb * passed[tok][i] for i in range(2)]
        adjoint = [moved[i] + gb for i in range(2)]
        line = jnp.sum(amp[0] * adjoint[0] + amp[1] * adjoint[1], axis=0, keepdims=True)
        z_edge = jnp.where(row_id == tok, line, z_edge)

    span_c = chunk_of.astype(f32)
    carry = []
    for i in range(2):
        into_late = after[i] * jnp.exp(-rates[i] * (toks * span_c - (fringe - 1.0)))
        into_early = adjoint[i] * jnp.exp(-rates[i] * (toks * (chunks - 1.0 - span_c) + 1.0))
        carry.append(amp[i] * (early * into_early + late * into_late))

    def reply_body(step_index, values):
        tok = half * step_index + (1 - half) * (toks - 1 - step_index)
        keep(part, tok, values[0] + values[1])
        return (values[0] * decay[0], values[1] * decay[1])

    lax.fori_loop(0, toks, reply_body, tuple(carry), unroll=16)

    patch = (row_id < fringe) & (chunk_of == 0) & (jnp.broadcast_to(late, (8, lanes)) > 0.5)
    y_edge = rounded(y_edge)
    z_edge = rounded(z_edge)
    for start, count in ((0, 8), (8, 24), (32, 32), (64, 32), (96, 32)):
        span = slice(start, start + count)
        reply = folded(part, 8 * start, count)
        conv = rounded(fwd_ref[span, :] + late * reply)
        turn = rounded(bwd_ref[span, :] + early * reply)
        hat = [hat_ref[stream, span, :] for stream in range(3)]
        if start == 0:
            conv = jnp.where(patch, y_edge, conv)
            turn = jnp.where(patch, z_edge, turn)
            hat = [jnp.where(patch, hats[stream], hat[stream]) for stream in range(3)]
        grads[0, span, :] = grad_ref[span, :] * conv
        grads[1, span, :] = turn * hat[2]
        grads[2, span, :] = turn * hat[1]
        outs[0, span, :] = hat[0] * conv
    edge_grads = (grad_edge * y_edge, z_edge * hats[2], z_edge * hats[1])
    for stream in range(3):
        head = pltpu.roll(grads[stream, 0:PAD, :], lanes - 1, 1)
        grads[stream, toks : toks + PAD, :] = jnp.where(
            chunk_of < chunks - 1, head, early * edge_grads[stream]
        )
    block = 32
    for stream in range(3):
        for start in range(0, toks, block):
            total = None
            for tap in range(TAPS):
                term = (
                    tap_row(prm_ref, stream, tap)
                    * grads[stream, start + tap : start + tap + block, :]
                )
                total = term if total is None else total + term
            outs[1 + stream, start : start + block, :] = total

    single = jnp.where(chunk_of == 0, scale, 0.0)
    forced = [amp[i] * after[i] for i in range(2)]
    turned = [amp[i] * adjoint[i] for i in range(2)]
    short = [
        edge0[SHORT + 8 * i : SHORT + 8 * i + 8, :] + edge1[SHORT + 8 * i : SHORT + 8 * i + 8, :]
        for i in range(3)
    ]
    for stream in range(3):
        live_grad = edge_grads[stream] * live
        for tap in range(TAPS):
            index = stream * TAPS + tap
            term = live_grad * edges[stream, 8 - tap : 16 - tap, :]
            ref, slot = (edge1, tap) if stream == 0 else (edge0, (stream - 1) * TAPS + tap)
            drive = forced if stream == 0 else turned
            for i in range(2):
                lo = RESPONSE + 16 * slot + 8 * i
                term = term + drive[i] * ref[lo : lo + 8, :]
            line = jnp.sum(term, axis=0, keepdims=True)
            short[index // 8] = short[index // 8] + jnp.where(row_id == index % 8, line, 0.0)
    r_all = []
    k_all = []
    for i in range(2):
        first_r, late_r = pair(edge0, RSUM)[i], pair(edge1, RSUM)[i]
        first_k, late_k = pair(edge0, KSUM)[i], pair(edge1, KSUM)[i]
        lag_early, lag_late = pair(edge0, DERIV)[i], pair(edge1, DERIV)[i]
        r_all.append(first_r + late_r + decay[i] * back[i] * after[i] + r_edge[i])
        k_all.append(
            first_k
            + late_k
            + decay[i] * lag_early * adjoint[i]
            + decay[i] * after[i] * (lag_late - back[i])
            + k_edge[i]
        )
    every = jnp.concatenate(
        [value * single for value in short]
        + [root[i] * r_all[i] * single for i in range(2)]
        + [amp[i] * (0.5 * r_all[i] - rates[i] * k_all[i]) * single for i in range(2)],
        axis=0,
    )
    totals = exact_dot(pick, every, ((1,), (1,)))
    modal_ref[...] = totals[:, 24:56]

    per_tile = toks // chunks
    for stream in range(4):
        for group in range(OWNED // per_tile):
            tile = outs[stream, :, group * toks : (group + 1) * toks].T
            for c in range(per_tile):
                out_rows[
                    pl.ds(stream * OWNED + group * per_tile + c, chunks, stride=ROWS_OUT), :
                ] = tile[c * chunks : (c + 1) * chunks]
    wide = jnp.concatenate([totals[:, 0:24], jnp.zeros((8, toks - 24), f32)], axis=1)
    for group in range(2):
        line = wide[4 * group : 4 * group + 1, :]
        for chan in range(1, 4):
            at = 4 * group + chan
            line = line + pltpu.roll(wide, 32 * chan, 1)[at : at + 1, :]
        upper = rounded(line)
        out_rows[pl.ds(32 + group, chunks, stride=ROWS_OUT), :] = jnp.broadcast_to(
            upper, (chunks, toks)
        )
        out_rows[pl.ds(34 + group, chunks, stride=ROWS_OUT), :] = jnp.broadcast_to(
            line - upper, (chunks, toks)
        )
    for spare in range(36, ROWS_OUT):
        out_rows[pl.ds(spare, chunks, stride=ROWS_OUT), :] = jnp.zeros((chunks, toks), f32)
    send_ref[...] = out_rows[...].reshape(send_ref.shape).astype(jnp.bfloat16)


def run_pack(query_in, key_in, value_in, grad_out):
    chans, toks = query_in.shape
    owners = chans // OWNED
    return pl.pallas_call(
        pack_kernel,
        in_specs=[pl.BlockSpec(memory_space=pltpu.HBM)] * 4,
        out_shape=jax.ShapeDtypeStruct((owners, ROWS_IN, toks), jnp.bfloat16),
        scratch_shapes=[
            pltpu.VMEM((4, chans, toks), jnp.bfloat16),
            pltpu.VMEM((4, chans, toks), jnp.float32),
            pltpu.VMEM((owners * ROWS_IN, toks), jnp.float32),
            pltpu.SemaphoreType.DMA((4,)),
        ],
        compiler_params=pltpu.CompilerParams(vmem_limit_bytes=VMEM_LIMIT),
    )(query_in, key_in, value_in, grad_out)


def run_first(half, recv, prm):
    chunks, _, toks = recv.shape
    lanes = OWNED * chunks
    f32 = jnp.float32
    plane = jax.ShapeDtypeStruct((toks, lanes), f32)
    vmem = pl.BlockSpec(memory_space=pltpu.VMEM)
    return pl.pallas_call(
        first_kernel,
        in_specs=[pl.BlockSpec(memory_space=pltpu.SMEM), vmem, vmem],
        out_shape=(
            plane,
            jax.ShapeDtypeStruct((3, toks, lanes), f32),
            plane,
            plane,
            jax.ShapeDtypeStruct((OWNED, MESSAGE), f32),
        ),
        scratch_shapes=[
            pltpu.VMEM((chunks * ROWS_IN, toks), f32),
            pltpu.VMEM((4, PAD + toks, lanes), f32),
            pltpu.VMEM((toks, lanes), f32),
            pltpu.VMEM((toks, lanes), f32),
            pltpu.VMEM((3, toks, lanes), f32),
            pltpu.VMEM((2, 8 * toks, lanes // 2), f32),
            pltpu.VMEM((2, 8 * toks, lanes // 2), f32),
            pltpu.VMEM((16 * toks, lanes), f32),
            pltpu.VMEM((2 * TAPS, toks, lanes), f32),
            pltpu.VMEM((2, 8 * 24, lanes // 2), f32),
            pltpu.VMEM((MESSAGE, lanes), f32),
        ],
        compiler_params=pltpu.CompilerParams(vmem_limit_bytes=VMEM_LIMIT),
    )(half, recv, prm)


def run_second(half, own, other, prm, grad, hat, fwd, bwd):
    toks, lanes = grad.shape
    chunks = lanes // OWNED
    f32 = jnp.float32
    vmem = pl.BlockSpec(memory_space=pltpu.VMEM)
    return pl.pallas_call(
        second_kernel,
        in_specs=[pl.BlockSpec(memory_space=pltpu.SMEM)] + [vmem] * 7,
        out_shape=(
            jax.ShapeDtypeStruct((chunks, ROWS_OUT, toks), jnp.bfloat16),
            jax.ShapeDtypeStruct((OWNED, 2 * MODES), f32),
        ),
        scratch_shapes=[
            pltpu.VMEM((MESSAGE, lanes), f32),
            pltpu.VMEM((MESSAGE, lanes), f32),
            pltpu.VMEM((3, 16, lanes), f32),
            pltpu.VMEM((2, 8 * toks, lanes // 2), f32),
            pltpu.VMEM((4, toks, lanes), f32),
            pltpu.VMEM((3, toks + PAD, lanes), f32),
            pltpu.VMEM((chunks * ROWS_OUT, toks), f32),
        ],
        compiler_params=pltpu.CompilerParams(vmem_limit_bytes=VMEM_LIMIT),
    )(half, own, other, prm, grad, hat, fwd, bwd)


def run_unpack(recv):
    owners, _, toks = recv.shape
    chans = OWNED * owners
    whole = jax.ShapeDtypeStruct((chans, toks), jnp.bfloat16)
    return pl.pallas_call(
        unpack_kernel,
        out_shape=(whole,) * 4 + (jax.ShapeDtypeStruct((3, TAPS, chans), jnp.float32),),
        scratch_shapes=[
            pltpu.VMEM((owners * ROWS_OUT, toks), jnp.float32),
            pltpu.VMEM((5, chans, toks), jnp.float32),
        ],
        compiler_params=pltpu.CompilerParams(vmem_limit_bytes=VMEM_LIMIT),
    )(recv)


def parameter_rows(weights, residue, log_rate, chunks):
    rows = jnp.concatenate(
        [
            weights.reshape(3 * TAPS, OWNED),
            jnp.zeros((3, OWNED), jnp.float32),
            log_rate.T,
            residue.T,
        ],
        axis=0,
    )
    return jnp.repeat(rows, chunks, axis=1)


def local(query_in, key_in, value_in, short_weight, residue, log_rate, grad_out):
    devices = lax.axis_size("seq")
    chunks = devices // 2
    chans = query_in.shape[0]
    me = lax.axis_index("seq")
    half = me // chunks
    index = me % chunks
    groups = [list(range(chunks)), list(range(chunks, devices))]
    across = [(i, (i + chunks) % devices) for i in range(devices)]

    mine = jnp.concatenate([log_rate, residue], axis=1)
    theirs = lax.ppermute(mine, "seq", across)
    modal_params = jnp.where(
        half == 0, jnp.concatenate([mine, theirs]), jnp.concatenate([theirs, mine])
    )
    weights = jnp.concatenate(
        [
            lax.dynamic_slice(short_weight, (0, 0, 4 * index + at), (3, TAPS, 4))
            for at in (0, chans // 2)
        ],
        axis=2,
    )
    prm = parameter_rows(weights, modal_params[:, MODES:], modal_params[:, :MODES], chunks)
    which = half.reshape(1).astype(jnp.int32)

    send = run_pack(query_in, key_in, value_in, grad_out)
    recv = lax.all_to_all(send, "seq", 0, 0, tiled=True, axis_index_groups=groups)
    grad, hat, fwd, bwd, message = run_first(which, recv, prm)
    other = lax.ppermute(message, "seq", across)
    back, modal = run_second(which, message, other, prm, grad, hat, fwd, bwd)
    final = lax.all_to_all(back, "seq", 0, 0, tiled=True, axis_index_groups=groups)
    output, grad_query, grad_key, grad_value, grad_short = run_unpack(final)
    own_modal = lax.dynamic_slice(modal, (4 * half, 0), (4, 2 * MODES))
    return (
        output,
        grad_query,
        grad_key,
        grad_value,
        grad_short,
        own_modal[:, :MODES],
        own_modal[:, MODES:],
    )


def solution(mesh):
    return jax.shard_map(
        local,
        mesh=mesh,
        in_specs=(
            P("chan", "seq"),
            P("chan", "seq"),
            P("chan", "seq"),
            P(None, None, "chan"),
            P(("chan", "seq"), None),
            P(("chan", "seq"), None),
            P("chan", "seq"),
        ),
        out_specs=(
            P("chan", "seq"),
            P("chan", "seq"),
            P("chan", "seq"),
            P("chan", "seq"),
            P(None, None, "chan"),
            P(("chan", "seq"), None),
            P(("chan", "seq"), None),
        ),
        check_vma=False,
    )
```

```python
import math

import jax
import jax.numpy as jnp
from jax import lax
from jax.experimental import pallas as pl
from jax.experimental.pallas import tpu as pltpu
from jax.sharding import PartitionSpec as P

TAPS = 7
MODES = 16
PAD = 8
OWNED = 8
ROWS_IN = 4 * OWNED
ROWS_OUT = 40
VMEM_LIMIT = 40 * 1024 * 1024

STATE, DERIV, RSUM, KSUM, EDGE, SHORT, RESPONSE, MESSAGE = 0, 16, 32, 48, 64, 96, 128, 384


def first_row(chan, chans):
    return chan if chan < 4 else chans // 2 + chan - 4


def pack_kernel(query_ref, key_ref, value_ref, grad_ref, send_ref, held, wide, mixed_rows, sems):
    owners = send_ref.shape[0]
    chans = query_ref.shape[0]
    copies = [
        pltpu.make_async_copy(ref, held.at[stream], sems.at[stream])
        for stream, ref in enumerate((query_ref, key_ref, value_ref, grad_ref))
    ]
    for copy in copies:
        copy.start()
    for stream, copy in enumerate(copies):
        copy.wait()
        wide[stream] = held[stream].astype(jnp.float32)
        for chan in range(OWNED):
            mixed_rows[pl.ds(stream * OWNED + chan, owners, stride=ROWS_IN), :] = wide[
                stream, pl.ds(first_row(chan, chans), owners, stride=4), :
            ]
    send_ref[...] = mixed_rows[...].reshape(send_ref.shape).astype(jnp.bfloat16)


def unpack_kernel(recv_ref, out_ref, gq_ref, gk_ref, gv_ref, short_ref, rows, wide):
    owners = recv_ref.shape[0]
    chans = out_ref.shape[0]
    rows[...] = recv_ref[...].reshape(rows.shape).astype(jnp.float32)
    for stream, ref in enumerate((out_ref, gq_ref, gk_ref, gv_ref)):
        for chan in range(OWNED):
            wide[stream, pl.ds(first_row(chan, chans), owners, stride=4), :] = rows[
                pl.ds(stream * OWNED + chan, owners, stride=ROWS_OUT), :
            ]
        ref[...] = wide[stream].astype(jnp.bfloat16)
    for group in range(2):
        short = (
            rows[pl.ds(32 + group, owners, stride=ROWS_OUT), :]
            + rows[pl.ds(34 + group, owners, stride=ROWS_OUT), :]
        )
        for chan in range(4):
            wide[4, pl.ds(first_row(4 * group + chan, chans), owners, stride=4), :] = pltpu.roll(
                short, (128 - 32 * chan) % 128, 1
            )
    turned = wide[4].T
    for stream in range(3):
        short_ref[stream] = turned[stream * TAPS : (stream + 1) * TAPS, :]


def lane_ids(chunks, rows):
    lane = lax.broadcasted_iota(jnp.int32, (rows, OWNED * chunks), 1)
    return lane % chunks, lane // chunks


def owner_pick(chunks):
    owner = lane_ids(chunks, OWNED)[1]
    return (owner == lax.broadcasted_iota(jnp.int32, owner.shape, 0)).astype(jnp.float32)


def exact_dot(left, right, dims):
    return lax.dot_general(
        left,
        right,
        (dims, ((), ())),
        precision=lax.Precision.HIGHEST,
        preferred_element_type=jnp.float32,
    )


def modal_rows(prm_ref):
    rates = [jnp.exp(prm_ref[24 + 8 * i : 32 + 8 * i, :]) for i in range(2)]
    resid = [prm_ref[40 + 8 * i : 48 + 8 * i, :] for i in range(2)]
    decay = [jnp.exp(-r) for r in rates]
    root = [jnp.sqrt(2.0 * r) for r in rates]
    amp = [resid[i] * root[i] for i in range(2)]
    return rates, decay, root, amp


def keep(ref, tok, value):
    lanes = ref.shape[2]
    for half in range(2):
        ref[half, pl.ds(pl.multiple_of(8 * tok, 8), 8), :] = value[
            :, half * lanes : (half + 1) * lanes
        ]


def folded(ref, first, count):
    halves = []
    for half in range(2):
        total = None
        for sub in range(8):
            term = ref[half, pl.ds(first + sub, count, stride=8), :]
            total = term if total is None else total + term
        halves.append(total)
    return jnp.concatenate(halves, axis=1)


def tap_row(prm_ref, stream, tap):
    index = stream * TAPS + tap
    return prm_ref[index : index + 1, :]


def rounded(value):
    return value.astype(jnp.bfloat16).astype(jnp.float32)


def first_kernel(
    half_ref,
    recv_ref,
    prm_ref,
    grad_ref,
    hat_ref,
    fwd_ref,
    bwd_ref,
    msg_ref,
    raw,
    xt,
    mixed,
    gmixed,
    base,
    part_y,
    part_z,
    states,
    weighted,
    sums,
    rows,
):
    chunks = recv_ref.shape[0]
    toks = recv_ref.shape[2]
    lanes = OWNED * chunks
    f32 = jnp.float32
    chunk_of, _ = lane_ids(chunks, 8)
    half = half_ref[0]
    late = half.astype(f32)
    early = 1.0 - late
    zero = jnp.zeros((8, lanes), f32)
    block = 32

    raw[...] = recv_ref[...].reshape(raw.shape).astype(f32)
    per_tile = toks // chunks
    for stream in range(4):
        for group in range(OWNED // per_tile):
            tile = jnp.concatenate(
                [
                    raw[
                        pl.ds(stream * OWNED + group * per_tile + c, chunks, stride=ROWS_IN), :
                    ]
                    for c in range(per_tile)
                ],
                axis=0,
            )
            xt[stream, PAD : PAD + toks, group * toks : (group + 1) * toks] = tile.T
    for stream in range(3):
        tail = pltpu.roll(xt[stream, toks : toks + PAD, :], 1, 1)
        xt[stream, 0:PAD, :] = jnp.where(chunk_of >= 1, tail, 0.0)

    fringe = (lax.broadcasted_iota(jnp.int32, (8, lanes), 0) < TAPS - 1) & (chunk_of == 0)
    kept = 1.0 - jnp.where(fringe, late, 0.0)
    for start in range(0, toks, block):
        filtered = []
        for stream in range(3):
            total = None
            for tap in range(TAPS):
                lo = PAD - tap + start
                term = tap_row(prm_ref, stream, tap) * xt[stream, lo : lo + block, :]
                total = term if total is None else total + term
            filtered.append(total)
            hat_ref[stream, start : start + block, :] = total
        grad = xt[3, PAD + start : PAD + start + block, :]
        mixed[start : start + block, :] = rounded(filtered[1] * filtered[2])
        gmixed[start : start + block, :] = rounded(grad * filtered[0])
        grad_ref[start : start + block, :] = grad
        base[0, start : start + block, :] = grad
        base[1, start : start + block, :] = filtered[2]
        base[2, start : start + block, :] = filtered[1]
    mixed[0:8, :] = mixed[0:8, :] * kept
    gmixed[0:8, :] = gmixed[0:8, :] * kept
    for stream in range(3):
        base[stream, 0:8, :] = base[stream, 0:8, :] * kept

    rates, decay, _, amp = modal_rows(prm_ref)

    def row_of(ref, tok):
        return jnp.broadcast_to(ref[pl.ds(tok, 1), :], (8, lanes))

    def local_body(tok, carry):
        e0, e1, f0, f1 = carry
        xb = row_of(mixed, tok)
        gb = row_of(gmixed, toks - 1 - tok)
        return (
            decay[0] * e0 + xb,
            decay[1] * e1 + xb,
            decay[0] * f0 + gb,
            decay[1] * f1 + gb,
        )

    e0, e1, f0, f1 = lax.fori_loop(0, toks, local_body, (zero,) * 4, unroll=16)
    ends = [e0, e1]
    heads = [f0, f1]
    step = 1
    while step < chunks:
        for i in range(2):
            power = jnp.exp(rates[i] * (-1.0 * toks * step))
            moved = jnp.where(chunk_of >= step, pltpu.roll(ends[i], step, 1), 0.0)
            ends[i] = ends[i] + power * moved
            moved = jnp.where(chunk_of < chunks - step, pltpu.roll(heads[i], lanes - step, 1), 0.0)
            heads[i] = heads[i] + power * moved
        step *= 2
    start_h = [jnp.where(chunk_of >= 1, pltpu.roll(e, 1, 1), 0.0) for e in ends]
    start_p = [jnp.where(chunk_of < chunks - 1, pltpu.roll(f, lanes - 1, 1), 0.0) for f in heads]

    def forward_body(tok, carry):
        h0, h1, r0, r1, d0, d1 = carry
        xb = row_of(mixed, tok)
        gb = row_of(gmixed, tok)
        h0 = decay[0] * h0 + xb
        h1 = decay[1] * h1 + xb
        keep(part_y, tok, amp[0] * h0 + amp[1] * h1)
        states[pl.ds(pl.multiple_of(16 * tok, 8), 8), :] = h0
        states[pl.ds(pl.multiple_of(16 * tok + 8, 8), 8), :] = h1
        return (
            h0,
            h1,
            r0 + gb * h0,
            r1 + gb * h1,
            decay[0] * d0 + h0,
            decay[1] * d1 + h1,
        )

    _, _, r0, r1, d0, d1 = lax.fori_loop(
        0, toks, forward_body, (start_h[0], start_h[1]) + (zero,) * 4, unroll=16
    )

    def backward_body(step_index, carry):
        p0, p1, k0, k1, c0, c1 = carry
        tok = toks - 1 - step_index
        gb = row_of(gmixed, tok)
        q0 = decay[0] * p0
        q1 = decay[1] * p1
        k0 = k0 + states[pl.ds(pl.multiple_of(16 * tok, 8), 8), :] * q0
        k1 = k1 + states[pl.ds(pl.multiple_of(16 * tok + 8, 8), 8), :] * q1
        p0 = q0 + gb
        p1 = q1 + gb
        keep(part_z, tok, amp[0] * p0 + amp[1] * p1)
        return (p0, p1, k0, k1, decay[0] * c0 + p0, decay[1] * c1 + p1)

    _, _, k0, k1, c0, c1 = lax.fori_loop(
        0, toks, backward_body, (start_p[0], start_p[1]) + (zero,) * 4, unroll=16
    )

    for start in range(0, toks, block):
        fwd_ref[start : start + block, :] = folded(part_y, 8 * start, block)
        bwd_ref[start : start + block, :] = folded(part_z, 8 * start, block)

    for stream in range(3):
        tap_sums = [zero for _ in range(TAPS)]
        for start in range(0, toks, block):
            conv = (fwd_ref if stream == 0 else bwd_ref)[start : start + block, :]
            own = conv * base[stream, start : start + block, :]
            for tap in range(TAPS):
                lo = PAD - tap + start
                prod = own * xt[stream, lo : lo + block, :]
                for sub in range(0, block, 8):
                    tap_sums[tap] = tap_sums[tap] + prod[sub : sub + 8, :]
        for tap in range(TAPS):
            keep(sums, stream * TAPS + tap, tap_sums[tap])
    for index in range(3 * TAPS, 24):
        keep(sums, index, zero)
    rows[SHORT : SHORT + 24, :] = folded(sums, 0, 24)
    rows[SHORT + 24 : RESPONSE, :] = zero

    def fill(slot, stream):
        for tap in range(TAPS):
            for start in range(0, toks, block):
                lo = PAD - tap + start
                weighted[slot + tap, start : start + block, :] = (
                    base[stream, start : start + block, :] * xt[stream, lo : lo + block, :]
                )

    span_c = chunk_of.astype(f32)
    power_early = [jnp.exp(-r * (toks * (chunks - 1.0 - span_c) + 1.0)) for r in rates]
    power_late = [jnp.exp(-r * (toks * span_c - (TAPS - 2.0))) for r in rates]

    def respond(slot, powers, reverse):
        def body(step_index, carry):
            tok = toks - 1 - step_index if reverse else step_index
            out = []
            for tap in range(TAPS):
                wb = row_of(weighted.at[slot + tap], tok)
                for i in range(2):
                    out.append(decay[i] * carry[2 * tap + i] + wb)
            return tuple(out)

        total = lax.fori_loop(0, toks, body, (zero,) * (2 * TAPS), unroll=8)
        for tap in range(TAPS):
            for i in range(2):
                lo = RESPONSE + 16 * (slot + tap) + 8 * i
                rows[lo : lo + 8, :] = total[2 * tap + i] * powers[i]

    @pl.when(half == 0)
    def _():
        fill(0, 1)
        fill(TAPS, 2)
        respond(0, power_early, False)
        respond(TAPS, power_early, False)
        for stream in range(4):
            lo = EDGE + 8 * stream
            rows[lo : lo + 8, :] = jnp.where(
                chunk_of == chunks - 1, xt[stream, toks : toks + PAD, :], 0.0
            )
        for i in range(2):
            weight = jnp.exp(-rates[i] * (toks * (chunks - 1.0 - span_c)))
            rows[STATE + 8 * i : STATE + 8 * i + 8, :] = jnp.where(
                chunk_of == chunks - 1, ends[i], 0.0
            )
            rows[DERIV + 8 * i : DERIV + 8 * i + 8, :] = (d0, d1)[i] * weight

    @pl.when(half != 0)
    def _():
        fill(0, 0)
        respond(0, power_late, True)
        for lo in range(RESPONSE + 16 * TAPS, RESPONSE + 32 * TAPS, 8):
            rows[lo : lo + 8, :] = zero
        for stream in range(4):
            lo = EDGE + 8 * stream
            rows[lo : lo + 8, :] = jnp.where(chunk_of == 0, xt[stream, PAD : 2 * PAD, :], 0.0)
        for i in range(2):
            grow = jnp.exp(rates[i] * (TAPS - 1.0))
            weight = jnp.exp(-rates[i] * (toks * span_c))
            first = jnp.where(chunk_of == 0, heads[i], 0.0)
            rows[STATE + 8 * i : STATE + 8 * i + 8, :] = first * grow
            rows[DERIV + 8 * i : DERIV + 8 * i + 8, :] = (
                (c0, c1)[i] * weight - (TAPS - 1.0) * first
            ) * grow

    for i in range(2):
        rows[RSUM + 8 * i : RSUM + 8 * i + 8, :] = (r0, r1)[i]
        rows[KSUM + 8 * i : KSUM + 8 * i + 8, :] = (k0, k1)[i]
    for lo in range(RESPONSE + 32 * TAPS, MESSAGE, 8):
        rows[lo : lo + 8, :] = zero
    msg_ref[...] = exact_dot(owner_pick(chunks), rows[...], ((1,), (1,)))


def second_kernel(
    half_ref,
    own_ref,
    other_ref,
    prm_ref,
    grad_ref,
    hat_ref,
    fwd_ref,
    bwd_ref,
    send_ref,
    modal_ref,
    edge0,
    edge1,
    edges,
    part,
    outs,
    grads,
    out_rows,
):
    toks, lanes = grad_ref.shape
    chunks = lanes // OWNED
    f32 = jnp.float32
    chunk_of, _ = lane_ids(chunks, 8)
    scale = 1.0 / math.sqrt(2 * chunks * toks)
    half = half_ref[0]
    late = half.astype(f32)
    early = 1.0 - late
    rates, decay, root, amp = modal_rows(prm_ref)
    pick = owner_pick(chunks)
    fringe = TAPS - 1
    zero = jnp.zeros((8, lanes), f32)

    own = own_ref[...]
    other = other_ref[...]
    edge0[...] = exact_dot(own * early + other * late, pick, ((0,), (0,)))
    edge1[...] = exact_dot(own * late + other * early, pick, ((0,), (0,)))

    def pair(ref, first):
        return [ref[first + 8 * i : first + 8 * i + 8, :] for i in range(2)]

    row_id = lax.broadcasted_iota(jnp.int32, (8, lanes), 0)
    live = jnp.where(row_id < fringe, 1.0, 0.0)
    hats = []
    for stream in range(3):
        edges[stream, 0:8, :] = edge0[EDGE + 8 * stream : EDGE + 8 * stream + 8, :]
        edges[stream, 8:16, :] = edge1[EDGE + 8 * stream : EDGE + 8 * stream + 8, :]
        total = None
        for tap in range(TAPS):
            term = tap_row(prm_ref, stream, tap) * edges[stream, 8 - tap : 16 - tap, :]
            total = term if total is None else total + term
        hats.append(total)
    grad_edge = edge1[EDGE + 24 : EDGE + 32, :]
    x_edge = rounded(hats[1] * hats[2])
    g_edge = rounded(grad_edge * hats[0])

    state = pair(edge0, STATE)
    passed = []
    y_edge = zero
    for tok in range(fringe):
        xb = jnp.broadcast_to(x_edge[tok : tok + 1, :], (8, lanes))
        state = [decay[i] * state[i] + xb for i in range(2)]
        passed.append(state)
        line = jnp.sum(amp[0] * state[0] + amp[1] * state[1], axis=0, keepdims=True)
        y_edge = jnp.where(row_id == tok, line, y_edge)
    after = state
    back = pair(edge1, STATE)
    r_edge = [zero, zero]
    k_edge = [zero, zero]
    z_edge = zero
    adjoint = back
    for tok in range(fringe - 1, -1, -1):
        gb = jnp.broadcast_to(g_edge[tok : tok + 1, :], (8, lanes))
        moved = [decay[i] * adjoint[i] for i in range(2)]
        k_edge = [k_edge[i] + passed[tok][i] * moved[i] for i in range(2)]
        r_edge = [r_edge[i] + gb * passed[tok][i] for i in range(2)]
        adjoint = [moved[i] + gb for i in range(2)]
        line = jnp.sum(amp[0] * adjoint[0] + amp[1] * adjoint[1], axis=0, keepdims=True)
        z_edge = jnp.where(row_id == tok, line, z_edge)

    span_c = chunk_of.astype(f32)
    carry = []
    for i in range(2):
        into_late = after[i] * jnp.exp(-rates[i] * (toks * span_c - (fringe - 1.0)))
        into_early = adjoint[i] * jnp.exp(-rates[i] * (toks * (chunks - 1.0 - span_c) + 1.0))
        carry.append(amp[i] * (early * into_early + late * into_late))

    def reply_body(step_index, values):
        tok = half * step_index + (1 - half) * (toks - 1 - step_index)
        keep(part, tok, values[0] + values[1])
        return (values[0] * decay[0], values[1] * decay[1])

    lax.fori_loop(0, toks, reply_body, tuple(carry), unroll=16)

    patch = (row_id < fringe) & (chunk_of == 0) & (jnp.broadcast_to(late, (8, lanes)) > 0.5)
    y_edge = rounded(y_edge)
    z_edge = rounded(z_edge)
    for start, count in ((0, 8), (8, 24), (32, 32), (64, 32), (96, 32)):
        span = slice(start, start + count)
        reply = folded(part, 8 * start, count)
        conv = rounded(fwd_ref[span, :] + late * reply)
        turn = rounded(bwd_ref[span, :] + early * reply)
        hat = [hat_ref[stream, span, :] for stream in range(3)]
        if start == 0:
            conv = jnp.where(patch, y_edge, conv)
            turn = jnp.where(patch, z_edge, turn)
            hat = [jnp.where(patch, hats[stream], hat[stream]) for stream in range(3)]
        grads[0, span, :] = grad_ref[span, :] * conv
        grads[1, span, :] = turn * hat[2]
        grads[2, span, :] = turn * hat[1]
        outs[0, span, :] = hat[0] * conv
    edge_grads = (grad_edge * y_edge, z_edge * hats[2], z_edge * hats[1])
    for stream in range(3):
        head = pltpu.roll(grads[stream, 0:PAD, :], lanes - 1, 1)
        grads[stream, toks : toks + PAD, :] = jnp.where(
            chunk_of < chunks - 1, head, early * edge_grads[stream]
        )
    block = 32
    for stream in range(3):
        for start in range(0, toks, block):
            total = None
            for tap in range(TAPS):
                term = (
                    tap_row(prm_ref, stream, tap)
                    * grads[stream, start + tap : start + tap + block, :]
                )
                total = term if total is None else total + term
            outs[1 + stream, start : start + block, :] = total

    single = jnp.where(chunk_of == 0, scale, 0.0)
    forced = [amp[i] * after[i] for i in range(2)]
    turned = [amp[i] * adjoint[i] for i in range(2)]
    short = [
        edge0[SHORT + 8 * i : SHORT + 8 * i + 8, :] + edge1[SHORT + 8 * i : SHORT + 8 * i + 8, :]
        for i in range(3)
    ]
    for stream in range(3):
        live_grad = edge_grads[stream] * live
        for tap in range(TAPS):
            index = stream * TAPS + tap
            term = live_grad * edges[stream, 8 - tap : 16 - tap, :]
            ref, slot = (edge1, tap) if stream == 0 else (edge0, (stream - 1) * TAPS + tap)
            drive = forced if stream == 0 else turned
            for i in range(2):
                lo = RESPONSE + 16 * slot + 8 * i
                term = term + drive[i] * ref[lo : lo + 8, :]
            line = jnp.sum(term, axis=0, keepdims=True)
            short[index // 8] = short[index // 8] + jnp.where(row_id == index % 8, line, 0.0)
    r_all = []
    k_all = []
    for i in range(2):
        first_r, late_r = pair(edge0, RSUM)[i], pair(edge1, RSUM)[i]
        first_k, late_k = pair(edge0, KSUM)[i], pair(edge1, KSUM)[i]
        lag_early, lag_late = pair(edge0, DERIV)[i], pair(edge1, DERIV)[i]
        r_all.append(first_r + late_r + decay[i] * back[i] * after[i] + r_edge[i])
        k_all.append(
            first_k
            + late_k
            + decay[i] * lag_early * adjoint[i]
            + decay[i] * after[i] * (lag_late - back[i])
            + k_edge[i]
        )
    every = jnp.concatenate(
        [value * single for value in short]
        + [root[i] * r_all[i] * single for i in range(2)]
        + [amp[i] * (0.5 * r_all[i] - rates[i] * k_all[i]) * single for i in range(2)],
        axis=0,
    )
    totals = exact_dot(pick, every, ((1,), (1,)))
    modal_ref[...] = totals[:, 24:56]

    per_tile = toks // chunks
    for stream in range(4):
        for group in range(OWNED // per_tile):
            tile = outs[stream, :, group * toks : (group + 1) * toks].T
            for c in range(per_tile):
                out_rows[
                    pl.ds(stream * OWNED + group * per_tile + c, chunks, stride=ROWS_OUT), :
                ] = tile[c * chunks : (c + 1) * chunks]
    wide = jnp.concatenate([totals[:, 0:24], jnp.zeros((8, toks - 24), f32)], axis=1)
    for group in range(2):
        line = wide[4 * group : 4 * group + 1, :]
        for chan in range(1, 4):
            at = 4 * group + chan
            line = line + pltpu.roll(wide, 32 * chan, 1)[at : at + 1, :]
        upper = rounded(line)
        out_rows[pl.ds(32 + group, chunks, stride=ROWS_OUT), :] = jnp.broadcast_to(
            upper, (chunks, toks)
        )
        out_rows[pl.ds(34 + group, chunks, stride=ROWS_OUT), :] = jnp.broadcast_to(
            line - upper, (chunks, toks)
        )
    for spare in range(36, ROWS_OUT):
        out_rows[pl.ds(spare, chunks, stride=ROWS_OUT), :] = jnp.zeros((chunks, toks), f32)
    send_ref[...] = out_rows[...].reshape(send_ref.shape).astype(jnp.bfloat16)


def run_pack(query_in, key_in, value_in, grad_out):
    chans, toks = query_in.shape
    owners = chans // OWNED
    return pl.pallas_call(
        pack_kernel,
        in_specs=[pl.BlockSpec(memory_space=pltpu.HBM)] * 4,
        out_shape=jax.ShapeDtypeStruct((owners, ROWS_IN, toks), jnp.bfloat16),
        scratch_shapes=[
            pltpu.VMEM((4, chans, toks), jnp.bfloat16),
            pltpu.VMEM((4, chans, toks), jnp.float32),
            pltpu.VMEM((owners * ROWS_IN, toks), jnp.float32),
            pltpu.SemaphoreType.DMA((4,)),
        ],
        compiler_params=pltpu.CompilerParams(vmem_limit_bytes=VMEM_LIMIT),
    )(*[pltpu.with_memory_space_constraint(x, pltpu.HBM) for x in (query_in, key_in, value_in, grad_out)])


def modal_kernel(rate_ref, residue_ref, after_ref, both_ref):
    both_ref[:, :MODES] = rate_ref[...]
    both_ref[:, MODES:] = residue_ref[...]


def run_modal(log_rate, residue, after):
    vmem = pl.BlockSpec(memory_space=pltpu.VMEM)
    return pl.pallas_call(
        modal_kernel,
        in_specs=[vmem, vmem, pl.BlockSpec(memory_space=pltpu.HBM)],
        out_shape=jax.ShapeDtypeStruct((log_rate.shape[0], 2 * MODES), jnp.float32),
        cost_estimate=pl.CostEstimate(flops=10**10, bytes_accessed=10**8, transcendentals=0),
    )(log_rate, residue, pltpu.with_memory_space_constraint(after, pltpu.HBM))


def run_first(half, recv, prm):
    chunks, _, toks = recv.shape
    lanes = OWNED * chunks
    f32 = jnp.float32
    plane = jax.ShapeDtypeStruct((toks, lanes), f32)
    vmem = pl.BlockSpec(memory_space=pltpu.VMEM)
    return pl.pallas_call(
        first_kernel,
        in_specs=[pl.BlockSpec(memory_space=pltpu.SMEM), vmem, vmem],
        out_shape=(
            plane,
            jax.ShapeDtypeStruct((3, toks, lanes), f32),
            plane,
            plane,
            jax.ShapeDtypeStruct((OWNED, MESSAGE), f32),
        ),
        scratch_shapes=[
            pltpu.VMEM((chunks * ROWS_IN, toks), f32),
            pltpu.VMEM((4, PAD + toks, lanes), f32),
            pltpu.VMEM((toks, lanes), f32),
            pltpu.VMEM((toks, lanes), f32),
            pltpu.VMEM((3, toks, lanes), f32),
            pltpu.VMEM((2, 8 * toks, lanes // 2), f32),
            pltpu.VMEM((2, 8 * toks, lanes // 2), f32),
            pltpu.VMEM((16 * toks, lanes), f32),
            pltpu.VMEM((2 * TAPS, toks, lanes), f32),
            pltpu.VMEM((2, 8 * 24, lanes // 2), f32),
            pltpu.VMEM((MESSAGE, lanes), f32),
        ],
        compiler_params=pltpu.CompilerParams(vmem_limit_bytes=VMEM_LIMIT),
    )(half, recv, prm)


def run_second(half, own, other, prm, grad, hat, fwd, bwd):
    toks, lanes = grad.shape
    chunks = lanes // OWNED
    f32 = jnp.float32
    vmem = pl.BlockSpec(memory_space=pltpu.VMEM)
    return pl.pallas_call(
        second_kernel,
        in_specs=[pl.BlockSpec(memory_space=pltpu.SMEM)] + [vmem] * 7,
        out_shape=(
            jax.ShapeDtypeStruct((chunks, ROWS_OUT, toks), jnp.bfloat16),
            jax.ShapeDtypeStruct((OWNED, 2 * MODES), f32),
        ),
        scratch_shapes=[
            pltpu.VMEM((MESSAGE, lanes), f32),
            pltpu.VMEM((MESSAGE, lanes), f32),
            pltpu.VMEM((3, 16, lanes), f32),
            pltpu.VMEM((2, 8 * toks, lanes // 2), f32),
            pltpu.VMEM((4, toks, lanes), f32),
            pltpu.VMEM((3, toks + PAD, lanes), f32),
            pltpu.VMEM((chunks * ROWS_OUT, toks), f32),
        ],
        compiler_params=pltpu.CompilerParams(vmem_limit_bytes=VMEM_LIMIT),
    )(half, own, other, prm, grad, hat, fwd, bwd)


def run_unpack(recv):
    owners, _, toks = recv.shape
    chans = OWNED * owners
    whole = jax.ShapeDtypeStruct((chans, toks), jnp.bfloat16)
    return pl.pallas_call(
        unpack_kernel,
        out_shape=(whole,) * 4 + (jax.ShapeDtypeStruct((3, TAPS, chans), jnp.float32),),
        scratch_shapes=[
            pltpu.VMEM((owners * ROWS_OUT, toks), jnp.float32),
            pltpu.VMEM((5, chans, toks), jnp.float32),
        ],
        compiler_params=pltpu.CompilerParams(vmem_limit_bytes=VMEM_LIMIT),
    )(recv)


def parameter_rows(weights, residue, log_rate, chunks):
    rows = jnp.concatenate(
        [
            weights.reshape(3 * TAPS, OWNED),
            jnp.zeros((3, OWNED), jnp.float32),
            log_rate.T,
            residue.T,
        ],
        axis=0,
    )
    return jnp.repeat(rows, chunks, axis=1)


def local(query_in, key_in, value_in, short_weight, residue, log_rate, grad_out):
    devices = lax.axis_size("seq")
    chunks = devices // 2
    chans = query_in.shape[0]
    me = lax.axis_index("seq")
    half = me // chunks
    index = me % chunks
    groups = [list(range(chunks)), list(range(chunks, devices))]
    across = [(i, (i + chunks) % devices) for i in range(devices)]

    send = run_pack(query_in, key_in, value_in, grad_out)
    mine = run_modal(log_rate, residue, send)
    theirs = lax.ppermute(mine, "seq", across)
    modal_params = jnp.where(
        half == 0, jnp.concatenate([mine, theirs]), jnp.concatenate([theirs, mine])
    )
    weights = jnp.concatenate(
        [
            lax.dynamic_slice(short_weight, (0, 0, 4 * index + at), (3, TAPS, 4))
            for at in (0, chans // 2)
        ],
        axis=2,
    )
    prm = parameter_rows(weights, modal_params[:, MODES:], modal_params[:, :MODES], chunks)
    which = half.reshape(1).astype(jnp.int32)

    recv = lax.all_to_all(send, "seq", 0, 0, tiled=True, axis_index_groups=groups)
    grad, hat, fwd, bwd, message = run_first(which, recv, prm)
    other = lax.ppermute(message, "seq", across)
    back, modal = run_second(which, message, other, prm, grad, hat, fwd, bwd)
    final = lax.all_to_all(back, "seq", 0, 0, tiled=True, axis_index_groups=groups)
    output, grad_query, grad_key, grad_value, grad_short = run_unpack(final)
    own_modal = lax.dynamic_slice(modal, (4 * half, 0), (4, 2 * MODES))
    return (
        output,
        grad_query,
        grad_key,
        grad_value,
        grad_short,
        own_modal[:, :MODES],
        own_modal[:, MODES:],
    )


def solution(mesh):
    return jax.shard_map(
        local,
        mesh=mesh,
        in_specs=(
            P("chan", "seq"),
            P("chan", "seq"),
            P("chan", "seq"),
            P(None, None, "chan"),
            P(("chan", "seq"), None),
            P(("chan", "seq"), None),
            P("chan", "seq"),
        ),
        out_specs=(
            P("chan", "seq"),
            P("chan", "seq"),
            P("chan", "seq"),
            P("chan", "seq"),
            P(None, None, "chan"),
            P(("chan", "seq"), None),
            P(("chan", "seq"), None),
        ),
        check_vma=False,
    )
```

```python
import math

import jax
import jax.numpy as jnp
from jax import lax
from jax.experimental import pallas as pl
from jax.experimental.pallas import tpu as pltpu
from jax.sharding import PartitionSpec as P

TAPS = 7
MODES = 16
PAD = 8
OWNED = 8
ROWS_IN = 4 * OWNED
ROWS_OUT = 40
VMEM_LIMIT = 40 * 1024 * 1024

STATE, DERIV, RSUM, KSUM, EDGE, SHORT, COMPACT = 0, 16, 32, 48, 64, 96, 128
MESSAGE = OWNED + 16


def first_row(chan, chans):
    return chan if chan < 4 else chans // 2 + chan - 4


def pack_kernel(query_ref, key_ref, value_ref, grad_ref, send_ref, held, wide, mixed_rows, sems):
    owners = send_ref.shape[0]
    chans = query_ref.shape[0]
    copies = [
        pltpu.make_async_copy(ref, held.at[stream], sems.at[stream])
        for stream, ref in enumerate((query_ref, key_ref, value_ref, grad_ref))
    ]
    for copy in copies:
        copy.start()
    for stream, copy in enumerate(copies):
        copy.wait()
        wide[stream] = held[stream].astype(jnp.float32)
        for chan in range(OWNED):
            mixed_rows[pl.ds(stream * OWNED + chan, owners, stride=ROWS_IN), :] = wide[
                stream, pl.ds(first_row(chan, chans), owners, stride=4), :
            ]
    send_ref[...] = mixed_rows[...].reshape(send_ref.shape).astype(jnp.bfloat16)


def unpack_kernel(recv_ref, out_ref, gq_ref, gk_ref, gv_ref, short_ref, rows, wide):
    owners = recv_ref.shape[0]
    chans = out_ref.shape[0]
    rows[...] = recv_ref[...].reshape(rows.shape).astype(jnp.float32)
    for stream, ref in enumerate((out_ref, gq_ref, gk_ref, gv_ref)):
        for chan in range(OWNED):
            wide[stream, pl.ds(first_row(chan, chans), owners, stride=4), :] = rows[
                pl.ds(stream * OWNED + chan, owners, stride=ROWS_OUT), :
            ]
        ref[...] = wide[stream].astype(jnp.bfloat16)
    for group in range(2):
        short = (
            rows[pl.ds(32 + group, owners, stride=ROWS_OUT), :]
            + rows[pl.ds(34 + group, owners, stride=ROWS_OUT), :]
        )
        for chan in range(4):
            wide[4, pl.ds(first_row(4 * group + chan, chans), owners, stride=4), :] = pltpu.roll(
                short, (128 - 32 * chan) % 128, 1
            )
    turned = wide[4].T
    for stream in range(3):
        short_ref[stream] = turned[stream * TAPS : (stream + 1) * TAPS, :]


def lane_ids(chunks, rows):
    lane = lax.broadcasted_iota(jnp.int32, (rows, OWNED * chunks), 1)
    return lane % chunks, lane // chunks


def owner_pick(chunks):
    owner = lane_ids(chunks, OWNED)[1]
    return (owner == lax.broadcasted_iota(jnp.int32, owner.shape, 0)).astype(jnp.float32)


def three_parts(value):
    upper = rounded(value)
    middle = rounded(value - upper)
    return [upper, middle, value - upper - middle]


def lane_sums(value, chunks):
    shape = (value.shape[1], 128)
    owner = lax.broadcasted_iota(jnp.int32, shape, 0) // chunks
    pick = (owner == lax.broadcasted_iota(jnp.int32, shape, 1)).astype(jnp.float32)
    pick = pick.astype(jnp.bfloat16)
    total = None
    for part in reversed(three_parts(value)):
        term = jnp.dot(part.astype(jnp.bfloat16), pick, preferred_element_type=jnp.float32)
        total = term if total is None else total + term
    return total


def lane_spread(value, chunks):
    pick = owner_pick(chunks)
    return lax.dot_general(
        jnp.concatenate(three_parts(value), axis=0).astype(jnp.bfloat16),
        jnp.concatenate([pick] * 3, axis=0).astype(jnp.bfloat16),
        (((0,), (0,)), ((), ())),
        preferred_element_type=jnp.float32,
    )


def one_line(value, first, count, width):
    line = value[first : first + 1, :]
    for chan in range(1, count):
        at = first + chan
        line = line + pltpu.roll(value, width * chan, 1)[at : at + 1, :]
    return line


def modal_rows(prm_ref):
    rates = [jnp.exp(prm_ref[24 + 8 * i : 32 + 8 * i, :]) for i in range(2)]
    resid = [prm_ref[40 + 8 * i : 48 + 8 * i, :] for i in range(2)]
    decay = [jnp.exp(-r) for r in rates]
    root = [jnp.sqrt(2.0 * r) for r in rates]
    amp = [resid[i] * root[i] for i in range(2)]
    return rates, decay, root, amp


def keep(ref, tok, value):
    lanes = ref.shape[2]
    for half in range(2):
        ref[half, pl.ds(pl.multiple_of(8 * tok, 8), 8), :] = value[
            :, half * lanes : (half + 1) * lanes
        ]


def folded(ref, first, count):
    halves = []
    for half in range(2):
        total = None
        for sub in range(8):
            term = ref[half, pl.ds(first + sub, count, stride=8), :]
            total = term if total is None else total + term
        halves.append(total)
    return jnp.concatenate(halves, axis=1)


def tap_row(prm_ref, stream, tap):
    index = stream * TAPS + tap
    return prm_ref[index : index + 1, :]


def rounded(value):
    return value.astype(jnp.bfloat16).astype(jnp.float32)


def first_kernel(
    half_ref,
    recv_ref,
    prm_ref,
    rate_ref,
    grad_ref,
    hat_ref,
    fwd_ref,
    bwd_ref,
    msg_ref,
    raw,
    xt,
    mixed,
    gmixed,
    base,
    part_y,
    part_z,
    states,
    upper_w,
    lower_w,
    sums,
    rows,
):
    chunks = recv_ref.shape[0]
    toks = recv_ref.shape[2]
    lanes = OWNED * chunks
    f32 = jnp.float32
    chunk_of, _ = lane_ids(chunks, 8)
    half = half_ref[0]
    late = half.astype(f32)
    early = 1.0 - late
    zero = jnp.zeros((8, lanes), f32)
    block = 32

    raw[...] = recv_ref[...].reshape(raw.shape).astype(f32)
    per_tile = toks // chunks
    for stream in range(4):
        for group in range(OWNED // per_tile):
            tile = jnp.concatenate(
                [
                    raw[
                        pl.ds(stream * OWNED + group * per_tile + c, chunks, stride=ROWS_IN), :
                    ]
                    for c in range(per_tile)
                ],
                axis=0,
            )
            xt[stream, PAD : PAD + toks, group * toks : (group + 1) * toks] = tile.T
    for stream in range(3):
        tail = pltpu.roll(xt[stream, toks : toks + PAD, :], 1, 1)
        xt[stream, 0:PAD, :] = jnp.where(chunk_of >= 1, tail, 0.0)

    fringe = (lax.broadcasted_iota(jnp.int32, (8, lanes), 0) < TAPS - 1) & (chunk_of == 0)
    kept = 1.0 - jnp.where(fringe, late, 0.0)
    for start in range(0, toks, block):
        filtered = []
        for stream in range(3):
            total = None
            for tap in range(TAPS):
                lo = PAD - tap + start
                term = tap_row(prm_ref, stream, tap) * xt[stream, lo : lo + block, :]
                total = term if total is None else total + term
            filtered.append(total)
            hat_ref[stream, start : start + block, :] = total
        grad = xt[3, PAD + start : PAD + start + block, :]
        mixed[start : start + block, :] = rounded(filtered[1] * filtered[2])
        gmixed[start : start + block, :] = rounded(grad * filtered[0])
        grad_ref[start : start + block, :] = grad
        base[0, start : start + block, :] = grad
        base[1, start : start + block, :] = filtered[2]
        base[2, start : start + block, :] = filtered[1]
    mixed[0:8, :] = mixed[0:8, :] * kept
    gmixed[0:8, :] = gmixed[0:8, :] * kept
    for stream in range(3):
        base[stream, 0:8, :] = base[stream, 0:8, :] * kept

    rates, decay, _, amp = modal_rows(prm_ref)

    def row_of(ref, tok):
        return jnp.broadcast_to(ref[pl.ds(tok, 1), :], (8, lanes))

    def local_body(tok, carry):
        e0, e1, f0, f1 = carry
        xb = row_of(mixed, tok)
        gb = row_of(gmixed, toks - 1 - tok)
        return (
            decay[0] * e0 + xb,
            decay[1] * e1 + xb,
            decay[0] * f0 + gb,
            decay[1] * f1 + gb,
        )

    e0, e1, f0, f1 = lax.fori_loop(0, toks, local_body, (zero,) * 4, unroll=16)
    ends = [e0, e1]
    heads = [f0, f1]
    step = 1
    while step < chunks:
        for i in range(2):
            power = jnp.exp(rates[i] * (-1.0 * toks * step))
            moved = jnp.where(chunk_of >= step, pltpu.roll(ends[i], step, 1), 0.0)
            ends[i] = ends[i] + power * moved
            moved = jnp.where(chunk_of < chunks - step, pltpu.roll(heads[i], lanes - step, 1), 0.0)
            heads[i] = heads[i] + power * moved
        step *= 2
    start_h = [jnp.where(chunk_of >= 1, pltpu.roll(e, 1, 1), 0.0) for e in ends]
    start_p = [jnp.where(chunk_of < chunks - 1, pltpu.roll(f, lanes - 1, 1), 0.0) for f in heads]

    def forward_body(tok, carry):
        h0, h1, r0, r1, d0, d1 = carry
        xb = row_of(mixed, tok)
        gb = row_of(gmixed, tok)
        h0 = decay[0] * h0 + xb
        h1 = decay[1] * h1 + xb
        keep(part_y, tok, amp[0] * h0 + amp[1] * h1)
        states[pl.ds(pl.multiple_of(16 * tok, 8), 8), :] = h0
        states[pl.ds(pl.multiple_of(16 * tok + 8, 8), 8), :] = h1
        return (
            h0,
            h1,
            r0 + gb * h0,
            r1 + gb * h1,
            decay[0] * d0 + h0,
            decay[1] * d1 + h1,
        )

    _, _, r0, r1, d0, d1 = lax.fori_loop(
        0, toks, forward_body, (start_h[0], start_h[1]) + (zero,) * 4, unroll=16
    )

    def backward_body(step_index, carry):
        p0, p1, k0, k1, c0, c1 = carry
        tok = toks - 1 - step_index
        gb = row_of(gmixed, tok)
        q0 = decay[0] * p0
        q1 = decay[1] * p1
        k0 = k0 + states[pl.ds(pl.multiple_of(16 * tok, 8), 8), :] * q0
        k1 = k1 + states[pl.ds(pl.multiple_of(16 * tok + 8, 8), 8), :] * q1
        p0 = q0 + gb
        p1 = q1 + gb
        keep(part_z, tok, amp[0] * p0 + amp[1] * p1)
        return (p0, p1, k0, k1, decay[0] * c0 + p0, decay[1] * c1 + p1)

    _, _, k0, k1, c0, c1 = lax.fori_loop(
        0, toks, backward_body, (start_p[0], start_p[1]) + (zero,) * 4, unroll=16
    )

    for start in range(0, toks, block):
        fwd_ref[start : start + block, :] = folded(part_y, 8 * start, block)
        bwd_ref[start : start + block, :] = folded(part_z, 8 * start, block)

    for stream in range(3):
        tap_sums = [zero for _ in range(TAPS)]
        for start in range(0, toks, block):
            conv = (fwd_ref if stream == 0 else bwd_ref)[start : start + block, :]
            own = conv * base[stream, start : start + block, :]
            for tap in range(TAPS):
                lo = PAD - tap + start
                prod = own * xt[stream, lo : lo + block, :]
                for sub in range(0, block, 8):
                    tap_sums[tap] = tap_sums[tap] + prod[sub : sub + 8, :]
        for tap in range(TAPS):
            keep(sums, stream * TAPS + tap, tap_sums[tap])
    for index in range(3 * TAPS, 24):
        keep(sums, index, zero)
    rows[SHORT : SHORT + 24, :] = folded(sums, 0, 24)
    rows[SHORT + 24 : COMPACT, :] = zero

    bf16 = jnp.bfloat16
    rate_line = jnp.exp(rate_ref[...])
    rate_line = jnp.concatenate([rate_line, jnp.zeros((OWNED, toks - MODES), f32)], axis=1)
    rate_line = one_line(rate_line, 0, OWNED, MODES)
    row_lane = lax.broadcasted_iota(jnp.int32, (lanes, toks), 0)
    col_owner = lax.broadcasted_iota(jnp.int32, (lanes, toks), 1) // MODES
    row_chunk = (row_lane % chunks).astype(f32)
    spread = late * (toks * row_chunk - (TAPS - 2.0)) + early * (
        toks * (chunks - 1.0 - row_chunk) + 1.0
    )
    across = jnp.where(row_lane // chunks == col_owner, jnp.exp(-rate_line * spread), 0.0)
    across_hi = across.astype(bf16)
    across_lo = (across - across_hi.astype(f32)).astype(bf16)
    row_tok = lax.broadcasted_iota(jnp.int32, (toks, toks), 0).astype(f32)
    along = jnp.exp(-rate_line * (late * row_tok + early * (toks - 1.0 - row_tok)))

    def respond(slot, stream):
        for tap in range(TAPS):
            for start in range(0, toks, block):
                span = slice(start, start + block)
                lo = PAD - tap + start
                value = base[stream, span, :] * xt[stream, lo : lo + block, :]
                upper = value.astype(bf16)
                upper_w[tap, span, :] = upper
                lower_w[tap, span, :] = (value - upper.astype(f32)).astype(bf16)
            total = (
                jnp.dot(upper_w[tap], across_lo, preferred_element_type=f32)
                + jnp.dot(lower_w[tap], across_hi, preferred_element_type=f32)
                + jnp.dot(upper_w[tap], across_hi, preferred_element_type=f32)
            )
            at = OWNED + slot + tap
            msg_ref[at : at + 1, :] = jnp.sum(total * along, axis=0, keepdims=True)

    span_c = chunk_of.astype(f32)
    msg_ref[OWNED:MESSAGE, :] = jnp.zeros((MESSAGE - OWNED, toks), f32)

    @pl.when(half == 0)
    def _():
        respond(0, 1)
        respond(TAPS, 2)
        for stream in range(4):
            lo = EDGE + 8 * stream
            rows[lo : lo + 8, :] = jnp.where(
                chunk_of == chunks - 1, xt[stream, toks : toks + PAD, :], 0.0
            )
        for i in range(2):
            weight = jnp.exp(-rates[i] * (toks * (chunks - 1.0 - span_c)))
            rows[STATE + 8 * i : STATE + 8 * i + 8, :] = jnp.where(
                chunk_of == chunks - 1, ends[i], 0.0
            )
            rows[DERIV + 8 * i : DERIV + 8 * i + 8, :] = (d0, d1)[i] * weight

    @pl.when(half != 0)
    def _():
        respond(0, 0)
        for stream in range(4):
            lo = EDGE + 8 * stream
            rows[lo : lo + 8, :] = jnp.where(chunk_of == 0, xt[stream, PAD : 2 * PAD, :], 0.0)
        for i in range(2):
            grow = jnp.exp(rates[i] * (TAPS - 1.0))
            weight = jnp.exp(-rates[i] * (toks * span_c))
            first = jnp.where(chunk_of == 0, heads[i], 0.0)
            rows[STATE + 8 * i : STATE + 8 * i + 8, :] = first * grow
            rows[DERIV + 8 * i : DERIV + 8 * i + 8, :] = (
                (c0, c1)[i] * weight - (TAPS - 1.0) * first
            ) * grow

    for i in range(2):
        rows[RSUM + 8 * i : RSUM + 8 * i + 8, :] = (r0, r1)[i]
        rows[KSUM + 8 * i : KSUM + 8 * i + 8, :] = (k0, k1)[i]
    msg_ref[0:OWNED, :] = lane_sums(rows[...], chunks).T[:OWNED, :]


def second_kernel(
    half_ref,
    own_ref,
    other_ref,
    prm_ref,
    grad_ref,
    hat_ref,
    fwd_ref,
    bwd_ref,
    send_ref,
    modal_ref,
    edge0,
    edge1,
    edges,
    part,
    driven,
    outs,
    grads,
    out_rows,
):
    toks, lanes = grad_ref.shape
    chunks = lanes // OWNED
    f32 = jnp.float32
    chunk_of, _ = lane_ids(chunks, 8)
    scale = 1.0 / math.sqrt(2 * chunks * toks)
    half = half_ref[0]
    late = half.astype(f32)
    early = 1.0 - late
    rates, decay, root, amp = modal_rows(prm_ref)
    fringe = TAPS - 1
    zero = jnp.zeros((8, lanes), f32)

    own = own_ref[...]
    other = other_ref[...]
    message0 = own * early + other * late
    message1 = own * late + other * early
    edge0[...] = lane_spread(message0[0:OWNED, :], chunks)
    edge1[...] = lane_spread(message1[0:OWNED, :], chunks)

    def pair(ref, first):
        return [ref[first + 8 * i : first + 8 * i + 8, :] for i in range(2)]

    row_id = lax.broadcasted_iota(jnp.int32, (8, lanes), 0)
    live = jnp.where(row_id < fringe, 1.0, 0.0)
    hats = []
    for stream in range(3):
        edges[stream, 0:8, :] = edge0[EDGE + 8 * stream : EDGE + 8 * stream + 8, :]
        edges[stream, 8:16, :] = edge1[EDGE + 8 * stream : EDGE + 8 * stream + 8, :]
        total = None
        for tap in range(TAPS):
            term = tap_row(prm_ref, stream, tap) * edges[stream, 8 - tap : 16 - tap, :]
            total = term if total is None else total + term
        hats.append(total)
    grad_edge = edge1[EDGE + 24 : EDGE + 32, :]
    x_edge = rounded(hats[1] * hats[2])
    g_edge = rounded(grad_edge * hats[0])

    state = pair(edge0, STATE)
    passed = []
    y_edge = zero
    for tok in range(fringe):
        xb = jnp.broadcast_to(x_edge[tok : tok + 1, :], (8, lanes))
        state = [decay[i] * state[i] + xb for i in range(2)]
        passed.append(state)
        line = jnp.sum(amp[0] * state[0] + amp[1] * state[1], axis=0, keepdims=True)
        y_edge = jnp.where(row_id == tok, line, y_edge)
    after = state
    back = pair(edge1, STATE)
    r_edge = [zero, zero]
    k_edge = [zero, zero]
    z_edge = zero
    adjoint = back
    for tok in range(fringe - 1, -1, -1):
        gb = jnp.broadcast_to(g_edge[tok : tok + 1, :], (8, lanes))
        moved = [decay[i] * adjoint[i] for i in range(2)]
        k_edge = [k_edge[i] + passed[tok][i] * moved[i] for i in range(2)]
        r_edge = [r_edge[i] + gb * passed[tok][i] for i in range(2)]
        adjoint = [moved[i] + gb for i in range(2)]
        line = jnp.sum(amp[0] * adjoint[0] + amp[1] * adjoint[1], axis=0, keepdims=True)
        z_edge = jnp.where(row_id == tok, line, z_edge)

    span_c = chunk_of.astype(f32)
    carry = []
    for i in range(2):
        into_late = after[i] * jnp.exp(-rates[i] * (toks * span_c - (fringe - 1.0)))
        into_early = adjoint[i] * jnp.exp(-rates[i] * (toks * (chunks - 1.0 - span_c) + 1.0))
        carry.append(amp[i] * (early * into_early + late * into_late))

    sub = row_id.astype(f32)[:, :128]
    sub = late * sub + early * (7.0 - sub)
    stride8 = [jnp.exp(-8.0 * r) for r in rates]
    blocks = toks // 8
    for cut in range(lanes // 128):
        cols = slice(cut * 128, (cut + 1) * 128)
        modes = []
        factors = []
        for i in range(2):
            for m in range(8):
                rate = jnp.broadcast_to(rates[i][m : m + 1, cols], (8, 128))
                lead = jnp.broadcast_to(carry[i][m : m + 1, cols], (8, 128))
                modes.append(lead * jnp.exp(-rate * sub))
                factors.append(jnp.broadcast_to(stride8[i][m : m + 1, cols], (8, 128)))

        def reply_body(step_index, values, cols=cols, factors=factors):
            at = half * step_index + (1 - half) * (blocks - 1 - step_index)
            total = list(values)
            while len(total) > 1:
                total = [total[k] + total[k + 1] for k in range(0, len(total), 2)]
            part[pl.ds(pl.multiple_of(8 * at, 8), 8), cols] = total[0]
            return tuple(v * f for v, f in zip(values, factors))

        lax.fori_loop(0, blocks, reply_body, tuple(modes), unroll=4)

    patch = (row_id < fringe) & (chunk_of == 0) & (jnp.broadcast_to(late, (8, lanes)) > 0.5)
    y_edge = rounded(y_edge)
    z_edge = rounded(z_edge)
    for start, count in ((0, 8), (8, 24), (32, 32), (64, 32), (96, 32)):
        span = slice(start, start + count)
        reply = part[span, :]
        conv = rounded(fwd_ref[span, :] + late * reply)
        turn = rounded(bwd_ref[span, :] + early * reply)
        hat = [hat_ref[stream, span, :] for stream in range(3)]
        if start == 0:
            conv = jnp.where(patch, y_edge, conv)
            turn = jnp.where(patch, z_edge, turn)
            hat = [jnp.where(patch, hats[stream], hat[stream]) for stream in range(3)]
        grads[0, span, :] = grad_ref[span, :] * conv
        grads[1, span, :] = turn * hat[2]
        grads[2, span, :] = turn * hat[1]
        outs[0, span, :] = hat[0] * conv
    edge_grads = (grad_edge * y_edge, z_edge * hats[2], z_edge * hats[1])
    for stream in range(3):
        head = pltpu.roll(grads[stream, 0:PAD, :], lanes - 1, 1)
        grads[stream, toks : toks + PAD, :] = jnp.where(
            chunk_of < chunks - 1, head, early * edge_grads[stream]
        )
    block = 32
    for stream in range(3):
        for start in range(0, toks, block):
            total = None
            for tap in range(TAPS):
                term = (
                    tap_row(prm_ref, stream, tap)
                    * grads[stream, start + tap : start + tap + block, :]
                )
                total = term if total is None else total + term
            outs[1 + stream, start : start + block, :] = total

    single = jnp.where(chunk_of == 0, scale, 0.0)
    drives = jnp.concatenate(
        [amp[i] * after[i] * single for i in range(2)]
        + [amp[i] * adjoint[i] * single for i in range(2)]
        + [jnp.zeros((toks - 4 * 8, lanes), f32)],
        axis=0,
    )
    drives = lane_sums(drives, chunks).T[:OWNED, :]
    in_first = lax.broadcasted_iota(jnp.int32, (OWNED, toks), 1) < MODES
    forced = one_line(jnp.where(in_first, drives, 0.0), 0, OWNED, MODES)
    turned = pltpu.roll(drives, toks - MODES, 1)
    turned = one_line(jnp.where(in_first, turned, 0.0), 0, OWNED, MODES)
    driven[0:TAPS, :] = message1[OWNED : OWNED + TAPS, :] * forced
    driven[TAPS : 3 * TAPS, :] = message0[OWNED : OWNED + 2 * TAPS, :] * turned
    driven[3 * TAPS : 24, :] = jnp.zeros((24 - 3 * TAPS, toks), f32)
    short = [
        edge0[SHORT + 8 * i : SHORT + 8 * i + 8, :] + edge1[SHORT + 8 * i : SHORT + 8 * i + 8, :]
        for i in range(3)
    ]
    for stream in range(3):
        live_grad = edge_grads[stream] * live
        for tap in range(TAPS):
            index = stream * TAPS + tap
            term = live_grad * edges[stream, 8 - tap : 16 - tap, :]
            line = jnp.sum(term, axis=0, keepdims=True)
            short[index // 8] = short[index // 8] + jnp.where(row_id == index % 8, line, 0.0)
    r_all = []
    k_all = []
    for i in range(2):
        first_r, late_r = pair(edge0, RSUM)[i], pair(edge1, RSUM)[i]
        first_k, late_k = pair(edge0, KSUM)[i], pair(edge1, KSUM)[i]
        lag_early, lag_late = pair(edge0, DERIV)[i], pair(edge1, DERIV)[i]
        r_all.append(first_r + late_r + decay[i] * back[i] * after[i] + r_edge[i])
        k_all.append(
            first_k
            + late_k
            + decay[i] * lag_early * adjoint[i]
            + decay[i] * after[i] * (lag_late - back[i])
            + k_edge[i]
        )
    columns = jnp.concatenate(
        [value * single for value in short]
        + [root[i] * r_all[i] * single for i in range(2)]
        + [amp[i] * (0.5 * r_all[i] - rates[i] * k_all[i]) * single for i in range(2)],
        axis=0,
    )
    columns = lane_sums(columns, chunks)
    replies = lane_sums(driven[...], MODES)
    columns = jnp.concatenate(
        [columns[0:24, :] + replies, columns[24:56, :], jnp.zeros((128 - 56, 128), f32)], axis=0
    )
    totals = columns.T[:OWNED, :]
    modal_ref[...] = totals[:, 24:56]

    per_tile = toks // chunks
    for stream in range(4):
        for group in range(OWNED // per_tile):
            tile = outs[stream, :, group * toks : (group + 1) * toks].T
            for c in range(per_tile):
                out_rows[
                    pl.ds(stream * OWNED + group * per_tile + c, chunks, stride=ROWS_OUT), :
                ] = tile[c * chunks : (c + 1) * chunks]
    wide = jnp.concatenate([totals[:, 0:24], jnp.zeros((8, toks - 24), f32)], axis=1)
    for group in range(2):
        line = one_line(wide, 4 * group, 4, 32)
        upper = rounded(line)
        out_rows[pl.ds(32 + group, chunks, stride=ROWS_OUT), :] = jnp.broadcast_to(
            upper, (chunks, toks)
        )
        out_rows[pl.ds(34 + group, chunks, stride=ROWS_OUT), :] = jnp.broadcast_to(
            line - upper, (chunks, toks)
        )
    for spare in range(36, ROWS_OUT):
        out_rows[pl.ds(spare, chunks, stride=ROWS_OUT), :] = jnp.zeros((chunks, toks), f32)
    send_ref[...] = out_rows[...].reshape(send_ref.shape).astype(jnp.bfloat16)


def run_pack(query_in, key_in, value_in, grad_out):
    chans, toks = query_in.shape
    owners = chans // OWNED
    return pl.pallas_call(
        pack_kernel,
        in_specs=[pl.BlockSpec(memory_space=pltpu.HBM)] * 4,
        out_shape=jax.ShapeDtypeStruct((owners, ROWS_IN, toks), jnp.bfloat16),
        scratch_shapes=[
            pltpu.VMEM((4, chans, toks), jnp.bfloat16),
            pltpu.VMEM((4, chans, toks), jnp.float32),
            pltpu.VMEM((owners * ROWS_IN, toks), jnp.float32),
            pltpu.SemaphoreType.DMA((4,)),
        ],
        compiler_params=pltpu.CompilerParams(vmem_limit_bytes=VMEM_LIMIT),
    )(*[pltpu.with_memory_space_constraint(x, pltpu.HBM) for x in (query_in, key_in, value_in, grad_out)])


def modal_kernel(both_ref, after_ref, out_ref):
    out_ref[...] = both_ref[...]


def run_modal(both, after):
    vmem = pl.BlockSpec(memory_space=pltpu.VMEM)
    return pl.pallas_call(
        modal_kernel,
        in_specs=[vmem, pl.BlockSpec(memory_space=pltpu.HBM)],
        out_specs=vmem,
        out_shape=jax.ShapeDtypeStruct(both.shape, jnp.float32),
        cost_estimate=pl.CostEstimate(flops=2 * 10**10, bytes_accessed=1024, transcendentals=0),
    )(both, pltpu.with_memory_space_constraint(after, pltpu.HBM))


def run_first(half, recv, prm, log_rate):
    chunks, _, toks = recv.shape
    lanes = OWNED * chunks
    f32 = jnp.float32
    plane = jax.ShapeDtypeStruct((toks, lanes), f32)
    vmem = pl.BlockSpec(memory_space=pltpu.VMEM)
    return pl.pallas_call(
        first_kernel,
        in_specs=[pl.BlockSpec(memory_space=pltpu.SMEM), vmem, vmem, vmem],
        out_shape=(
            plane,
            jax.ShapeDtypeStruct((3, toks, lanes), f32),
            plane,
            plane,
            jax.ShapeDtypeStruct((MESSAGE, toks), f32),
        ),
        scratch_shapes=[
            pltpu.VMEM((chunks * ROWS_IN, toks), f32),
            pltpu.VMEM((4, PAD + toks, lanes), f32),
            pltpu.VMEM((toks, lanes), f32),
            pltpu.VMEM((toks, lanes), f32),
            pltpu.VMEM((3, toks, lanes), f32),
            pltpu.VMEM((2, 8 * toks, lanes // 2), f32),
            pltpu.VMEM((2, 8 * toks, lanes // 2), f32),
            pltpu.VMEM((16 * toks, lanes), f32),
            pltpu.VMEM((TAPS, toks, lanes), jnp.bfloat16),
            pltpu.VMEM((TAPS, toks, lanes), jnp.bfloat16),
            pltpu.VMEM((2, 8 * 24, lanes // 2), f32),
            pltpu.VMEM((COMPACT, lanes), f32),
        ],
        compiler_params=pltpu.CompilerParams(vmem_limit_bytes=VMEM_LIMIT),
    )(half, recv, prm, log_rate)


def run_second(half, own, other, prm, grad, hat, fwd, bwd):
    toks, lanes = grad.shape
    chunks = lanes // OWNED
    f32 = jnp.float32
    vmem = pl.BlockSpec(memory_space=pltpu.VMEM)
    return pl.pallas_call(
        second_kernel,
        in_specs=[pl.BlockSpec(memory_space=pltpu.SMEM)] + [vmem] * 7,
        out_shape=(
            jax.ShapeDtypeStruct((chunks, ROWS_OUT, toks), jnp.bfloat16),
            jax.ShapeDtypeStruct((OWNED, 2 * MODES), f32),
        ),
        scratch_shapes=[
            pltpu.VMEM((COMPACT, lanes), f32),
            pltpu.VMEM((COMPACT, lanes), f32),
            pltpu.VMEM((3, 16, lanes), f32),
            pltpu.VMEM((toks, lanes), f32),
            pltpu.VMEM((24, toks), f32),
            pltpu.VMEM((4, toks, lanes), f32),
            pltpu.VMEM((3, toks + PAD, lanes), f32),
            pltpu.VMEM((chunks * ROWS_OUT, toks), f32),
        ],
        compiler_params=pltpu.CompilerParams(vmem_limit_bytes=VMEM_LIMIT),
    )(half, own, other, prm, grad, hat, fwd, bwd)


def run_unpack(recv):
    owners, _, toks = recv.shape
    chans = OWNED * owners
    whole = jax.ShapeDtypeStruct((chans, toks), jnp.bfloat16)
    return pl.pallas_call(
        unpack_kernel,
        out_shape=(whole,) * 4 + (jax.ShapeDtypeStruct((3, TAPS, chans), jnp.float32),),
        scratch_shapes=[
            pltpu.VMEM((owners * ROWS_OUT, toks), jnp.float32),
            pltpu.VMEM((5, chans, toks), jnp.float32),
        ],
        compiler_params=pltpu.CompilerParams(vmem_limit_bytes=VMEM_LIMIT),
    )(recv)


def parameter_rows(weights, residue, log_rate, chunks):
    rows = jnp.concatenate(
        [
            weights.reshape(3 * TAPS, OWNED),
            jnp.zeros((3, OWNED), jnp.float32),
            log_rate.T,
            residue.T,
        ],
        axis=0,
    )
    return jnp.repeat(rows, chunks, axis=1)


def local(query_in, key_in, value_in, short_weight, residue, log_rate, grad_out):
    devices = lax.axis_size("seq")
    chunks = devices // 2
    chans = query_in.shape[0]
    me = lax.axis_index("seq")
    half = me // chunks
    index = me % chunks
    groups = [list(range(chunks)), list(range(chunks, devices))]
    across = [(i, (i + chunks) % devices) for i in range(devices)]

    send = run_pack(query_in, key_in, value_in, grad_out)
    mine = run_modal(jnp.concatenate([log_rate, residue], axis=1), send)
    theirs = lax.ppermute(mine, "seq", across)
    modal_params = jnp.where(
        half == 0, jnp.concatenate([mine, theirs]), jnp.concatenate([theirs, mine])
    )
    weights = jnp.concatenate(
        [
            lax.dynamic_slice(short_weight, (0, 0, 4 * index + at), (3, TAPS, 4))
            for at in (0, chans // 2)
        ],
        axis=2,
    )
    prm = parameter_rows(weights, modal_params[:, MODES:], modal_params[:, :MODES], chunks)
    which = half.reshape(1).astype(jnp.int32)

    recv = lax.all_to_all(send, "seq", 0, 0, tiled=True, axis_index_groups=groups)
    grad, hat, fwd, bwd, message = run_first(which, recv, prm, modal_params[:, :MODES])
    other = lax.ppermute(message, "seq", across)
    back, modal = run_second(which, message, other, prm, grad, hat, fwd, bwd)
    final = lax.all_to_all(back, "seq", 0, 0, tiled=True, axis_index_groups=groups)
    output, grad_query, grad_key, grad_value, grad_short = run_unpack(final)
    own_modal = lax.dynamic_slice(modal, (4 * half, 0), (4, 2 * MODES))
    return (
        output,
        grad_query,
        grad_key,
        grad_value,
        grad_short,
        own_modal[:, :MODES],
        own_modal[:, MODES:],
    )


def solution(mesh):
    return jax.shard_map(
        local,
        mesh=mesh,
        in_specs=(
            P("chan", "seq"),
            P("chan", "seq"),
            P("chan", "seq"),
            P(None, None, "chan"),
            P(("chan", "seq"), None),
            P(("chan", "seq"), None),
            P("chan", "seq"),
        ),
        out_specs=(
            P("chan", "seq"),
            P("chan", "seq"),
            P("chan", "seq"),
            P("chan", "seq"),
            P(None, None, "chan"),
            P(("chan", "seq"), None),
            P(("chan", "seq"), None),
        ),
        check_vma=False,
    )
```

```python
import math

import jax
import jax.numpy as jnp
from jax import lax
from jax.experimental import pallas as pl
from jax.experimental.pallas import tpu as pltpu
from jax.sharding import PartitionSpec as P

TAPS = 7
MODES = 16
PAD = 8
OWNED = 8
ROWS_IN = 4 * OWNED
ROWS_OUT = 40
VMEM_LIMIT = 16 * 1024 * 1024

STATE, DERIV, RSUM, KSUM, EDGE, SHORT, COMPACT = 0, 16, 32, 48, 64, 96, 128
MESSAGE = OWNED + 16


def first_row(chan, chans):
    return chan if chan < 4 else chans // 2 + chan - 4


def pack_kernel(query_ref, key_ref, value_ref, grad_ref, send_ref, held, wide, mixed_rows, sems):
    owners = send_ref.shape[0]
    chans = query_ref.shape[0]
    copies = [
        pltpu.make_async_copy(ref, held.at[stream], sems.at[stream])
        for stream, ref in enumerate((query_ref, key_ref, value_ref, grad_ref))
    ]
    for copy in copies:
        copy.start()
    for stream, copy in enumerate(copies):
        copy.wait()
        wide[stream] = held[stream].astype(jnp.float32)
        for chan in range(OWNED):
            mixed_rows[pl.ds(stream * OWNED + chan, owners, stride=ROWS_IN), :] = wide[
                stream, pl.ds(first_row(chan, chans), owners, stride=4), :
            ]
    send_ref[...] = mixed_rows[...].reshape(send_ref.shape).astype(jnp.bfloat16)


def unpack_kernel(recv_ref, out_ref, gq_ref, gk_ref, gv_ref, short_ref, rows, wide):
    owners = recv_ref.shape[0]
    chans = out_ref.shape[0]
    rows[...] = recv_ref[...].reshape(rows.shape).astype(jnp.float32)
    for stream, ref in enumerate((out_ref, gq_ref, gk_ref, gv_ref)):
        for chan in range(OWNED):
            wide[stream, pl.ds(first_row(chan, chans), owners, stride=4), :] = rows[
                pl.ds(stream * OWNED + chan, owners, stride=ROWS_OUT), :
            ]
        ref[...] = wide[stream].astype(jnp.bfloat16)
    for group in range(2):
        short = (
            rows[pl.ds(32 + group, owners, stride=ROWS_OUT), :]
            + rows[pl.ds(34 + group, owners, stride=ROWS_OUT), :]
        )
        for chan in range(4):
            wide[4, pl.ds(first_row(4 * group + chan, chans), owners, stride=4), :] = pltpu.roll(
                short, (128 - 32 * chan) % 128, 1
            )
    turned = wide[4].T
    for stream in range(3):
        short_ref[stream] = turned[stream * TAPS : (stream + 1) * TAPS, :]


def lane_ids(chunks, rows):
    lane = lax.broadcasted_iota(jnp.int32, (rows, OWNED * chunks), 1)
    return lane % chunks, lane // chunks


def owner_pick(chunks):
    owner = lane_ids(chunks, OWNED)[1]
    return (owner == lax.broadcasted_iota(jnp.int32, owner.shape, 0)).astype(jnp.float32)


def three_parts(value):
    upper = rounded(value)
    middle = rounded(value - upper)
    return [upper, middle, value - upper - middle]


def lane_sums(value, chunks):
    shape = (value.shape[1], 128)
    owner = lax.broadcasted_iota(jnp.int32, shape, 0) // chunks
    pick = (owner == lax.broadcasted_iota(jnp.int32, shape, 1)).astype(jnp.float32)
    pick = pick.astype(jnp.bfloat16)
    total = None
    for part in reversed(three_parts(value)):
        term = jnp.dot(part.astype(jnp.bfloat16), pick, preferred_element_type=jnp.float32)
        total = term if total is None else total + term
    return total


def lane_spread(value, chunks):
    pick = owner_pick(chunks)
    return lax.dot_general(
        jnp.concatenate(three_parts(value), axis=0).astype(jnp.bfloat16),
        jnp.concatenate([pick] * 3, axis=0).astype(jnp.bfloat16),
        (((0,), (0,)), ((), ())),
        preferred_element_type=jnp.float32,
    )


def one_line(value, first, count, width):
    line = value[first : first + 1, :]
    for chan in range(1, count):
        at = first + chan
        line = line + pltpu.roll(value, width * chan, 1)[at : at + 1, :]
    return line


def modal_rows(modal_ref):
    rates = [jnp.exp(modal_ref[8 * i : 8 * i + 8, :]) for i in range(2)]
    resid = [modal_ref[16 + 8 * i : 24 + 8 * i, :] for i in range(2)]
    decay = [jnp.exp(-r) for r in rates]
    root = [jnp.sqrt(2.0 * r) for r in rates]
    amp = [resid[i] * root[i] for i in range(2)]
    return rates, decay, root, amp


def keep(ref, tok, value):
    lanes = ref.shape[2]
    for half in range(2):
        ref[half, pl.ds(pl.multiple_of(8 * tok, 8), 8), :] = value[
            :, half * lanes : (half + 1) * lanes
        ]


def folded(ref, first, count):
    halves = []
    for half in range(2):
        total = None
        for sub in range(8):
            term = ref[half, pl.ds(first + sub, count, stride=8), :]
            total = term if total is None else total + term
        halves.append(total)
    return jnp.concatenate(halves, axis=1)


def tap_row(taps_ref, stream, tap):
    index = stream * TAPS + tap
    return taps_ref[index : index + 1, :]


def rounded(value):
    return value.astype(jnp.bfloat16).astype(jnp.float32)


def filter_kernel(
    half_ref,
    recv_ref,
    taps_ref,
    xt,
    hat_ref,
    mixed,
    gmixed,
    base,
    upper_w,
    lower_w,
    raw,
):
    chunks = recv_ref.shape[0]
    toks = recv_ref.shape[2]
    lanes = OWNED * chunks
    f32 = jnp.float32
    chunk_of, _ = lane_ids(chunks, 8)
    half = half_ref[0]
    late = half.astype(f32)
    block = 32

    raw[...] = recv_ref[...].reshape(raw.shape).astype(f32)
    per_tile = toks // chunks
    for stream in range(4):
        for group in range(OWNED // per_tile):
            tile = jnp.concatenate(
                [
                    raw[
                        pl.ds(stream * OWNED + group * per_tile + c, chunks, stride=ROWS_IN), :
                    ]
                    for c in range(per_tile)
                ],
                axis=0,
            )
            xt[stream, PAD : PAD + toks, group * toks : (group + 1) * toks] = tile.T
    for stream in range(3):
        tail = pltpu.roll(xt[stream, toks : toks + PAD, :], 1, 1)
        xt[stream, 0:PAD, :] = jnp.where(chunk_of >= 1, tail, 0.0)

    fringe = (lax.broadcasted_iota(jnp.int32, (8, lanes), 0) < TAPS - 1) & (chunk_of == 0)
    kept = 1.0 - jnp.where(fringe, late, 0.0)
    for start in range(0, toks, block):
        filtered = []
        for stream in range(3):
            total = None
            for tap in range(TAPS):
                lo = PAD - tap + start
                term = tap_row(taps_ref, stream, tap) * xt[stream, lo : lo + block, :]
                total = term if total is None else total + term
            filtered.append(total)
            hat_ref[stream, start : start + block, :] = total
        grad = xt[3, PAD + start : PAD + start + block, :]
        mixed[start : start + block, :] = rounded(filtered[1] * filtered[2])
        gmixed[start : start + block, :] = rounded(grad * filtered[0])
        base[0, start : start + block, :] = grad
        base[1, start : start + block, :] = filtered[2]
        base[2, start : start + block, :] = filtered[1]
    mixed[0:8, :] = mixed[0:8, :] * kept
    gmixed[0:8, :] = gmixed[0:8, :] * kept
    for stream in range(3):
        base[stream, 0:8, :] = base[stream, 0:8, :] * kept

    def weigh(slot, stream):
        for tap in range(TAPS):
            for start in range(0, toks, block):
                span = slice(start, start + block)
                lo = PAD - tap + start
                value = base[stream, span, :] * xt[stream, lo : lo + block, :]
                upper = value.astype(jnp.bfloat16)
                upper_w[slot + tap, span, :] = upper
                lower_w[slot + tap, span, :] = (value - upper.astype(f32)).astype(jnp.bfloat16)

    @pl.when(half == 0)
    def _():
        weigh(0, 1)
        weigh(TAPS, 2)

    @pl.when(half != 0)
    def _():
        weigh(0, 0)


def first_kernel(
    half_ref,
    modal_ref,
    rate_ref,
    xt,
    mixed,
    gmixed,
    base,
    upper_w,
    lower_w,
    fwd_ref,
    bwd_ref,
    msg_ref,
    part_y,
    part_z,
    states,
    sums,
    rows,
):
    toks, lanes = mixed.shape
    chunks = lanes // OWNED
    f32 = jnp.float32
    chunk_of, _ = lane_ids(chunks, 8)
    half = half_ref[0]
    late = half.astype(f32)
    early = 1.0 - late
    zero = jnp.zeros((8, lanes), f32)
    block = 32

    rates, decay, _, amp = modal_rows(modal_ref)

    def row_of(ref, tok):
        return jnp.broadcast_to(ref[pl.ds(tok, 1), :], (8, lanes))

    def local_body(tok, carry):
        e0, e1, f0, f1 = carry
        xb = row_of(mixed, tok)
        gb = row_of(gmixed, toks - 1 - tok)
        return (
            decay[0] * e0 + xb,
            decay[1] * e1 + xb,
            decay[0] * f0 + gb,
            decay[1] * f1 + gb,
        )

    e0, e1, f0, f1 = lax.fori_loop(0, toks, local_body, (zero,) * 4, unroll=16)
    ends = [e0, e1]
    heads = [f0, f1]
    step = 1
    while step < chunks:
        for i in range(2):
            power = jnp.exp(rates[i] * (-1.0 * toks * step))
            moved = jnp.where(chunk_of >= step, pltpu.roll(ends[i], step, 1), 0.0)
            ends[i] = ends[i] + power * moved
            moved = jnp.where(chunk_of < chunks - step, pltpu.roll(heads[i], lanes - step, 1), 0.0)
            heads[i] = heads[i] + power * moved
        step *= 2
    start_h = [jnp.where(chunk_of >= 1, pltpu.roll(e, 1, 1), 0.0) for e in ends]
    start_p = [jnp.where(chunk_of < chunks - 1, pltpu.roll(f, lanes - 1, 1), 0.0) for f in heads]

    def forward_body(tok, carry):
        h0, h1, r0, r1, d0, d1 = carry
        xb = row_of(mixed, tok)
        gb = row_of(gmixed, tok)
        h0 = decay[0] * h0 + xb
        h1 = decay[1] * h1 + xb
        keep(part_y, tok, amp[0] * h0 + amp[1] * h1)
        states[pl.ds(pl.multiple_of(16 * tok, 8), 8), :] = h0
        states[pl.ds(pl.multiple_of(16 * tok + 8, 8), 8), :] = h1
        return (
            h0,
            h1,
            r0 + gb * h0,
            r1 + gb * h1,
            decay[0] * d0 + h0,
            decay[1] * d1 + h1,
        )

    _, _, r0, r1, d0, d1 = lax.fori_loop(
        0, toks, forward_body, (start_h[0], start_h[1]) + (zero,) * 4, unroll=16
    )

    def backward_body(step_index, carry):
        p0, p1, k0, k1, c0, c1 = carry
        tok = toks - 1 - step_index
        gb = row_of(gmixed, tok)
        q0 = decay[0] * p0
        q1 = decay[1] * p1
        k0 = k0 + states[pl.ds(pl.multiple_of(16 * tok, 8), 8), :] * q0
        k1 = k1 + states[pl.ds(pl.multiple_of(16 * tok + 8, 8), 8), :] * q1
        p0 = q0 + gb
        p1 = q1 + gb
        keep(part_z, tok, amp[0] * p0 + amp[1] * p1)
        return (p0, p1, k0, k1, decay[0] * c0 + p0, decay[1] * c1 + p1)

    _, _, k0, k1, c0, c1 = lax.fori_loop(
        0, toks, backward_body, (start_p[0], start_p[1]) + (zero,) * 4, unroll=16
    )

    for start in range(0, toks, block):
        fwd_ref[start : start + block, :] = folded(part_y, 8 * start, block)
        bwd_ref[start : start + block, :] = folded(part_z, 8 * start, block)

    for stream in range(3):
        tap_sums = [zero for _ in range(TAPS)]
        for start in range(0, toks, block):
            conv = (fwd_ref if stream == 0 else bwd_ref)[start : start + block, :]
            own = conv * base[stream, start : start + block, :]
            for tap in range(TAPS):
                lo = PAD - tap + start
                prod = own * xt[stream, lo : lo + block, :]
                for sub in range(0, block, 8):
                    tap_sums[tap] = tap_sums[tap] + prod[sub : sub + 8, :]
        for tap in range(TAPS):
            keep(sums, stream * TAPS + tap, tap_sums[tap])
    for index in range(3 * TAPS, 24):
        keep(sums, index, zero)
    rows[SHORT : SHORT + 24, :] = folded(sums, 0, 24)
    rows[SHORT + 24 : COMPACT, :] = zero

    bf16 = jnp.bfloat16
    rate_line = jnp.exp(rate_ref[...])
    rate_line = jnp.concatenate([rate_line, jnp.zeros((OWNED, toks - MODES), f32)], axis=1)
    rate_line = one_line(rate_line, 0, OWNED, MODES)
    row_lane = lax.broadcasted_iota(jnp.int32, (lanes, toks), 0)
    col_owner = lax.broadcasted_iota(jnp.int32, (lanes, toks), 1) // MODES
    row_chunk = (row_lane % chunks).astype(f32)
    spread = late * (toks * row_chunk - (TAPS - 2.0)) + early * (
        toks * (chunks - 1.0 - row_chunk) + 1.0
    )
    across = jnp.where(row_lane // chunks == col_owner, jnp.exp(-rate_line * spread), 0.0)
    across_hi = across.astype(bf16)
    across_lo = (across - across_hi.astype(f32)).astype(bf16)
    row_tok = lax.broadcasted_iota(jnp.int32, (toks, toks), 0).astype(f32)
    along = jnp.exp(-rate_line * (late * row_tok + early * (toks - 1.0 - row_tok)))

    def respond(slot):
        for tap in range(slot, slot + TAPS):
            total = (
                jnp.dot(upper_w[tap], across_lo, preferred_element_type=f32)
                + jnp.dot(lower_w[tap], across_hi, preferred_element_type=f32)
                + jnp.dot(upper_w[tap], across_hi, preferred_element_type=f32)
            )
            at = OWNED + tap
            msg_ref[at : at + 1, :] = jnp.sum(total * along, axis=0, keepdims=True)

    span_c = chunk_of.astype(f32)
    msg_ref[OWNED:MESSAGE, :] = jnp.zeros((MESSAGE - OWNED, toks), f32)

    @pl.when(half == 0)
    def _():
        respond(0)
        respond(TAPS)
        for stream in range(4):
            lo = EDGE + 8 * stream
            rows[lo : lo + 8, :] = jnp.where(
                chunk_of == chunks - 1, xt[stream, toks : toks + PAD, :], 0.0
            )
        for i in range(2):
            weight = jnp.exp(-rates[i] * (toks * (chunks - 1.0 - span_c)))
            rows[STATE + 8 * i : STATE + 8 * i + 8, :] = jnp.where(
                chunk_of == chunks - 1, ends[i], 0.0
            )
            rows[DERIV + 8 * i : DERIV + 8 * i + 8, :] = (d0, d1)[i] * weight

    @pl.when(half != 0)
    def _():
        respond(0)
        for stream in range(4):
            lo = EDGE + 8 * stream
            rows[lo : lo + 8, :] = jnp.where(chunk_of == 0, xt[stream, PAD : 2 * PAD, :], 0.0)
        for i in range(2):
            grow = jnp.exp(rates[i] * (TAPS - 1.0))
            weight = jnp.exp(-rates[i] * (toks * span_c))
            first = jnp.where(chunk_of == 0, heads[i], 0.0)
            rows[STATE + 8 * i : STATE + 8 * i + 8, :] = first * grow
            rows[DERIV + 8 * i : DERIV + 8 * i + 8, :] = (
                (c0, c1)[i] * weight - (TAPS - 1.0) * first
            ) * grow

    for i in range(2):
        rows[RSUM + 8 * i : RSUM + 8 * i + 8, :] = (r0, r1)[i]
        rows[KSUM + 8 * i : KSUM + 8 * i + 8, :] = (k0, k1)[i]
    msg_ref[0:OWNED, :] = lane_sums(rows[...], chunks).T[:OWNED, :]


def second_kernel(
    half_ref,
    own_ref,
    other_ref,
    taps_ref,
    modal_ref,
    xt,
    hat_ref,
    fwd_ref,
    bwd_ref,
    send_ref,
    sums_ref,
    edge0,
    edge1,
    edges,
    part,
    driven,
    outs,
    grads,
    out_rows,
):
    toks, lanes = fwd_ref.shape
    chunks = lanes // OWNED
    f32 = jnp.float32
    chunk_of, _ = lane_ids(chunks, 8)
    scale = 1.0 / math.sqrt(2 * chunks * toks)
    half = half_ref[0]
    late = half.astype(f32)
    early = 1.0 - late
    rates, decay, root, amp = modal_rows(modal_ref)
    fringe = TAPS - 1
    zero = jnp.zeros((8, lanes), f32)

    own = own_ref[...]
    other = other_ref[...]
    message0 = own * early + other * late
    message1 = own * late + other * early
    edge0[...] = lane_spread(message0[0:OWNED, :], chunks)
    edge1[...] = lane_spread(message1[0:OWNED, :], chunks)

    def pair(ref, first):
        return [ref[first + 8 * i : first + 8 * i + 8, :] for i in range(2)]

    row_id = lax.broadcasted_iota(jnp.int32, (8, lanes), 0)
    live = jnp.where(row_id < fringe, 1.0, 0.0)
    hats = []
    for stream in range(3):
        edges[stream, 0:8, :] = edge0[EDGE + 8 * stream : EDGE + 8 * stream + 8, :]
        edges[stream, 8:16, :] = edge1[EDGE + 8 * stream : EDGE + 8 * stream + 8, :]
        total = None
        for tap in range(TAPS):
            term = tap_row(taps_ref, stream, tap) * edges[stream, 8 - tap : 16 - tap, :]
            total = term if total is None else total + term
        hats.append(total)
    grad_edge = edge1[EDGE + 24 : EDGE + 32, :]
    x_edge = rounded(hats[1] * hats[2])
    g_edge = rounded(grad_edge * hats[0])

    state = pair(edge0, STATE)
    passed = []
    y_edge = zero
    for tok in range(fringe):
        xb = jnp.broadcast_to(x_edge[tok : tok + 1, :], (8, lanes))
        state = [decay[i] * state[i] + xb for i in range(2)]
        passed.append(state)
        line = jnp.sum(amp[0] * state[0] + amp[1] * state[1], axis=0, keepdims=True)
        y_edge = jnp.where(row_id == tok, line, y_edge)
    after = state
    back = pair(edge1, STATE)
    r_edge = [zero, zero]
    k_edge = [zero, zero]
    z_edge = zero
    adjoint = back
    for tok in range(fringe - 1, -1, -1):
        gb = jnp.broadcast_to(g_edge[tok : tok + 1, :], (8, lanes))
        moved = [decay[i] * adjoint[i] for i in range(2)]
        k_edge = [k_edge[i] + passed[tok][i] * moved[i] for i in range(2)]
        r_edge = [r_edge[i] + gb * passed[tok][i] for i in range(2)]
        adjoint = [moved[i] + gb for i in range(2)]
        line = jnp.sum(amp[0] * adjoint[0] + amp[1] * adjoint[1], axis=0, keepdims=True)
        z_edge = jnp.where(row_id == tok, line, z_edge)

    span_c = chunk_of.astype(f32)
    carry = []
    for i in range(2):
        into_late = after[i] * jnp.exp(-rates[i] * (toks * span_c - (fringe - 1.0)))
        into_early = adjoint[i] * jnp.exp(-rates[i] * (toks * (chunks - 1.0 - span_c) + 1.0))
        carry.append(amp[i] * (early * into_early + late * into_late))

    sub = row_id.astype(f32)[:, :128]
    sub = late * sub + early * (7.0 - sub)
    stride8 = [jnp.exp(-8.0 * r) for r in rates]
    blocks = toks // 8
    for cut in range(lanes // 128):
        cols = slice(cut * 128, (cut + 1) * 128)
        modes = []
        factors = []
        for i in range(2):
            for m in range(8):
                rate = jnp.broadcast_to(rates[i][m : m + 1, cols], (8, 128))
                lead = jnp.broadcast_to(carry[i][m : m + 1, cols], (8, 128))
                modes.append(lead * jnp.exp(-rate * sub))
                factors.append(jnp.broadcast_to(stride8[i][m : m + 1, cols], (8, 128)))

        def reply_body(step_index, values, cols=cols, factors=factors):
            at = half * step_index + (1 - half) * (blocks - 1 - step_index)
            total = list(values)
            while len(total) > 1:
                total = [total[k] + total[k + 1] for k in range(0, len(total), 2)]
            part[pl.ds(pl.multiple_of(8 * at, 8), 8), cols] = total[0]
            return tuple(v * f for v, f in zip(values, factors))

        lax.fori_loop(0, blocks, reply_body, tuple(modes), unroll=4)

    patch = (row_id < fringe) & (chunk_of == 0) & (jnp.broadcast_to(late, (8, lanes)) > 0.5)
    y_edge = rounded(y_edge)
    z_edge = rounded(z_edge)
    for start, count in ((0, 8), (8, 24), (32, 32), (64, 32), (96, 32)):
        span = slice(start, start + count)
        reply = part[span, :]
        conv = rounded(fwd_ref[span, :] + late * reply)
        turn = rounded(bwd_ref[span, :] + early * reply)
        hat = [hat_ref[stream, span, :] for stream in range(3)]
        if start == 0:
            conv = jnp.where(patch, y_edge, conv)
            turn = jnp.where(patch, z_edge, turn)
            hat = [jnp.where(patch, hats[stream], hat[stream]) for stream in range(3)]
        grads[0, span, :] = xt[3, PAD + start : PAD + start + count, :] * conv
        grads[1, span, :] = turn * hat[2]
        grads[2, span, :] = turn * hat[1]
        outs[0, span, :] = hat[0] * conv
    edge_grads = (grad_edge * y_edge, z_edge * hats[2], z_edge * hats[1])
    for stream in range(3):
        head = pltpu.roll(grads[stream, 0:PAD, :], lanes - 1, 1)
        grads[stream, toks : toks + PAD, :] = jnp.where(
            chunk_of < chunks - 1, head, early * edge_grads[stream]
        )
    block = 32
    for stream in range(3):
        for start in range(0, toks, block):
            total = None
            for tap in range(TAPS):
                term = (
                    tap_row(taps_ref, stream, tap)
                    * grads[stream, start + tap : start + tap + block, :]
                )
                total = term if total is None else total + term
            outs[1 + stream, start : start + block, :] = total

    single = jnp.where(chunk_of == 0, scale, 0.0)
    drives = jnp.concatenate(
        [amp[i] * after[i] * single for i in range(2)]
        + [amp[i] * adjoint[i] * single for i in range(2)]
        + [jnp.zeros((toks - 4 * 8, lanes), f32)],
        axis=0,
    )
    drives = lane_sums(drives, chunks).T[:OWNED, :]
    in_first = lax.broadcasted_iota(jnp.int32, (OWNED, toks), 1) < MODES
    forced = one_line(jnp.where(in_first, drives, 0.0), 0, OWNED, MODES)
    turned = pltpu.roll(drives, toks - MODES, 1)
    turned = one_line(jnp.where(in_first, turned, 0.0), 0, OWNED, MODES)
    driven[0:TAPS, :] = message1[OWNED : OWNED + TAPS, :] * forced
    driven[TAPS : 3 * TAPS, :] = message0[OWNED : OWNED + 2 * TAPS, :] * turned
    driven[3 * TAPS : 24, :] = jnp.zeros((24 - 3 * TAPS, toks), f32)
    short = [
        edge0[SHORT + 8 * i : SHORT + 8 * i + 8, :] + edge1[SHORT + 8 * i : SHORT + 8 * i + 8, :]
        for i in range(3)
    ]
    for stream in range(3):
        live_grad = edge_grads[stream] * live
        for tap in range(TAPS):
            index = stream * TAPS + tap
            term = live_grad * edges[stream, 8 - tap : 16 - tap, :]
            line = jnp.sum(term, axis=0, keepdims=True)
            short[index // 8] = short[index // 8] + jnp.where(row_id == index % 8, line, 0.0)
    r_all = []
    k_all = []
    for i in range(2):
        first_r, late_r = pair(edge0, RSUM)[i], pair(edge1, RSUM)[i]
        first_k, late_k = pair(edge0, KSUM)[i], pair(edge1, KSUM)[i]
        lag_early, lag_late = pair(edge0, DERIV)[i], pair(edge1, DERIV)[i]
        r_all.append(first_r + late_r + decay[i] * back[i] * after[i] + r_edge[i])
        k_all.append(
            first_k
            + late_k
            + decay[i] * lag_early * adjoint[i]
            + decay[i] * after[i] * (lag_late - back[i])
            + k_edge[i]
        )
    columns = jnp.concatenate(
        [value * single for value in short]
        + [root[i] * r_all[i] * single for i in range(2)]
        + [amp[i] * (0.5 * r_all[i] - rates[i] * k_all[i]) * single for i in range(2)],
        axis=0,
    )
    columns = lane_sums(columns, chunks)
    replies = lane_sums(driven[...], MODES)
    columns = jnp.concatenate(
        [columns[0:24, :] + replies, columns[24:56, :], jnp.zeros((128 - 56, 128), f32)], axis=0
    )
    totals = columns.T[:OWNED, :]
    sums_ref[...] = totals[:, 24:56]

    per_tile = toks // chunks
    for stream in range(4):
        for group in range(OWNED // per_tile):
            tile = outs[stream, :, group * toks : (group + 1) * toks].T
            for c in range(per_tile):
                out_rows[
                    pl.ds(stream * OWNED + group * per_tile + c, chunks, stride=ROWS_OUT), :
                ] = tile[c * chunks : (c + 1) * chunks]
    wide = jnp.concatenate([totals[:, 0:24], jnp.zeros((8, toks - 24), f32)], axis=1)
    for group in range(2):
        line = one_line(wide, 4 * group, 4, 32)
        upper = rounded(line)
        out_rows[pl.ds(32 + group, chunks, stride=ROWS_OUT), :] = jnp.broadcast_to(
            upper, (chunks, toks)
        )
        out_rows[pl.ds(34 + group, chunks, stride=ROWS_OUT), :] = jnp.broadcast_to(
            line - upper, (chunks, toks)
        )
    for spare in range(36, ROWS_OUT):
        out_rows[pl.ds(spare, chunks, stride=ROWS_OUT), :] = jnp.zeros((chunks, toks), f32)
    send_ref[...] = out_rows[...].reshape(send_ref.shape).astype(jnp.bfloat16)


def run_pack(query_in, key_in, value_in, grad_out):
    chans, toks = query_in.shape
    owners = chans // OWNED
    return pl.pallas_call(
        pack_kernel,
        in_specs=[pl.BlockSpec(memory_space=pltpu.HBM)] * 4,
        out_shape=jax.ShapeDtypeStruct((owners, ROWS_IN, toks), jnp.bfloat16),
        scratch_shapes=[
            pltpu.VMEM((4, chans, toks), jnp.bfloat16),
            pltpu.VMEM((4, chans, toks), jnp.float32),
            pltpu.VMEM((owners * ROWS_IN, toks), jnp.float32),
            pltpu.SemaphoreType.DMA((4,)),
        ],
        compiler_params=pltpu.CompilerParams(vmem_limit_bytes=VMEM_LIMIT),
    )(*[pltpu.with_memory_space_constraint(x, pltpu.HBM) for x in (query_in, key_in, value_in, grad_out)])


def modal_kernel(both_ref, after_ref, out_ref):
    out_ref[...] = both_ref[...]


def run_modal(both, after):
    vmem = pl.BlockSpec(memory_space=pltpu.VMEM)
    return pl.pallas_call(
        modal_kernel,
        in_specs=[vmem, pl.BlockSpec(memory_space=pltpu.HBM)],
        out_specs=vmem,
        out_shape=jax.ShapeDtypeStruct(both.shape, jnp.float32),
        cost_estimate=pl.CostEstimate(flops=2 * 10**10, bytes_accessed=1024, transcendentals=0),
        compiler_params=pltpu.CompilerParams(vmem_limit_bytes=1024 * 1024),
    )(both, pltpu.with_memory_space_constraint(after, pltpu.HBM))


def plane(*shape, dtype=jnp.float32):
    return jax.ShapeDtypeStruct(shape, dtype)


def run_filter(half, recv, taps):
    chunks, _, toks = recv.shape
    lanes = OWNED * chunks
    vmem = pl.BlockSpec(memory_space=pltpu.VMEM)
    return pl.pallas_call(
        filter_kernel,
        in_specs=[pl.BlockSpec(memory_space=pltpu.SMEM), vmem, vmem],
        out_shape=(
            plane(4, PAD + toks, lanes),
            plane(3, toks, lanes),
            plane(toks, lanes),
            plane(toks, lanes),
            plane(3, toks, lanes),
            plane(2 * TAPS, toks, lanes, dtype=jnp.bfloat16),
            plane(2 * TAPS, toks, lanes, dtype=jnp.bfloat16),
        ),
        scratch_shapes=[pltpu.VMEM((chunks * ROWS_IN, toks), jnp.float32)],
        cost_estimate=pl.CostEstimate(flops=2 * 10**10, bytes_accessed=1024, transcendentals=0),
        compiler_params=pltpu.CompilerParams(vmem_limit_bytes=VMEM_LIMIT),
    )(half, recv, taps)


def run_first(half, modal, log_rate, xt, mixed, gmixed, base, upper_w, lower_w):
    toks, lanes = mixed.shape
    f32 = jnp.float32
    vmem = pl.BlockSpec(memory_space=pltpu.VMEM)
    return pl.pallas_call(
        first_kernel,
        in_specs=[pl.BlockSpec(memory_space=pltpu.SMEM)] + [vmem] * 8,
        out_shape=(plane(toks, lanes), plane(toks, lanes), plane(MESSAGE, toks)),
        scratch_shapes=[
            pltpu.VMEM((2, 8 * toks, lanes // 2), f32),
            pltpu.VMEM((2, 8 * toks, lanes // 2), f32),
            pltpu.VMEM((16 * toks, lanes), f32),
            pltpu.VMEM((2, 8 * 24, lanes // 2), f32),
            pltpu.VMEM((COMPACT, lanes), f32),
        ],
        compiler_params=pltpu.CompilerParams(vmem_limit_bytes=VMEM_LIMIT),
    )(half, modal, log_rate, xt, mixed, gmixed, base, upper_w, lower_w)


def run_second(half, own, other, taps, modal, xt, hat, fwd, bwd):
    toks, lanes = fwd.shape
    chunks = lanes // OWNED
    f32 = jnp.float32
    vmem = pl.BlockSpec(memory_space=pltpu.VMEM)
    return pl.pallas_call(
        second_kernel,
        in_specs=[pl.BlockSpec(memory_space=pltpu.SMEM)] + [vmem] * 8,
        out_shape=(
            plane(chunks, ROWS_OUT, toks, dtype=jnp.bfloat16),
            plane(OWNED, 2 * MODES),
        ),
        scratch_shapes=[
            pltpu.VMEM((COMPACT, lanes), f32),
            pltpu.VMEM((COMPACT, lanes), f32),
            pltpu.VMEM((3, 16, lanes), f32),
            pltpu.VMEM((toks, lanes), f32),
            pltpu.VMEM((24, toks), f32),
            pltpu.VMEM((4, toks, lanes), f32),
            pltpu.VMEM((3, toks + PAD, lanes), f32),
            pltpu.VMEM((chunks * ROWS_OUT, toks), f32),
        ],
        compiler_params=pltpu.CompilerParams(vmem_limit_bytes=VMEM_LIMIT),
    )(half, own, other, taps, modal, xt, hat, fwd, bwd)


def run_unpack(recv):
    owners, _, toks = recv.shape
    chans = OWNED * owners
    whole = jax.ShapeDtypeStruct((chans, toks), jnp.bfloat16)
    return pl.pallas_call(
        unpack_kernel,
        out_shape=(whole,) * 4 + (jax.ShapeDtypeStruct((3, TAPS, chans), jnp.float32),),
        scratch_shapes=[
            pltpu.VMEM((owners * ROWS_OUT, toks), jnp.float32),
            pltpu.VMEM((5, chans, toks), jnp.float32),
        ],
        compiler_params=pltpu.CompilerParams(vmem_limit_bytes=VMEM_LIMIT),
    )(recv)


def tap_rows(weights, chunks):
    rows = jnp.concatenate(
        [weights.reshape(3 * TAPS, OWNED), jnp.zeros((3, OWNED), jnp.float32)], axis=0
    )
    return jnp.repeat(rows, chunks, axis=1)


def local(query_in, key_in, value_in, short_weight, residue, log_rate, grad_out):
    devices = lax.axis_size("seq")
    chunks = devices // 2
    chans = query_in.shape[0]
    me = lax.axis_index("seq")
    half = me // chunks
    index = me % chunks
    groups = [list(range(chunks)), list(range(chunks, devices))]
    across = [(i, (i + chunks) % devices) for i in range(devices)]

    send = run_pack(query_in, key_in, value_in, grad_out)
    mine = run_modal(jnp.concatenate([log_rate, residue], axis=1), send)
    theirs = lax.ppermute(mine, "seq", across)
    weights = jnp.concatenate(
        [
            lax.dynamic_slice(short_weight, (0, 0, 4 * index + at), (3, TAPS, 4))
            for at in (0, chans // 2)
        ],
        axis=2,
    )
    taps = tap_rows(weights, chunks)
    which = half.reshape(1).astype(jnp.int32)

    recv = lax.all_to_all(send, "seq", 0, 0, tiled=True, axis_index_groups=groups)
    xt, hat, *inner = run_filter(which, recv, taps)
    theirs, inner = lax.optimization_barrier((theirs, inner))
    modal_params = jnp.where(
        half == 0, jnp.concatenate([mine, theirs]), jnp.concatenate([theirs, mine])
    )
    modal = jnp.repeat(modal_params.T, chunks, axis=1)
    fwd, bwd, message = run_first(which, modal, modal_params[:, :MODES], xt, *inner)
    other = lax.ppermute(message, "seq", across)
    back, sums = run_second(which, message, other, taps, modal, xt, hat, fwd, bwd)
    final = lax.all_to_all(back, "seq", 0, 0, tiled=True, axis_index_groups=groups)
    output, grad_query, grad_key, grad_value, grad_short = run_unpack(final)
    own_modal = lax.dynamic_slice(sums, (4 * half, 0), (4, 2 * MODES))
    return (
        output,
        grad_query,
        grad_key,
        grad_value,
        grad_short,
        own_modal[:, :MODES],
        own_modal[:, MODES:],
    )


def solution(mesh):
    return jax.shard_map(
        local,
        mesh=mesh,
        in_specs=(
            P("chan", "seq"),
            P("chan", "seq"),
            P("chan", "seq"),
            P(None, None, "chan"),
            P(("chan", "seq"), None),
            P(("chan", "seq"), None),
            P("chan", "seq"),
        ),
        out_specs=(
            P("chan", "seq"),
            P("chan", "seq"),
            P("chan", "seq"),
            P("chan", "seq"),
            P(None, None, "chan"),
            P(("chan", "seq"), None),
            P(("chan", "seq"), None),
        ),
        check_vma=False,
    )
```

```python
import math

import jax
import jax.numpy as jnp
from jax import lax
from jax.experimental import pallas as pl
from jax.experimental.pallas import tpu as pltpu
from jax.sharding import PartitionSpec as P

TAPS = 7
MODES = 16
PAD = 8
OWNED = 8
ROWS_IN = 4 * OWNED
ROWS_OUT = 40
VMEM_LIMIT = 16 * 1024 * 1024

STATE, DERIV, RSUM, KSUM, EDGE, SHORT, COMPACT = 0, 16, 32, 48, 64, 96, 128
MESSAGE = OWNED + 16


def first_row(chan, chans):
    return chan if chan < 4 else chans // 2 + chan - 4


def pack_kernel(query_ref, key_ref, value_ref, grad_ref, send_ref, held, wide, mixed_rows, sems):
    owners = send_ref.shape[0]
    chans = query_ref.shape[0]
    copies = [
        pltpu.make_async_copy(ref, held.at[stream], sems.at[stream])
        for stream, ref in enumerate((query_ref, key_ref, value_ref, grad_ref))
    ]
    for copy in copies:
        copy.start()
    for stream, copy in enumerate(copies):
        copy.wait()
        wide[stream] = held[stream].astype(jnp.float32)
        for chan in range(OWNED):
            mixed_rows[pl.ds(stream * OWNED + chan, owners, stride=ROWS_IN), :] = wide[
                stream, pl.ds(first_row(chan, chans), owners, stride=4), :
            ]
    send_ref[...] = mixed_rows[...].reshape(send_ref.shape).astype(jnp.bfloat16)


def unpack_kernel(recv_ref, out_ref, gq_ref, gk_ref, gv_ref, short_ref, rows, wide):
    owners = recv_ref.shape[0]
    chans = out_ref.shape[0]
    rows[...] = recv_ref[...].reshape(rows.shape).astype(jnp.float32)
    for stream, ref in enumerate((out_ref, gq_ref, gk_ref, gv_ref)):
        for chan in range(OWNED):
            wide[stream, pl.ds(first_row(chan, chans), owners, stride=4), :] = rows[
                pl.ds(stream * OWNED + chan, owners, stride=ROWS_OUT), :
            ]
        ref[...] = wide[stream].astype(jnp.bfloat16)
    for group in range(2):
        short = (
            rows[pl.ds(32 + group, owners, stride=ROWS_OUT), :]
            + rows[pl.ds(34 + group, owners, stride=ROWS_OUT), :]
        )
        for chan in range(4):
            wide[4, pl.ds(first_row(4 * group + chan, chans), owners, stride=4), :] = pltpu.roll(
                short, (128 - 32 * chan) % 128, 1
            )
    turned = wide[4].T
    for stream in range(3):
        short_ref[stream] = turned[stream * TAPS : (stream + 1) * TAPS, :]


def lane_ids(chunks, rows):
    lane = lax.broadcasted_iota(jnp.int32, (rows, OWNED * chunks), 1)
    return lane % chunks, lane // chunks


def owner_pick(chunks):
    owner = lane_ids(chunks, OWNED)[1]
    return (owner == lax.broadcasted_iota(jnp.int32, owner.shape, 0)).astype(jnp.float32)


def three_parts(value):
    upper = rounded(value)
    middle = rounded(value - upper)
    return [upper, middle, value - upper - middle]


def lane_sums(value, chunks):
    shape = (value.shape[1], 128)
    owner = lax.broadcasted_iota(jnp.int32, shape, 0) // chunks
    pick = (owner == lax.broadcasted_iota(jnp.int32, shape, 1)).astype(jnp.float32)
    pick = pick.astype(jnp.bfloat16)
    total = None
    for part in reversed(three_parts(value)):
        term = jnp.dot(part.astype(jnp.bfloat16), pick, preferred_element_type=jnp.float32)
        total = term if total is None else total + term
    return total


def lane_spread(value, chunks):
    pick = owner_pick(chunks)
    return lax.dot_general(
        jnp.concatenate(three_parts(value), axis=0).astype(jnp.bfloat16),
        jnp.concatenate([pick] * 3, axis=0).astype(jnp.bfloat16),
        (((0,), (0,)), ((), ())),
        preferred_element_type=jnp.float32,
    )


def one_line(value, first, count, width):
    line = value[first : first + 1, :]
    for chan in range(1, count):
        at = first + chan
        line = line + pltpu.roll(value, width * chan, 1)[at : at + 1, :]
    return line


def modal_rows(modal_ref):
    rates = [jnp.exp(modal_ref[8 * i : 8 * i + 8, :]) for i in range(2)]
    resid = [modal_ref[16 + 8 * i : 24 + 8 * i, :] for i in range(2)]
    decay = [jnp.exp(-r) for r in rates]
    root = [jnp.sqrt(2.0 * r) for r in rates]
    amp = [resid[i] * root[i] for i in range(2)]
    return rates, decay, root, amp


def keep(ref, tok, value):
    lanes = ref.shape[2]
    for half in range(2):
        ref[half, pl.ds(pl.multiple_of(8 * tok, 8), 8), :] = value[
            :, half * lanes : (half + 1) * lanes
        ]


def folded(ref, first, count):
    halves = []
    for half in range(2):
        total = None
        for sub in range(8):
            term = ref[half, pl.ds(first + sub, count, stride=8), :]
            total = term if total is None else total + term
        halves.append(total)
    return jnp.concatenate(halves, axis=1)


def tap_row(taps_ref, stream, tap):
    index = stream * TAPS + tap
    return taps_ref[index : index + 1, :]


def rounded(value):
    return value.astype(jnp.bfloat16).astype(jnp.float32)


def filter_kernel(
    half_ref,
    recv_ref,
    taps_ref,
    xt,
    hat_ref,
    base,
    raw,
):
    mixed, gmixed = base.at[3], base.at[4]
    chunks = recv_ref.shape[0]
    toks = recv_ref.shape[2]
    lanes = OWNED * chunks
    f32 = jnp.float32
    chunk_of, _ = lane_ids(chunks, 8)
    half = half_ref[0]
    late = half.astype(f32)
    block = 32

    raw[...] = recv_ref[...].reshape(raw.shape).astype(f32)
    per_tile = toks // chunks
    for stream in range(4):
        for group in range(OWNED // per_tile):
            tile = jnp.concatenate(
                [
                    raw[
                        pl.ds(stream * OWNED + group * per_tile + c, chunks, stride=ROWS_IN), :
                    ]
                    for c in range(per_tile)
                ],
                axis=0,
            )
            xt[stream, PAD : PAD + toks, group * toks : (group + 1) * toks] = tile.T
    for stream in range(3):
        tail = pltpu.roll(xt[stream, toks : toks + PAD, :], 1, 1)
        xt[stream, 0:PAD, :] = jnp.where(chunk_of >= 1, tail, 0.0)

    fringe = (lax.broadcasted_iota(jnp.int32, (8, lanes), 0) < TAPS - 1) & (chunk_of == 0)
    kept = 1.0 - jnp.where(fringe, late, 0.0)
    for start in range(0, toks, block):
        filtered = []
        for stream in range(3):
            total = None
            for tap in range(TAPS):
                lo = PAD - tap + start
                term = tap_row(taps_ref, stream, tap) * xt[stream, lo : lo + block, :]
                total = term if total is None else total + term
            filtered.append(total)
            hat_ref[stream, start : start + block, :] = total
        grad = xt[3, PAD + start : PAD + start + block, :]
        mixed[start : start + block, :] = rounded(filtered[1] * filtered[2])
        gmixed[start : start + block, :] = rounded(grad * filtered[0])
        base[0, start : start + block, :] = grad
        base[1, start : start + block, :] = filtered[2]
        base[2, start : start + block, :] = filtered[1]
    mixed[0:8, :] = mixed[0:8, :] * kept
    gmixed[0:8, :] = gmixed[0:8, :] * kept
    for stream in range(3):
        base[stream, 0:8, :] = base[stream, 0:8, :] * kept


def first_kernel(
    half_ref,
    modal_ref,
    rate_ref,
    xt,
    base,
    conv_ref,
    msg_ref,
    part_y,
    part_z,
    states,
    upper_w,
    lower_w,
    sums,
    rows,
):
    _, toks, lanes = base.shape
    mixed, gmixed = base.at[3], base.at[4]
    fwd_ref, bwd_ref = conv_ref.at[0], conv_ref.at[1]
    chunks = lanes // OWNED
    f32 = jnp.float32
    chunk_of, _ = lane_ids(chunks, 8)
    half = half_ref[0]
    late = half.astype(f32)
    early = 1.0 - late
    zero = jnp.zeros((8, lanes), f32)
    block = 32

    rates, decay, _, amp = modal_rows(modal_ref)

    def row_of(ref, tok):
        return jnp.broadcast_to(ref[pl.ds(tok, 1), :], (8, lanes))

    def local_body(tok, carry):
        e0, e1, f0, f1 = carry
        xb = row_of(mixed, tok)
        gb = row_of(gmixed, toks - 1 - tok)
        return (
            decay[0] * e0 + xb,
            decay[1] * e1 + xb,
            decay[0] * f0 + gb,
            decay[1] * f1 + gb,
        )

    e0, e1, f0, f1 = lax.fori_loop(0, toks, local_body, (zero,) * 4, unroll=16)
    ends = [e0, e1]
    heads = [f0, f1]
    step = 1
    while step < chunks:
        for i in range(2):
            power = jnp.exp(rates[i] * (-1.0 * toks * step))
            moved = jnp.where(chunk_of >= step, pltpu.roll(ends[i], step, 1), 0.0)
            ends[i] = ends[i] + power * moved
            moved = jnp.where(chunk_of < chunks - step, pltpu.roll(heads[i], lanes - step, 1), 0.0)
            heads[i] = heads[i] + power * moved
        step *= 2
    start_h = [jnp.where(chunk_of >= 1, pltpu.roll(e, 1, 1), 0.0) for e in ends]
    start_p = [jnp.where(chunk_of < chunks - 1, pltpu.roll(f, lanes - 1, 1), 0.0) for f in heads]

    def forward_body(tok, carry):
        h0, h1, r0, r1, d0, d1 = carry
        xb = row_of(mixed, tok)
        gb = row_of(gmixed, tok)
        h0 = decay[0] * h0 + xb
        h1 = decay[1] * h1 + xb
        keep(part_y, tok, amp[0] * h0 + amp[1] * h1)
        states[pl.ds(pl.multiple_of(16 * tok, 8), 8), :] = h0
        states[pl.ds(pl.multiple_of(16 * tok + 8, 8), 8), :] = h1
        return (
            h0,
            h1,
            r0 + gb * h0,
            r1 + gb * h1,
            decay[0] * d0 + h0,
            decay[1] * d1 + h1,
        )

    _, _, r0, r1, d0, d1 = lax.fori_loop(
        0, toks, forward_body, (start_h[0], start_h[1]) + (zero,) * 4, unroll=16
    )

    def backward_body(step_index, carry):
        p0, p1, k0, k1, c0, c1 = carry
        tok = toks - 1 - step_index
        gb = row_of(gmixed, tok)
        q0 = decay[0] * p0
        q1 = decay[1] * p1
        k0 = k0 + states[pl.ds(pl.multiple_of(16 * tok, 8), 8), :] * q0
        k1 = k1 + states[pl.ds(pl.multiple_of(16 * tok + 8, 8), 8), :] * q1
        p0 = q0 + gb
        p1 = q1 + gb
        keep(part_z, tok, amp[0] * p0 + amp[1] * p1)
        return (p0, p1, k0, k1, decay[0] * c0 + p0, decay[1] * c1 + p1)

    _, _, k0, k1, c0, c1 = lax.fori_loop(
        0, toks, backward_body, (start_p[0], start_p[1]) + (zero,) * 4, unroll=16
    )

    for start in range(0, toks, block):
        fwd_ref[start : start + block, :] = folded(part_y, 8 * start, block)
        bwd_ref[start : start + block, :] = folded(part_z, 8 * start, block)

    for stream in range(3):
        tap_sums = [zero for _ in range(TAPS)]
        for start in range(0, toks, block):
            conv = (fwd_ref if stream == 0 else bwd_ref)[start : start + block, :]
            own = conv * base[stream, start : start + block, :]
            for tap in range(TAPS):
                lo = PAD - tap + start
                prod = own * xt[stream, lo : lo + block, :]
                for sub in range(0, block, 8):
                    tap_sums[tap] = tap_sums[tap] + prod[sub : sub + 8, :]
        for tap in range(TAPS):
            keep(sums, stream * TAPS + tap, tap_sums[tap])
    for index in range(3 * TAPS, 24):
        keep(sums, index, zero)
    rows[SHORT : SHORT + 24, :] = folded(sums, 0, 24)
    rows[SHORT + 24 : COMPACT, :] = zero

    bf16 = jnp.bfloat16
    rate_line = jnp.exp(rate_ref[...])
    rate_line = jnp.concatenate([rate_line, jnp.zeros((OWNED, toks - MODES), f32)], axis=1)
    rate_line = one_line(rate_line, 0, OWNED, MODES)
    row_lane = lax.broadcasted_iota(jnp.int32, (lanes, toks), 0)
    col_owner = lax.broadcasted_iota(jnp.int32, (lanes, toks), 1) // MODES
    row_chunk = (row_lane % chunks).astype(f32)
    spread = late * (toks * row_chunk - (TAPS - 2.0)) + early * (
        toks * (chunks - 1.0 - row_chunk) + 1.0
    )
    across = jnp.where(row_lane // chunks == col_owner, jnp.exp(-rate_line * spread), 0.0)
    across_hi = across.astype(bf16)
    across_lo = (across - across_hi.astype(f32)).astype(bf16)
    row_tok = lax.broadcasted_iota(jnp.int32, (toks, toks), 0).astype(f32)
    along = jnp.exp(-rate_line * (late * row_tok + early * (toks - 1.0 - row_tok)))

    def respond(slot, stream):
        for tap in range(TAPS):
            for start in range(0, toks, block):
                span = slice(start, start + block)
                lo = PAD - tap + start
                value = base[stream, span, :] * xt[stream, lo : lo + block, :]
                upper = value.astype(bf16)
                upper_w[tap, span, :] = upper
                lower_w[tap, span, :] = (value - upper.astype(f32)).astype(bf16)
            total = (
                jnp.dot(upper_w[tap], across_lo, preferred_element_type=f32)
                + jnp.dot(lower_w[tap], across_hi, preferred_element_type=f32)
                + jnp.dot(upper_w[tap], across_hi, preferred_element_type=f32)
            )
            at = OWNED + slot + tap
            msg_ref[at : at + 1, :] = jnp.sum(total * along, axis=0, keepdims=True)

    span_c = chunk_of.astype(f32)
    msg_ref[OWNED:MESSAGE, :] = jnp.zeros((MESSAGE - OWNED, toks), f32)

    @pl.when(half == 0)
    def _():
        respond(0, 1)
        respond(TAPS, 2)
        for stream in range(4):
            lo = EDGE + 8 * stream
            rows[lo : lo + 8, :] = jnp.where(
                chunk_of == chunks - 1, xt[stream, toks : toks + PAD, :], 0.0
            )
        for i in range(2):
            weight = jnp.exp(-rates[i] * (toks * (chunks - 1.0 - span_c)))
            rows[STATE + 8 * i : STATE + 8 * i + 8, :] = jnp.where(
                chunk_of == chunks - 1, ends[i], 0.0
            )
            rows[DERIV + 8 * i : DERIV + 8 * i + 8, :] = (d0, d1)[i] * weight

    @pl.when(half != 0)
    def _():
        respond(0, 0)
        for stream in range(4):
            lo = EDGE + 8 * stream
            rows[lo : lo + 8, :] = jnp.where(chunk_of == 0, xt[stream, PAD : 2 * PAD, :], 0.0)
        for i in range(2):
            grow = jnp.exp(rates[i] * (TAPS - 1.0))
            weight = jnp.exp(-rates[i] * (toks * span_c))
            first = jnp.where(chunk_of == 0, heads[i], 0.0)
            rows[STATE + 8 * i : STATE + 8 * i + 8, :] = first * grow
            rows[DERIV + 8 * i : DERIV + 8 * i + 8, :] = (
                (c0, c1)[i] * weight - (TAPS - 1.0) * first
            ) * grow

    for i in range(2):
        rows[RSUM + 8 * i : RSUM + 8 * i + 8, :] = (r0, r1)[i]
        rows[KSUM + 8 * i : KSUM + 8 * i + 8, :] = (k0, k1)[i]
    msg_ref[0:OWNED, :] = lane_sums(rows[...], chunks).T[:OWNED, :]


def second_kernel(
    half_ref,
    own_ref,
    other_ref,
    taps_ref,
    modal_ref,
    xt,
    hat_ref,
    conv_ref,
    send_ref,
    sums_ref,
    edge0,
    edge1,
    edges,
    part,
    driven,
    outs,
    grads,
    out_rows,
):
    _, toks, lanes = conv_ref.shape
    fwd_ref, bwd_ref = conv_ref.at[0], conv_ref.at[1]
    chunks = lanes // OWNED
    f32 = jnp.float32
    chunk_of, _ = lane_ids(chunks, 8)
    scale = 1.0 / math.sqrt(2 * chunks * toks)
    half = half_ref[0]
    late = half.astype(f32)
    early = 1.0 - late
    rates, decay, root, amp = modal_rows(modal_ref)
    fringe = TAPS - 1
    zero = jnp.zeros((8, lanes), f32)

    own = own_ref[...]
    other = other_ref[...]
    message0 = own * early + other * late
    message1 = own * late + other * early
    edge0[...] = lane_spread(message0[0:OWNED, :], chunks)
    edge1[...] = lane_spread(message1[0:OWNED, :], chunks)

    def pair(ref, first):
        return [ref[first + 8 * i : first + 8 * i + 8, :] for i in range(2)]

    row_id = lax.broadcasted_iota(jnp.int32, (8, lanes), 0)
    live = jnp.where(row_id < fringe, 1.0, 0.0)
    hats = []
    for stream in range(3):
        edges[stream, 0:8, :] = edge0[EDGE + 8 * stream : EDGE + 8 * stream + 8, :]
        edges[stream, 8:16, :] = edge1[EDGE + 8 * stream : EDGE + 8 * stream + 8, :]
        total = None
        for tap in range(TAPS):
            term = tap_row(taps_ref, stream, tap) * edges[stream, 8 - tap : 16 - tap, :]
            total = term if total is None else total + term
        hats.append(total)
    grad_edge = edge1[EDGE + 24 : EDGE + 32, :]
    x_edge = rounded(hats[1] * hats[2])
    g_edge = rounded(grad_edge * hats[0])

    state = pair(edge0, STATE)
    passed = []
    y_edge = zero
    for tok in range(fringe):
        xb = jnp.broadcast_to(x_edge[tok : tok + 1, :], (8, lanes))
        state = [decay[i] * state[i] + xb for i in range(2)]
        passed.append(state)
        line = jnp.sum(amp[0] * state[0] + amp[1] * state[1], axis=0, keepdims=True)
        y_edge = jnp.where(row_id == tok, line, y_edge)
    after = state
    back = pair(edge1, STATE)
    r_edge = [zero, zero]
    k_edge = [zero, zero]
    z_edge = zero
    adjoint = back
    for tok in range(fringe - 1, -1, -1):
        gb = jnp.broadcast_to(g_edge[tok : tok + 1, :], (8, lanes))
        moved = [decay[i] * adjoint[i] for i in range(2)]
        k_edge = [k_edge[i] + passed[tok][i] * moved[i] for i in range(2)]
        r_edge = [r_edge[i] + gb * passed[tok][i] for i in range(2)]
        adjoint = [moved[i] + gb for i in range(2)]
        line = jnp.sum(amp[0] * adjoint[0] + amp[1] * adjoint[1], axis=0, keepdims=True)
        z_edge = jnp.where(row_id == tok, line, z_edge)

    span_c = chunk_of.astype(f32)
    carry = []
    for i in range(2):
        into_late = after[i] * jnp.exp(-rates[i] * (toks * span_c - (fringe - 1.0)))
        into_early = adjoint[i] * jnp.exp(-rates[i] * (toks * (chunks - 1.0 - span_c) + 1.0))
        carry.append(amp[i] * (early * into_early + late * into_late))

    sub = row_id.astype(f32)[:, :128]
    sub = late * sub + early * (7.0 - sub)
    stride8 = [jnp.exp(-8.0 * r) for r in rates]
    blocks = toks // 8
    for cut in range(lanes // 128):
        cols = slice(cut * 128, (cut + 1) * 128)
        modes = []
        factors = []
        for i in range(2):
            for m in range(8):
                rate = jnp.broadcast_to(rates[i][m : m + 1, cols], (8, 128))
                lead = jnp.broadcast_to(carry[i][m : m + 1, cols], (8, 128))
                modes.append(lead * jnp.exp(-rate * sub))
                factors.append(jnp.broadcast_to(stride8[i][m : m + 1, cols], (8, 128)))

        def reply_body(step_index, values, cols=cols, factors=factors):
            at = half * step_index + (1 - half) * (blocks - 1 - step_index)
            total = list(values)
            while len(total) > 1:
                total = [total[k] + total[k + 1] for k in range(0, len(total), 2)]
            part[pl.ds(pl.multiple_of(8 * at, 8), 8), cols] = total[0]
            return tuple(v * f for v, f in zip(values, factors))

        lax.fori_loop(0, blocks, reply_body, tuple(modes), unroll=4)

    patch = (row_id < fringe) & (chunk_of == 0) & (jnp.broadcast_to(late, (8, lanes)) > 0.5)
    y_edge = rounded(y_edge)
    z_edge = rounded(z_edge)
    for start, count in ((0, 8), (8, 24), (32, 32), (64, 32), (96, 32)):
        span = slice(start, start + count)
        reply = part[span, :]
        conv = rounded(fwd_ref[span, :] + late * reply)
        turn = rounded(bwd_ref[span, :] + early * reply)
        hat = [hat_ref[stream, span, :] for stream in range(3)]
        if start == 0:
            conv = jnp.where(patch, y_edge, conv)
            turn = jnp.where(patch, z_edge, turn)
            hat = [jnp.where(patch, hats[stream], hat[stream]) for stream in range(3)]
        grads[0, span, :] = xt[3, PAD + start : PAD + start + count, :] * conv
        grads[1, span, :] = turn * hat[2]
        grads[2, span, :] = turn * hat[1]
        outs[0, span, :] = hat[0] * conv
    edge_grads = (grad_edge * y_edge, z_edge * hats[2], z_edge * hats[1])
    for stream in range(3):
        head = pltpu.roll(grads[stream, 0:PAD, :], lanes - 1, 1)
        grads[stream, toks : toks + PAD, :] = jnp.where(
            chunk_of < chunks - 1, head, early * edge_grads[stream]
        )
    block = 32
    for stream in range(3):
        for start in range(0, toks, block):
            total = None
            for tap in range(TAPS):
                term = (
                    tap_row(taps_ref, stream, tap)
                    * grads[stream, start + tap : start + tap + block, :]
                )
                total = term if total is None else total + term
            outs[1 + stream, start : start + block, :] = total

    single = jnp.where(chunk_of == 0, scale, 0.0)
    drives = jnp.concatenate(
        [amp[i] * after[i] * single for i in range(2)]
        + [amp[i] * adjoint[i] * single for i in range(2)]
        + [jnp.zeros((toks - 4 * 8, lanes), f32)],
        axis=0,
    )
    drives = lane_sums(drives, chunks).T[:OWNED, :]
    in_first = lax.broadcasted_iota(jnp.int32, (OWNED, toks), 1) < MODES
    forced = one_line(jnp.where(in_first, drives, 0.0), 0, OWNED, MODES)
    turned = pltpu.roll(drives, toks - MODES, 1)
    turned = one_line(jnp.where(in_first, turned, 0.0), 0, OWNED, MODES)
    driven[0:TAPS, :] = message1[OWNED : OWNED + TAPS, :] * forced
    driven[TAPS : 3 * TAPS, :] = message0[OWNED : OWNED + 2 * TAPS, :] * turned
    driven[3 * TAPS : 24, :] = jnp.zeros((24 - 3 * TAPS, toks), f32)
    short = [
        edge0[SHORT + 8 * i : SHORT + 8 * i + 8, :] + edge1[SHORT + 8 * i : SHORT + 8 * i + 8, :]
        for i in range(3)
    ]
    for stream in range(3):
        live_grad = edge_grads[stream] * live
        for tap in range(TAPS):
            index = stream * TAPS + tap
            term = live_grad * edges[stream, 8 - tap : 16 - tap, :]
            line = jnp.sum(term, axis=0, keepdims=True)
            short[index // 8] = short[index // 8] + jnp.where(row_id == index % 8, line, 0.0)
    r_all = []
    k_all = []
    for i in range(2):
        first_r, late_r = pair(edge0, RSUM)[i], pair(edge1, RSUM)[i]
        first_k, late_k = pair(edge0, KSUM)[i], pair(edge1, KSUM)[i]
        lag_early, lag_late = pair(edge0, DERIV)[i], pair(edge1, DERIV)[i]
        r_all.append(first_r + late_r + decay[i] * back[i] * after[i] + r_edge[i])
        k_all.append(
            first_k
            + late_k
            + decay[i] * lag_early * adjoint[i]
            + decay[i] * after[i] * (lag_late - back[i])
            + k_edge[i]
        )
    columns = jnp.concatenate(
        [value * single for value in short]
        + [root[i] * r_all[i] * single for i in range(2)]
        + [amp[i] * (0.5 * r_all[i] - rates[i] * k_all[i]) * single for i in range(2)],
        axis=0,
    )
    columns = lane_sums(columns, chunks)
    replies = lane_sums(driven[...], MODES)
    columns = jnp.concatenate(
        [columns[0:24, :] + replies, columns[24:56, :], jnp.zeros((128 - 56, 128), f32)], axis=0
    )
    totals = columns.T[:OWNED, :]
    sums_ref[...] = totals[:, 24:56]

    per_tile = toks // chunks
    for stream in range(4):
        for group in range(OWNED // per_tile):
            tile = outs[stream, :, group * toks : (group + 1) * toks].T
            for c in range(per_tile):
                out_rows[
                    pl.ds(stream * OWNED + group * per_tile + c, chunks, stride=ROWS_OUT), :
                ] = tile[c * chunks : (c + 1) * chunks]
    wide = jnp.concatenate([totals[:, 0:24], jnp.zeros((8, toks - 24), f32)], axis=1)
    for group in range(2):
        line = one_line(wide, 4 * group, 4, 32)
        upper = rounded(line)
        out_rows[pl.ds(32 + group, chunks, stride=ROWS_OUT), :] = jnp.broadcast_to(
            upper, (chunks, toks)
        )
        out_rows[pl.ds(34 + group, chunks, stride=ROWS_OUT), :] = jnp.broadcast_to(
            line - upper, (chunks, toks)
        )
    for spare in range(36, ROWS_OUT):
        out_rows[pl.ds(spare, chunks, stride=ROWS_OUT), :] = jnp.zeros((chunks, toks), f32)
    send_ref[...] = out_rows[...].reshape(send_ref.shape).astype(jnp.bfloat16)


def run_pack(query_in, key_in, value_in, grad_out):
    chans, toks = query_in.shape
    owners = chans // OWNED
    return pl.pallas_call(
        pack_kernel,
        in_specs=[pl.BlockSpec(memory_space=pltpu.HBM)] * 4,
        out_shape=jax.ShapeDtypeStruct((owners, ROWS_IN, toks), jnp.bfloat16),
        scratch_shapes=[
            pltpu.VMEM((4, chans, toks), jnp.bfloat16),
            pltpu.VMEM((4, chans, toks), jnp.float32),
            pltpu.VMEM((owners * ROWS_IN, toks), jnp.float32),
            pltpu.SemaphoreType.DMA((4,)),
        ],
        compiler_params=pltpu.CompilerParams(vmem_limit_bytes=VMEM_LIMIT),
    )(*[pltpu.with_memory_space_constraint(x, pltpu.HBM) for x in (query_in, key_in, value_in, grad_out)])


def modal_kernel(both_ref, after_ref, out_ref):
    out_ref[...] = both_ref[...]


def run_modal(both, after):
    vmem = pl.BlockSpec(memory_space=pltpu.VMEM)
    return pl.pallas_call(
        modal_kernel,
        in_specs=[vmem, pl.BlockSpec(memory_space=pltpu.HBM)],
        out_specs=vmem,
        out_shape=jax.ShapeDtypeStruct(both.shape, jnp.float32),
        cost_estimate=pl.CostEstimate(flops=2 * 10**10, bytes_accessed=1024, transcendentals=0),
        compiler_params=pltpu.CompilerParams(vmem_limit_bytes=1024 * 1024),
    )(both, pltpu.with_memory_space_constraint(after, pltpu.HBM))


def plane(*shape, dtype=jnp.float32):
    return jax.ShapeDtypeStruct(shape, dtype)


def run_filter(half, recv, taps):
    chunks, _, toks = recv.shape
    lanes = OWNED * chunks
    vmem = pl.BlockSpec(memory_space=pltpu.VMEM)
    return pl.pallas_call(
        filter_kernel,
        in_specs=[pl.BlockSpec(memory_space=pltpu.SMEM), vmem, vmem],
        out_shape=(
            plane(4, PAD + toks, lanes),
            plane(3, toks, lanes),
            plane(5, toks, lanes),
        ),
        scratch_shapes=[pltpu.VMEM((chunks * ROWS_IN, toks), jnp.float32)],
        cost_estimate=pl.CostEstimate(flops=2 * 10**10, bytes_accessed=1024, transcendentals=0),
        compiler_params=pltpu.CompilerParams(vmem_limit_bytes=VMEM_LIMIT),
    )(half, recv, taps)


def run_first(half, modal, log_rate, xt, base):
    _, toks, lanes = base.shape
    f32 = jnp.float32
    vmem = pl.BlockSpec(memory_space=pltpu.VMEM)
    return pl.pallas_call(
        first_kernel,
        in_specs=[pl.BlockSpec(memory_space=pltpu.SMEM)] + [vmem] * 4,
        out_shape=(plane(2, toks, lanes), plane(MESSAGE, toks)),
        scratch_shapes=[
            pltpu.VMEM((2, 8 * toks, lanes // 2), f32),
            pltpu.VMEM((2, 8 * toks, lanes // 2), f32),
            pltpu.VMEM((16 * toks, lanes), f32),
            pltpu.VMEM((TAPS, toks, lanes), jnp.bfloat16),
            pltpu.VMEM((TAPS, toks, lanes), jnp.bfloat16),
            pltpu.VMEM((2, 8 * 24, lanes // 2), f32),
            pltpu.VMEM((COMPACT, lanes), f32),
        ],
        compiler_params=pltpu.CompilerParams(vmem_limit_bytes=VMEM_LIMIT),
    )(half, modal, log_rate, xt, base)


def run_second(half, own, other, taps, modal, xt, hat, conv):
    _, toks, lanes = conv.shape
    chunks = lanes // OWNED
    f32 = jnp.float32
    vmem = pl.BlockSpec(memory_space=pltpu.VMEM)
    return pl.pallas_call(
        second_kernel,
        in_specs=[pl.BlockSpec(memory_space=pltpu.SMEM)] + [vmem] * 7,
        out_shape=(
            plane(chunks, ROWS_OUT, toks, dtype=jnp.bfloat16),
            plane(OWNED, 2 * MODES),
        ),
        scratch_shapes=[
            pltpu.VMEM((COMPACT, lanes), f32),
            pltpu.VMEM((COMPACT, lanes), f32),
            pltpu.VMEM((3, 16, lanes), f32),
            pltpu.VMEM((toks, lanes), f32),
            pltpu.VMEM((24, toks), f32),
            pltpu.VMEM((4, toks, lanes), f32),
            pltpu.VMEM((3, toks + PAD, lanes), f32),
            pltpu.VMEM((chunks * ROWS_OUT, toks), f32),
        ],
        compiler_params=pltpu.CompilerParams(vmem_limit_bytes=VMEM_LIMIT),
    )(half, own, other, taps, modal, xt, hat, conv)


def run_unpack(recv):
    owners, _, toks = recv.shape
    chans = OWNED * owners
    whole = jax.ShapeDtypeStruct((chans, toks), jnp.bfloat16)
    return pl.pallas_call(
        unpack_kernel,
        out_shape=(whole,) * 4 + (jax.ShapeDtypeStruct((3, TAPS, chans), jnp.float32),),
        scratch_shapes=[
            pltpu.VMEM((owners * ROWS_OUT, toks), jnp.float32),
            pltpu.VMEM((5, chans, toks), jnp.float32),
        ],
        compiler_params=pltpu.CompilerParams(vmem_limit_bytes=VMEM_LIMIT),
    )(recv)


def tap_rows(weights, chunks):
    rows = jnp.concatenate(
        [weights.reshape(3 * TAPS, OWNED), jnp.zeros((3, OWNED), jnp.float32)], axis=0
    )
    return jnp.repeat(rows, chunks, axis=1)


def local(query_in, key_in, value_in, short_weight, residue, log_rate, grad_out):
    devices = lax.axis_size("seq")
    chunks = devices // 2
    chans = query_in.shape[0]
    me = lax.axis_index("seq")
    half = me // chunks
    index = me % chunks
    groups = [list(range(chunks)), list(range(chunks, devices))]
    across = [(i, (i + chunks) % devices) for i in range(devices)]

    send = run_pack(query_in, key_in, value_in, grad_out)
    mine = run_modal(jnp.concatenate([log_rate, residue], axis=1), send)
    theirs = lax.ppermute(mine, "seq", across)
    weights = jnp.concatenate(
        [
            lax.dynamic_slice(short_weight, (0, 0, 4 * index + at), (3, TAPS, 4))
            for at in (0, chans // 2)
        ],
        axis=2,
    )
    taps = tap_rows(weights, chunks)
    which = half.reshape(1).astype(jnp.int32)

    recv = lax.all_to_all(send, "seq", 0, 0, tiled=True, axis_index_groups=groups)
    xt, hat, *inner = run_filter(which, recv, taps)
    theirs, inner = lax.optimization_barrier((theirs, inner))
    modal_params = jnp.where(
        half == 0, jnp.concatenate([mine, theirs]), jnp.concatenate([theirs, mine])
    )
    modal = jnp.repeat(modal_params.T, chunks, axis=1)
    conv, message = run_first(which, modal, modal_params[:, :MODES], xt, *inner)
    other = lax.ppermute(message, "seq", across)
    back, sums = run_second(which, message, other, taps, modal, xt, hat, conv)
    final = lax.all_to_all(back, "seq", 0, 0, tiled=True, axis_index_groups=groups)
    output, grad_query, grad_key, grad_value, grad_short = run_unpack(final)
    own_modal = lax.dynamic_slice(sums, (4 * half, 0), (4, 2 * MODES))
    return (
        output,
        grad_query,
        grad_key,
        grad_value,
        grad_short,
        own_modal[:, :MODES],
        own_modal[:, MODES:],
    )


def solution(mesh):
    return jax.shard_map(
        local,
        mesh=mesh,
        in_specs=(
            P("chan", "seq"),
            P("chan", "seq"),
            P("chan", "seq"),
            P(None, None, "chan"),
            P(("chan", "seq"), None),
            P(("chan", "seq"), None),
            P("chan", "seq"),
        ),
        out_specs=(
            P("chan", "seq"),
            P("chan", "seq"),
            P("chan", "seq"),
            P("chan", "seq"),
            P(None, None, "chan"),
            P(("chan", "seq"), None),
            P(("chan", "seq"), None),
        ),
        check_vma=False,
    )
```

```python
import math

import jax
import jax.numpy as jnp
from jax import lax
from jax.experimental import pallas as pl
from jax.experimental.pallas import tpu as pltpu
from jax.sharding import PartitionSpec as P

TAPS = 7
MODES = 16
PAD = 8
OWNED = 8
ROWS_IN = 4 * OWNED
ROWS_OUT = 36
VMEM_LIMIT = 16 * 1024 * 1024

STATE, DERIV, RSUM, KSUM, EDGE, SHORT, COMPACT = 0, 16, 32, 48, 64, 96, 128
MESSAGE = OWNED + 16


def first_row(chan, chans):
    return chan if chan < 4 else chans // 2 + chan - 4


def pack_kernel(query_ref, key_ref, value_ref, grad_ref, send_ref, held, wide, mixed_rows, sems):
    owners = send_ref.shape[0]
    chans = query_ref.shape[0]
    copies = [
        pltpu.make_async_copy(ref, held.at[stream], sems.at[stream])
        for stream, ref in enumerate((query_ref, key_ref, value_ref, grad_ref))
    ]
    for copy in copies:
        copy.start()
    for stream, copy in enumerate(copies):
        copy.wait()
        wide[stream] = held[stream].astype(jnp.float32)
        for chan in range(OWNED):
            mixed_rows[pl.ds(stream * OWNED + chan, owners, stride=ROWS_IN), :] = wide[
                stream, pl.ds(first_row(chan, chans), owners, stride=4), :
            ]
    send_ref[...] = mixed_rows[...].reshape(send_ref.shape).astype(jnp.bfloat16)


def unpack_kernel(
    recv_ref, out_ref, gq_ref, gk_ref, gv_ref, short_ref, rows, wide, staged, sems
):
    owners = recv_ref.shape[0] // ROWS_OUT
    chans = out_ref.shape[0]
    rows[...] = recv_ref[...].astype(jnp.float32)
    sends = []
    for stream, ref in enumerate((out_ref, gq_ref, gk_ref, gv_ref)):
        for chan in range(OWNED):
            wide[stream, pl.ds(first_row(chan, chans), owners, stride=4), :] = rows[
                pl.ds(stream * OWNED + chan, owners, stride=ROWS_OUT), :
            ]
        staged[stream] = wide[stream].astype(jnp.bfloat16)
        send = pltpu.make_async_copy(staged.at[stream], ref, sems.at[stream])
        send.start()
        sends.append(send)
    for group in range(2):
        short = (
            rows[pl.ds(32 + group, owners, stride=ROWS_OUT), :]
            + rows[pl.ds(34 + group, owners, stride=ROWS_OUT), :]
        )
        for chan in range(4):
            wide[4, pl.ds(first_row(4 * group + chan, chans), owners, stride=4), :] = pltpu.roll(
                short, (128 - 32 * chan) % 128, 1
            )
    turned = wide[4].T
    for stream in range(3):
        short_ref[stream] = turned[stream * TAPS : (stream + 1) * TAPS, :]
    for send in sends:
        send.wait()


def lane_ids(chunks, rows):
    lane = lax.broadcasted_iota(jnp.int32, (rows, OWNED * chunks), 1)
    return lane % chunks, lane // chunks


def owner_pick(chunks):
    owner = lane_ids(chunks, OWNED)[1]
    return (owner == lax.broadcasted_iota(jnp.int32, owner.shape, 0)).astype(jnp.float32)


def three_parts(value):
    upper = rounded(value)
    middle = rounded(value - upper)
    return [upper, middle, value - upper - middle]


def lane_sums(value, chunks):
    shape = (value.shape[1], 128)
    owner = lax.broadcasted_iota(jnp.int32, shape, 0) // chunks
    pick = (owner == lax.broadcasted_iota(jnp.int32, shape, 1)).astype(jnp.float32)
    pick = pick.astype(jnp.bfloat16)
    total = None
    for part in reversed(three_parts(value)):
        term = jnp.dot(part.astype(jnp.bfloat16), pick, preferred_element_type=jnp.float32)
        total = term if total is None else total + term
    return total


def lane_spread(value, chunks):
    pick = owner_pick(chunks)
    return lax.dot_general(
        jnp.concatenate(three_parts(value), axis=0).astype(jnp.bfloat16),
        jnp.concatenate([pick] * 3, axis=0).astype(jnp.bfloat16),
        (((0,), (0,)), ((), ())),
        preferred_element_type=jnp.float32,
    )


def one_line(value, first, count, width):
    line = value[first : first + 1, :]
    for chan in range(1, count):
        at = first + chan
        line = line + pltpu.roll(value, width * chan, 1)[at : at + 1, :]
    return line


def modal_rows(modal_ref):
    rates = [jnp.exp(modal_ref[8 * i : 8 * i + 8, :]) for i in range(2)]
    resid = [modal_ref[16 + 8 * i : 24 + 8 * i, :] for i in range(2)]
    decay = [jnp.exp(-r) for r in rates]
    root = [jnp.sqrt(2.0 * r) for r in rates]
    amp = [resid[i] * root[i] for i in range(2)]
    return rates, decay, root, amp


def keep(ref, tok, value):
    lanes = ref.shape[2]
    for half in range(2):
        ref[half, pl.ds(pl.multiple_of(8 * tok, 8), 8), :] = value[
            :, half * lanes : (half + 1) * lanes
        ]


def folded(ref, first, count):
    halves = []
    for half in range(2):
        total = None
        for sub in range(8):
            term = ref[half, pl.ds(first + sub, count, stride=8), :]
            total = term if total is None else total + term
        halves.append(total)
    return jnp.concatenate(halves, axis=1)


def tap_row(taps_ref, stream, tap):
    index = stream * TAPS + tap
    return taps_ref[index : index + 1, :]


def rounded(value):
    return value.astype(jnp.bfloat16).astype(jnp.float32)


def filter_kernel(
    half_ref,
    recv_ref,
    taps_ref,
    xt,
    hat_ref,
    base,
    raw,
):
    mixed, gmixed = base.at[3], base.at[4]
    chunks = recv_ref.shape[0]
    toks = recv_ref.shape[2]
    lanes = OWNED * chunks
    f32 = jnp.float32
    chunk_of, _ = lane_ids(chunks, 8)
    half = half_ref[0]
    late = half.astype(f32)
    block = 32

    raw[...] = recv_ref[...].reshape(raw.shape).astype(f32)
    per_tile = toks // chunks
    for stream in range(4):
        for group in range(OWNED // per_tile):
            tile = jnp.concatenate(
                [
                    raw[
                        pl.ds(stream * OWNED + group * per_tile + c, chunks, stride=ROWS_IN), :
                    ]
                    for c in range(per_tile)
                ],
                axis=0,
            )
            xt[stream, PAD : PAD + toks, group * toks : (group + 1) * toks] = tile.T
    for stream in range(3):
        tail = pltpu.roll(xt[stream, toks : toks + PAD, :], 1, 1)
        xt[stream, 0:PAD, :] = jnp.where(chunk_of >= 1, tail, 0.0)

    fringe = (lax.broadcasted_iota(jnp.int32, (8, lanes), 0) < TAPS - 1) & (chunk_of == 0)
    kept = 1.0 - jnp.where(fringe, late, 0.0)
    for start in range(0, toks, block):
        filtered = []
        for stream in range(3):
            total = None
            for tap in range(TAPS):
                lo = PAD - tap + start
                term = tap_row(taps_ref, stream, tap) * xt[stream, lo : lo + block, :]
                total = term if total is None else total + term
            filtered.append(total)
            hat_ref[stream, start : start + block, :] = total
        grad = xt[3, PAD + start : PAD + start + block, :]
        mixed[start : start + block, :] = rounded(filtered[1] * filtered[2])
        gmixed[start : start + block, :] = rounded(grad * filtered[0])
        base[0, start : start + block, :] = grad
        base[1, start : start + block, :] = filtered[2]
        base[2, start : start + block, :] = filtered[1]
    mixed[0:8, :] = mixed[0:8, :] * kept
    gmixed[0:8, :] = gmixed[0:8, :] * kept
    for stream in range(3):
        base[stream, 0:8, :] = base[stream, 0:8, :] * kept


def first_kernel(
    half_ref,
    modal_ref,
    rate_ref,
    xt,
    base,
    conv_ref,
    msg_ref,
    part_y,
    part_z,
    states,
    upper_w,
    lower_w,
    sums,
    rows,
):
    _, toks, lanes = base.shape
    mixed, gmixed = base.at[3], base.at[4]
    fwd_ref, bwd_ref = conv_ref.at[0], conv_ref.at[1]
    chunks = lanes // OWNED
    f32 = jnp.float32
    chunk_of, _ = lane_ids(chunks, 8)
    half = half_ref[0]
    late = half.astype(f32)
    early = 1.0 - late
    zero = jnp.zeros((8, lanes), f32)
    block = 32

    rates, decay, _, amp = modal_rows(modal_ref)

    def row_of(ref, tok):
        return jnp.broadcast_to(ref[pl.ds(tok, 1), :], (8, lanes))

    def local_body(tok, carry):
        e0, e1, f0, f1 = carry
        xb = row_of(mixed, tok)
        gb = row_of(gmixed, toks - 1 - tok)
        return (
            decay[0] * e0 + xb,
            decay[1] * e1 + xb,
            decay[0] * f0 + gb,
            decay[1] * f1 + gb,
        )

    e0, e1, f0, f1 = lax.fori_loop(0, toks, local_body, (zero,) * 4, unroll=16)
    ends = [e0, e1]
    heads = [f0, f1]
    step = 1
    while step < chunks:
        for i in range(2):
            power = jnp.exp(rates[i] * (-1.0 * toks * step))
            moved = jnp.where(chunk_of >= step, pltpu.roll(ends[i], step, 1), 0.0)
            ends[i] = ends[i] + power * moved
            moved = jnp.where(chunk_of < chunks - step, pltpu.roll(heads[i], lanes - step, 1), 0.0)
            heads[i] = heads[i] + power * moved
        step *= 2
    start_h = [jnp.where(chunk_of >= 1, pltpu.roll(e, 1, 1), 0.0) for e in ends]
    start_p = [jnp.where(chunk_of < chunks - 1, pltpu.roll(f, lanes - 1, 1), 0.0) for f in heads]

    def forward_body(tok, carry):
        h0, h1, r0, r1, d0, d1 = carry
        xb = row_of(mixed, tok)
        gb = row_of(gmixed, tok)
        h0 = decay[0] * h0 + xb
        h1 = decay[1] * h1 + xb
        keep(part_y, tok, amp[0] * h0 + amp[1] * h1)
        states[pl.ds(pl.multiple_of(16 * tok, 8), 8), :] = h0
        states[pl.ds(pl.multiple_of(16 * tok + 8, 8), 8), :] = h1
        return (
            h0,
            h1,
            r0 + gb * h0,
            r1 + gb * h1,
            decay[0] * d0 + h0,
            decay[1] * d1 + h1,
        )

    _, _, r0, r1, d0, d1 = lax.fori_loop(
        0, toks, forward_body, (start_h[0], start_h[1]) + (zero,) * 4, unroll=16
    )

    def backward_body(step_index, carry):
        p0, p1, k0, k1, c0, c1 = carry
        tok = toks - 1 - step_index
        gb = row_of(gmixed, tok)
        q0 = decay[0] * p0
        q1 = decay[1] * p1
        k0 = k0 + states[pl.ds(pl.multiple_of(16 * tok, 8), 8), :] * q0
        k1 = k1 + states[pl.ds(pl.multiple_of(16 * tok + 8, 8), 8), :] * q1
        p0 = q0 + gb
        p1 = q1 + gb
        keep(part_z, tok, amp[0] * p0 + amp[1] * p1)
        return (p0, p1, k0, k1, decay[0] * c0 + p0, decay[1] * c1 + p1)

    _, _, k0, k1, c0, c1 = lax.fori_loop(
        0, toks, backward_body, (start_p[0], start_p[1]) + (zero,) * 4, unroll=16
    )

    for start in range(0, toks, block):
        fwd_ref[start : start + block, :] = folded(part_y, 8 * start, block)
        bwd_ref[start : start + block, :] = folded(part_z, 8 * start, block)

    for stream in range(3):
        tap_sums = [zero for _ in range(TAPS)]
        for start in range(0, toks, block):
            conv = (fwd_ref if stream == 0 else bwd_ref)[start : start + block, :]
            own = conv * base[stream, start : start + block, :]
            for tap in range(TAPS):
                lo = PAD - tap + start
                prod = own * xt[stream, lo : lo + block, :]
                for sub in range(0, block, 8):
                    tap_sums[tap] = tap_sums[tap] + prod[sub : sub + 8, :]
        for tap in range(TAPS):
            keep(sums, stream * TAPS + tap, tap_sums[tap])
    for index in range(3 * TAPS, 24):
        keep(sums, index, zero)
    rows[SHORT : SHORT + 24, :] = folded(sums, 0, 24)
    rows[SHORT + 24 : COMPACT, :] = zero

    bf16 = jnp.bfloat16
    rate_line = jnp.exp(rate_ref[...])
    rate_line = jnp.concatenate([rate_line, jnp.zeros((OWNED, toks - MODES), f32)], axis=1)
    rate_line = one_line(rate_line, 0, OWNED, MODES)
    row_lane = lax.broadcasted_iota(jnp.int32, (lanes, toks), 0)
    col_owner = lax.broadcasted_iota(jnp.int32, (lanes, toks), 1) // MODES
    row_chunk = (row_lane % chunks).astype(f32)
    spread = late * (toks * row_chunk - (TAPS - 2.0)) + early * (
        toks * (chunks - 1.0 - row_chunk) + 1.0
    )
    across = jnp.where(row_lane // chunks == col_owner, jnp.exp(-rate_line * spread), 0.0)
    across_hi = across.astype(bf16)
    across_lo = (across - across_hi.astype(f32)).astype(bf16)
    row_tok = lax.broadcasted_iota(jnp.int32, (toks, toks), 0).astype(f32)
    along = jnp.exp(-rate_line * (late * row_tok + early * (toks - 1.0 - row_tok)))

    def respond(slot, stream):
        for tap in range(TAPS):
            for start in range(0, toks, block):
                span = slice(start, start + block)
                lo = PAD - tap + start
                value = base[stream, span, :] * xt[stream, lo : lo + block, :]
                upper = value.astype(bf16)
                upper_w[tap, span, :] = upper
                lower_w[tap, span, :] = (value - upper.astype(f32)).astype(bf16)
            total = (
                jnp.dot(upper_w[tap], across_lo, preferred_element_type=f32)
                + jnp.dot(lower_w[tap], across_hi, preferred_element_type=f32)
                + jnp.dot(upper_w[tap], across_hi, preferred_element_type=f32)
            )
            at = OWNED + slot + tap
            msg_ref[at : at + 1, :] = jnp.sum(total * along, axis=0, keepdims=True)

    span_c = chunk_of.astype(f32)
    msg_ref[OWNED:MESSAGE, :] = jnp.zeros((MESSAGE - OWNED, toks), f32)

    @pl.when(half == 0)
    def _():
        respond(0, 1)
        respond(TAPS, 2)
        for stream in range(4):
            lo = EDGE + 8 * stream
            rows[lo : lo + 8, :] = jnp.where(
                chunk_of == chunks - 1, xt[stream, toks : toks + PAD, :], 0.0
            )
        for i in range(2):
            weight = jnp.exp(-rates[i] * (toks * (chunks - 1.0 - span_c)))
            rows[STATE + 8 * i : STATE + 8 * i + 8, :] = jnp.where(
                chunk_of == chunks - 1, ends[i], 0.0
            )
            rows[DERIV + 8 * i : DERIV + 8 * i + 8, :] = (d0, d1)[i] * weight

    @pl.when(half != 0)
    def _():
        respond(0, 0)
        for stream in range(4):
            lo = EDGE + 8 * stream
            rows[lo : lo + 8, :] = jnp.where(chunk_of == 0, xt[stream, PAD : 2 * PAD, :], 0.0)
        for i in range(2):
            grow = jnp.exp(rates[i] * (TAPS - 1.0))
            weight = jnp.exp(-rates[i] * (toks * span_c))
            first = jnp.where(chunk_of == 0, heads[i], 0.0)
            rows[STATE + 8 * i : STATE + 8 * i + 8, :] = first * grow
            rows[DERIV + 8 * i : DERIV + 8 * i + 8, :] = (
                (c0, c1)[i] * weight - (TAPS - 1.0) * first
            ) * grow

    for i in range(2):
        rows[RSUM + 8 * i : RSUM + 8 * i + 8, :] = (r0, r1)[i]
        rows[KSUM + 8 * i : KSUM + 8 * i + 8, :] = (k0, k1)[i]
    msg_ref[0:OWNED, :] = lane_sums(rows[...], chunks).T[:OWNED, :]


def second_kernel(
    half_ref,
    own_ref,
    other_ref,
    taps_ref,
    modal_ref,
    xt,
    hat_ref,
    conv_ref,
    send_ref,
    sums_ref,
    edge0,
    edge1,
    edges,
    part,
    driven,
    outs,
    grads,
    out_rows,
):
    _, toks, lanes = conv_ref.shape
    fwd_ref, bwd_ref = conv_ref.at[0], conv_ref.at[1]
    chunks = lanes // OWNED
    f32 = jnp.float32
    chunk_of, _ = lane_ids(chunks, 8)
    scale = 1.0 / math.sqrt(2 * chunks * toks)
    half = half_ref[0]
    late = half.astype(f32)
    early = 1.0 - late
    rates, decay, root, amp = modal_rows(modal_ref)
    fringe = TAPS - 1
    zero = jnp.zeros((8, lanes), f32)

    own = own_ref[...]
    other = other_ref[...]
    message0 = own * early + other * late
    message1 = own * late + other * early
    edge0[...] = lane_spread(message0[0:OWNED, :], chunks)
    edge1[...] = lane_spread(message1[0:OWNED, :], chunks)

    def pair(ref, first):
        return [ref[first + 8 * i : first + 8 * i + 8, :] for i in range(2)]

    row_id = lax.broadcasted_iota(jnp.int32, (8, lanes), 0)
    live = jnp.where(row_id < fringe, 1.0, 0.0)
    hats = []
    for stream in range(3):
        edges[stream, 0:8, :] = edge0[EDGE + 8 * stream : EDGE + 8 * stream + 8, :]
        edges[stream, 8:16, :] = edge1[EDGE + 8 * stream : EDGE + 8 * stream + 8, :]
        total = None
        for tap in range(TAPS):
            term = tap_row(taps_ref, stream, tap) * edges[stream, 8 - tap : 16 - tap, :]
            total = term if total is None else total + term
        hats.append(total)
    grad_edge = edge1[EDGE + 24 : EDGE + 32, :]
    x_edge = rounded(hats[1] * hats[2])
    g_edge = rounded(grad_edge * hats[0])

    state = pair(edge0, STATE)
    passed = []
    y_edge = zero
    for tok in range(fringe):
        xb = jnp.broadcast_to(x_edge[tok : tok + 1, :], (8, lanes))
        state = [decay[i] * state[i] + xb for i in range(2)]
        passed.append(state)
        line = jnp.sum(amp[0] * state[0] + amp[1] * state[1], axis=0, keepdims=True)
        y_edge = jnp.where(row_id == tok, line, y_edge)
    after = state
    back = pair(edge1, STATE)
    r_edge = [zero, zero]
    k_edge = [zero, zero]
    z_edge = zero
    adjoint = back
    for tok in range(fringe - 1, -1, -1):
        gb = jnp.broadcast_to(g_edge[tok : tok + 1, :], (8, lanes))
        moved = [decay[i] * adjoint[i] for i in range(2)]
        k_edge = [k_edge[i] + passed[tok][i] * moved[i] for i in range(2)]
        r_edge = [r_edge[i] + gb * passed[tok][i] for i in range(2)]
        adjoint = [moved[i] + gb for i in range(2)]
        line = jnp.sum(amp[0] * adjoint[0] + amp[1] * adjoint[1], axis=0, keepdims=True)
        z_edge = jnp.where(row_id == tok, line, z_edge)

    span_c = chunk_of.astype(f32)
    carry = []
    for i in range(2):
        into_late = after[i] * jnp.exp(-rates[i] * (toks * span_c - (fringe - 1.0)))
        into_early = adjoint[i] * jnp.exp(-rates[i] * (toks * (chunks - 1.0 - span_c) + 1.0))
        carry.append(amp[i] * (early * into_early + late * into_late))

    sub = row_id.astype(f32)[:, :128]
    sub = late * sub + early * (7.0 - sub)
    stride8 = [jnp.exp(-8.0 * r) for r in rates]
    blocks = toks // 8
    for cut in range(lanes // 128):
        cols = slice(cut * 128, (cut + 1) * 128)
        modes = []
        factors = []
        for i in range(2):
            for m in range(8):
                rate = jnp.broadcast_to(rates[i][m : m + 1, cols], (8, 128))
                lead = jnp.broadcast_to(carry[i][m : m + 1, cols], (8, 128))
                modes.append(lead * jnp.exp(-rate * sub))
                factors.append(jnp.broadcast_to(stride8[i][m : m + 1, cols], (8, 128)))

        def reply_body(step_index, values, cols=cols, factors=factors):
            at = half * step_index + (1 - half) * (blocks - 1 - step_index)
            total = list(values)
            while len(total) > 1:
                total = [total[k] + total[k + 1] for k in range(0, len(total), 2)]
            part[pl.ds(pl.multiple_of(8 * at, 8), 8), cols] = total[0]
            return tuple(v * f for v, f in zip(values, factors))

        lax.fori_loop(0, blocks, reply_body, tuple(modes), unroll=4)

    patch = (row_id < fringe) & (chunk_of == 0) & (jnp.broadcast_to(late, (8, lanes)) > 0.5)
    y_edge = rounded(y_edge)
    z_edge = rounded(z_edge)
    for start, count in ((0, 8), (8, 24), (32, 32), (64, 32), (96, 32)):
        span = slice(start, start + count)
        reply = part[span, :]
        conv = rounded(fwd_ref[span, :] + late * reply)
        turn = rounded(bwd_ref[span, :] + early * reply)
        hat = [hat_ref[stream, span, :] for stream in range(3)]
        if start == 0:
            conv = jnp.where(patch, y_edge, conv)
            turn = jnp.where(patch, z_edge, turn)
            hat = [jnp.where(patch, hats[stream], hat[stream]) for stream in range(3)]
        grads[0, span, :] = xt[3, PAD + start : PAD + start + count, :] * conv
        grads[1, span, :] = turn * hat[2]
        grads[2, span, :] = turn * hat[1]
        outs[0, span, :] = hat[0] * conv
    edge_grads = (grad_edge * y_edge, z_edge * hats[2], z_edge * hats[1])
    for stream in range(3):
        head = pltpu.roll(grads[stream, 0:PAD, :], lanes - 1, 1)
        grads[stream, toks : toks + PAD, :] = jnp.where(
            chunk_of < chunks - 1, head, early * edge_grads[stream]
        )
    block = 32
    for stream in range(3):
        for start in range(0, toks, block):
            total = None
            for tap in range(TAPS):
                term = (
                    tap_row(taps_ref, stream, tap)
                    * grads[stream, start + tap : start + tap + block, :]
                )
                total = term if total is None else total + term
            outs[1 + stream, start : start + block, :] = total

    single = jnp.where(chunk_of == 0, scale, 0.0)
    drives = jnp.concatenate(
        [amp[i] * after[i] * single for i in range(2)]
        + [amp[i] * adjoint[i] * single for i in range(2)]
        + [jnp.zeros((toks - 4 * 8, lanes), f32)],
        axis=0,
    )
    drives = lane_sums(drives, chunks).T[:OWNED, :]
    in_first = lax.broadcasted_iota(jnp.int32, (OWNED, toks), 1) < MODES
    forced = one_line(jnp.where(in_first, drives, 0.0), 0, OWNED, MODES)
    turned = pltpu.roll(drives, toks - MODES, 1)
    turned = one_line(jnp.where(in_first, turned, 0.0), 0, OWNED, MODES)
    driven[0:TAPS, :] = message1[OWNED : OWNED + TAPS, :] * forced
    driven[TAPS : 3 * TAPS, :] = message0[OWNED : OWNED + 2 * TAPS, :] * turned
    driven[3 * TAPS : 24, :] = jnp.zeros((24 - 3 * TAPS, toks), f32)
    short = [
        edge0[SHORT + 8 * i : SHORT + 8 * i + 8, :] + edge1[SHORT + 8 * i : SHORT + 8 * i + 8, :]
        for i in range(3)
    ]
    for stream in range(3):
        live_grad = edge_grads[stream] * live
        for tap in range(TAPS):
            index = stream * TAPS + tap
            term = live_grad * edges[stream, 8 - tap : 16 - tap, :]
            line = jnp.sum(term, axis=0, keepdims=True)
            short[index // 8] = short[index // 8] + jnp.where(row_id == index % 8, line, 0.0)
    r_all = []
    k_all = []
    for i in range(2):
        first_r, late_r = pair(edge0, RSUM)[i], pair(edge1, RSUM)[i]
        first_k, late_k = pair(edge0, KSUM)[i], pair(edge1, KSUM)[i]
        lag_early, lag_late = pair(edge0, DERIV)[i], pair(edge1, DERIV)[i]
        r_all.append(first_r + late_r + decay[i] * back[i] * after[i] + r_edge[i])
        k_all.append(
            first_k
            + late_k
            + decay[i] * lag_early * adjoint[i]
            + decay[i] * after[i] * (lag_late - back[i])
            + k_edge[i]
        )
    columns = jnp.concatenate(
        [value * single for value in short]
        + [root[i] * r_all[i] * single for i in range(2)]
        + [amp[i] * (0.5 * r_all[i] - rates[i] * k_all[i]) * single for i in range(2)],
        axis=0,
    )
    columns = lane_sums(columns, chunks)
    replies = lane_sums(driven[...], MODES)
    columns = jnp.concatenate(
        [columns[0:24, :] + replies, columns[24:56, :], jnp.zeros((128 - 56, 128), f32)], axis=0
    )
    totals = columns.T[:OWNED, :]
    sums_ref[...] = totals[:, 24:56]

    per_tile = toks // chunks
    for stream in range(4):
        for group in range(OWNED // per_tile):
            tile = outs[stream, :, group * toks : (group + 1) * toks].T
            for c in range(per_tile):
                out_rows[
                    pl.ds(stream * OWNED + group * per_tile + c, chunks, stride=ROWS_OUT), :
                ] = tile[c * chunks : (c + 1) * chunks]
    wide = jnp.concatenate([totals[:, 0:24], jnp.zeros((8, toks - 24), f32)], axis=1)
    for group in range(2):
        line = one_line(wide, 4 * group, 4, 32)
        upper = rounded(line)
        out_rows[pl.ds(32 + group, chunks, stride=ROWS_OUT), :] = jnp.broadcast_to(
            upper, (chunks, toks)
        )
        out_rows[pl.ds(34 + group, chunks, stride=ROWS_OUT), :] = jnp.broadcast_to(
            line - upper, (chunks, toks)
        )
    send_ref[...] = out_rows[...].astype(jnp.bfloat16)


def run_pack(query_in, key_in, value_in, grad_out):
    chans, toks = query_in.shape
    owners = chans // OWNED
    return pl.pallas_call(
        pack_kernel,
        in_specs=[pl.BlockSpec(memory_space=pltpu.HBM)] * 4,
        out_shape=jax.ShapeDtypeStruct((owners, ROWS_IN, toks), jnp.bfloat16),
        scratch_shapes=[
            pltpu.VMEM((4, chans, toks), jnp.bfloat16),
            pltpu.VMEM((4, chans, toks), jnp.float32),
            pltpu.VMEM((owners * ROWS_IN, toks), jnp.float32),
            pltpu.SemaphoreType.DMA((4,)),
        ],
        compiler_params=pltpu.CompilerParams(vmem_limit_bytes=VMEM_LIMIT),
    )(*[pltpu.with_memory_space_constraint(x, pltpu.HBM) for x in (query_in, key_in, value_in, grad_out)])


def modal_kernel(both_ref, after_ref, out_ref):
    out_ref[...] = both_ref[...]


def run_modal(both, after):
    vmem = pl.BlockSpec(memory_space=pltpu.VMEM)
    return pl.pallas_call(
        modal_kernel,
        in_specs=[vmem, pl.BlockSpec(memory_space=pltpu.HBM)],
        out_specs=vmem,
        out_shape=jax.ShapeDtypeStruct(both.shape, jnp.float32),
        cost_estimate=pl.CostEstimate(flops=2 * 10**10, bytes_accessed=1024, transcendentals=0),
        compiler_params=pltpu.CompilerParams(vmem_limit_bytes=1024 * 1024),
    )(both, pltpu.with_memory_space_constraint(after, pltpu.HBM))


def plane(*shape, dtype=jnp.float32):
    return jax.ShapeDtypeStruct(shape, dtype)


def run_filter(half, recv, taps):
    chunks, _, toks = recv.shape
    lanes = OWNED * chunks
    vmem = pl.BlockSpec(memory_space=pltpu.VMEM)
    return pl.pallas_call(
        filter_kernel,
        in_specs=[pl.BlockSpec(memory_space=pltpu.SMEM), vmem, vmem],
        out_shape=(
            plane(4, PAD + toks, lanes),
            plane(3, toks, lanes),
            plane(5, toks, lanes),
        ),
        scratch_shapes=[pltpu.VMEM((chunks * ROWS_IN, toks), jnp.float32)],
        cost_estimate=pl.CostEstimate(flops=2 * 10**10, bytes_accessed=1024, transcendentals=0),
        compiler_params=pltpu.CompilerParams(vmem_limit_bytes=VMEM_LIMIT),
    )(half, recv, taps)


def run_first(half, modal, log_rate, xt, base):
    _, toks, lanes = base.shape
    f32 = jnp.float32
    vmem = pl.BlockSpec(memory_space=pltpu.VMEM)
    return pl.pallas_call(
        first_kernel,
        in_specs=[pl.BlockSpec(memory_space=pltpu.SMEM)] + [vmem] * 4,
        out_shape=(plane(2, toks, lanes), plane(MESSAGE, toks)),
        scratch_shapes=[
            pltpu.VMEM((2, 8 * toks, lanes // 2), f32),
            pltpu.VMEM((2, 8 * toks, lanes // 2), f32),
            pltpu.VMEM((16 * toks, lanes), f32),
            pltpu.VMEM((TAPS, toks, lanes), jnp.bfloat16),
            pltpu.VMEM((TAPS, toks, lanes), jnp.bfloat16),
            pltpu.VMEM((2, 8 * 24, lanes // 2), f32),
            pltpu.VMEM((COMPACT, lanes), f32),
        ],
        compiler_params=pltpu.CompilerParams(vmem_limit_bytes=VMEM_LIMIT),
    )(half, modal, log_rate, xt, base)


def run_second(half, own, other, taps, modal, xt, hat, conv):
    _, toks, lanes = conv.shape
    chunks = lanes // OWNED
    f32 = jnp.float32
    vmem = pl.BlockSpec(memory_space=pltpu.VMEM)
    return pl.pallas_call(
        second_kernel,
        in_specs=[pl.BlockSpec(memory_space=pltpu.SMEM)] + [vmem] * 7,
        out_shape=(
            plane(chunks * ROWS_OUT, toks, dtype=jnp.bfloat16),
            plane(OWNED, 2 * MODES),
        ),
        scratch_shapes=[
            pltpu.VMEM((COMPACT, lanes), f32),
            pltpu.VMEM((COMPACT, lanes), f32),
            pltpu.VMEM((3, 16, lanes), f32),
            pltpu.VMEM((toks, lanes), f32),
            pltpu.VMEM((24, toks), f32),
            pltpu.VMEM((4, toks, lanes), f32),
            pltpu.VMEM((3, toks + PAD, lanes), f32),
            pltpu.VMEM((chunks * ROWS_OUT, toks), f32),
        ],
        compiler_params=pltpu.CompilerParams(vmem_limit_bytes=VMEM_LIMIT),
    )(half, own, other, taps, modal, xt, hat, conv)


def run_unpack(recv):
    rows, toks = recv.shape
    owners = rows // ROWS_OUT
    chans = OWNED * owners
    whole = jax.ShapeDtypeStruct((chans, toks), jnp.bfloat16)
    return pl.pallas_call(
        unpack_kernel,
        out_specs=(pl.BlockSpec(memory_space=pltpu.HBM),) * 4
        + (pl.BlockSpec(memory_space=pltpu.VMEM),),
        out_shape=(whole,) * 4 + (jax.ShapeDtypeStruct((3, TAPS, chans), jnp.float32),),
        scratch_shapes=[
            pltpu.VMEM((owners * ROWS_OUT, toks), jnp.float32),
            pltpu.VMEM((5, chans, toks), jnp.float32),
            pltpu.VMEM((4, chans, toks), jnp.bfloat16),
            pltpu.SemaphoreType.DMA((4,)),
        ],
        compiler_params=pltpu.CompilerParams(vmem_limit_bytes=VMEM_LIMIT),
    )(recv)


def tap_rows(weights, chunks):
    rows = jnp.concatenate(
        [weights.reshape(3 * TAPS, OWNED), jnp.zeros((3, OWNED), jnp.float32)], axis=0
    )
    return jnp.repeat(rows, chunks, axis=1)


def local(query_in, key_in, value_in, short_weight, residue, log_rate, grad_out):
    devices = lax.axis_size("seq")
    chunks = devices // 2
    chans = query_in.shape[0]
    me = lax.axis_index("seq")
    half = me // chunks
    index = me % chunks
    groups = [list(range(chunks)), list(range(chunks, devices))]
    across = [(i, (i + chunks) % devices) for i in range(devices)]

    send = run_pack(query_in, key_in, value_in, grad_out)
    mine = run_modal(jnp.concatenate([log_rate, residue], axis=1), send)
    theirs = lax.ppermute(mine, "seq", across)
    weights = jnp.concatenate(
        [
            lax.dynamic_slice(short_weight, (0, 0, 4 * index + at), (3, TAPS, 4))
            for at in (0, chans // 2)
        ],
        axis=2,
    )
    taps = tap_rows(weights, chunks)
    which = half.reshape(1).astype(jnp.int32)

    recv = lax.all_to_all(send, "seq", 0, 0, tiled=True, axis_index_groups=groups)
    xt, hat, *inner = run_filter(which, recv, taps)
    theirs, inner = lax.optimization_barrier((theirs, inner))
    modal_params = jnp.where(
        half == 0, jnp.concatenate([mine, theirs]), jnp.concatenate([theirs, mine])
    )
    modal = jnp.repeat(modal_params.T, chunks, axis=1)
    conv, message = run_first(which, modal, modal_params[:, :MODES], xt, *inner)
    other = lax.ppermute(message, "seq", across)
    back, sums = run_second(which, message, other, taps, modal, xt, hat, conv)
    paired = back.reshape(chunks, ROWS_OUT // 4, 4, back.shape[1])
    final = lax.all_to_all(paired, "seq", 0, 0, tiled=True, axis_index_groups=groups)
    output, grad_query, grad_key, grad_value, grad_short = run_unpack(final.reshape(back.shape))
    own_modal = lax.dynamic_slice(sums, (4 * half, 0), (4, 2 * MODES))
    return (
        output,
        grad_query,
        grad_key,
        grad_value,
        grad_short,
        own_modal[:, :MODES],
        own_modal[:, MODES:],
    )


def solution(mesh):
    return jax.shard_map(
        local,
        mesh=mesh,
        in_specs=(
            P("chan", "seq"),
            P("chan", "seq"),
            P("chan", "seq"),
            P(None, None, "chan"),
            P(("chan", "seq"), None),
            P(("chan", "seq"), None),
            P("chan", "seq"),
        ),
        out_specs=(
            P("chan", "seq"),
            P("chan", "seq"),
            P("chan", "seq"),
            P("chan", "seq"),
            P(None, None, "chan"),
            P(("chan", "seq"), None),
            P(("chan", "seq"), None),
        ),
        check_vma=False,
    )
```

```python
import math

import jax
import jax.numpy as jnp
from jax import lax
from jax.experimental import pallas as pl
from jax.experimental.pallas import tpu as pltpu
from jax.sharding import PartitionSpec as P

TAPS = 7
MODES = 16
PAD = 8
OWNED = 8
ROWS_IN = 4 * OWNED
ROWS_OUT = 36
VMEM_LIMIT = 16 * 1024 * 1024

STATE, DERIV, RSUM, KSUM, EDGE, SHORT, COMPACT = 0, 16, 32, 48, 64, 96, 128
MESSAGE = OWNED + 16


def first_row(chan, chans):
    return chan if chan < 4 else chans // 2 + chan - 4


def pack_kernel(query_ref, key_ref, value_ref, grad_ref, send_ref, held, wide, mixed_rows, sems):
    owners = send_ref.shape[0]
    chans = query_ref.shape[0]
    copies = [
        pltpu.make_async_copy(ref, held.at[stream], sems.at[stream])
        for stream, ref in enumerate((query_ref, key_ref, value_ref, grad_ref))
    ]
    for copy in copies:
        copy.start()
    for stream, copy in enumerate(copies):
        copy.wait()
        wide[stream] = held[stream].astype(jnp.float32)
        for chan in range(OWNED):
            mixed_rows[pl.ds(stream * OWNED + chan, owners, stride=ROWS_IN), :] = wide[
                stream, pl.ds(first_row(chan, chans), owners, stride=4), :
            ]
    send_ref[...] = mixed_rows[...].reshape(send_ref.shape).astype(jnp.bfloat16)


def unpack_kernel(recv_ref, out_ref, gq_ref, gk_ref, gv_ref, short_ref, rows, wide):
    owners = recv_ref.shape[0] // ROWS_OUT
    chans = out_ref.shape[0]
    rows[...] = recv_ref[...].astype(jnp.float32)
    for stream, ref in enumerate((out_ref, gq_ref, gk_ref, gv_ref)):
        for chan in range(OWNED):
            wide[stream, pl.ds(first_row(chan, chans), owners, stride=4), :] = rows[
                pl.ds(stream * OWNED + chan, owners, stride=ROWS_OUT), :
            ]
        ref[...] = wide[stream].astype(jnp.bfloat16)
    for group in range(2):
        short = (
            rows[pl.ds(32 + group, owners, stride=ROWS_OUT), :]
            + rows[pl.ds(34 + group, owners, stride=ROWS_OUT), :]
        )
        for chan in range(4):
            wide[4, pl.ds(first_row(4 * group + chan, chans), owners, stride=4), :] = pltpu.roll(
                short, (128 - 32 * chan) % 128, 1
            )
    turned = wide[4].T
    for stream in range(3):
        short_ref[stream] = turned[stream * TAPS : (stream + 1) * TAPS, :]


def lane_ids(chunks, rows):
    lane = lax.broadcasted_iota(jnp.int32, (rows, OWNED * chunks), 1)
    return lane % chunks, lane // chunks


def owner_pick(chunks):
    owner = lane_ids(chunks, OWNED)[1]
    return (owner == lax.broadcasted_iota(jnp.int32, owner.shape, 0)).astype(jnp.float32)


def three_parts(value):
    upper = rounded(value)
    middle = rounded(value - upper)
    return [upper, middle, value - upper - middle]


def lane_sums(value, chunks):
    shape = (value.shape[1], 128)
    owner = lax.broadcasted_iota(jnp.int32, shape, 0) // chunks
    pick = (owner == lax.broadcasted_iota(jnp.int32, shape, 1)).astype(jnp.float32)
    pick = pick.astype(jnp.bfloat16)
    total = None
    for part in reversed(three_parts(value)):
        term = jnp.dot(part.astype(jnp.bfloat16), pick, preferred_element_type=jnp.float32)
        total = term if total is None else total + term
    return total


def lane_spread(value, chunks):
    pick = owner_pick(chunks)
    return lax.dot_general(
        jnp.concatenate(three_parts(value), axis=0).astype(jnp.bfloat16),
        jnp.concatenate([pick] * 3, axis=0).astype(jnp.bfloat16),
        (((0,), (0,)), ((), ())),
        preferred_element_type=jnp.float32,
    )


def one_line(value, first, count, width):
    line = value[first : first + 1, :]
    for chan in range(1, count):
        at = first + chan
        line = line + pltpu.roll(value, width * chan, 1)[at : at + 1, :]
    return line


def modal_rows(modal_ref):
    rates = [jnp.exp(modal_ref[8 * i : 8 * i + 8, :]) for i in range(2)]
    resid = [modal_ref[16 + 8 * i : 24 + 8 * i, :] for i in range(2)]
    decay = [jnp.exp(-r) for r in rates]
    root = [jnp.sqrt(2.0 * r) for r in rates]
    amp = [resid[i] * root[i] for i in range(2)]
    return rates, decay, root, amp


def keep(ref, tok, value):
    lanes = ref.shape[2]
    for half in range(2):
        ref[half, pl.ds(pl.multiple_of(8 * tok, 8), 8), :] = value[
            :, half * lanes : (half + 1) * lanes
        ]


def folded(ref, first, count):
    halves = []
    for half in range(2):
        total = None
        for sub in range(8):
            term = ref[half, pl.ds(first + sub, count, stride=8), :]
            total = term if total is None else total + term
        halves.append(total)
    return jnp.concatenate(halves, axis=1)


def tap_row(taps_ref, stream, tap):
    index = stream * TAPS + tap
    return taps_ref[index : index + 1, :]


def rounded(value):
    return value.astype(jnp.bfloat16).astype(jnp.float32)


def filter_kernel(
    half_ref,
    recv_ref,
    taps_ref,
    xt,
    hat_ref,
    base,
    raw,
):
    mixed, gmixed = base.at[3], base.at[4]
    chunks = recv_ref.shape[0]
    toks = recv_ref.shape[2]
    lanes = OWNED * chunks
    f32 = jnp.float32
    chunk_of, _ = lane_ids(chunks, 8)
    half = half_ref[0]
    late = half.astype(f32)
    block = 32

    raw[...] = recv_ref[...].reshape(raw.shape).astype(f32)
    per_tile = toks // chunks
    for stream in range(4):
        for group in range(OWNED // per_tile):
            tile = jnp.concatenate(
                [
                    raw[
                        pl.ds(stream * OWNED + group * per_tile + c, chunks, stride=ROWS_IN), :
                    ]
                    for c in range(per_tile)
                ],
                axis=0,
            )
            xt[stream, PAD : PAD + toks, group * toks : (group + 1) * toks] = tile.T
    for stream in range(3):
        tail = pltpu.roll(xt[stream, toks : toks + PAD, :], 1, 1)
        xt[stream, 0:PAD, :] = jnp.where(chunk_of >= 1, tail, 0.0)

    fringe = (lax.broadcasted_iota(jnp.int32, (8, lanes), 0) < TAPS - 1) & (chunk_of == 0)
    kept = 1.0 - jnp.where(fringe, late, 0.0)
    for start in range(0, toks, block):
        filtered = []
        for stream in range(3):
            total = None
            for tap in range(TAPS):
                lo = PAD - tap + start
                term = tap_row(taps_ref, stream, tap) * xt[stream, lo : lo + block, :]
                total = term if total is None else total + term
            filtered.append(total)
            hat_ref[stream, start : start + block, :] = total
        grad = xt[3, PAD + start : PAD + start + block, :]
        mixed[start : start + block, :] = rounded(filtered[1] * filtered[2])
        gmixed[start : start + block, :] = rounded(grad * filtered[0])
        base[0, start : start + block, :] = grad
        base[1, start : start + block, :] = filtered[2]
        base[2, start : start + block, :] = filtered[1]
    mixed[0:8, :] = mixed[0:8, :] * kept
    gmixed[0:8, :] = gmixed[0:8, :] * kept
    for stream in range(3):
        base[stream, 0:8, :] = base[stream, 0:8, :] * kept


def first_kernel(
    half_ref,
    modal_ref,
    rate_ref,
    xt,
    base,
    conv_ref,
    msg_ref,
    part_y,
    part_z,
    states,
    upper_w,
    lower_w,
    sums,
    rows,
):
    _, toks, lanes = base.shape
    mixed, gmixed = base.at[3], base.at[4]
    fwd_ref, bwd_ref = conv_ref.at[0], conv_ref.at[1]
    chunks = lanes // OWNED
    f32 = jnp.float32
    chunk_of, _ = lane_ids(chunks, 8)
    half = half_ref[0]
    late = half.astype(f32)
    early = 1.0 - late
    zero = jnp.zeros((8, lanes), f32)
    block = 32

    rates, decay, _, amp = modal_rows(modal_ref)

    def row_of(ref, tok):
        return jnp.broadcast_to(ref[pl.ds(tok, 1), :], (8, lanes))

    def local_body(tok, carry):
        e0, e1, f0, f1 = carry
        xb = row_of(mixed, tok)
        gb = row_of(gmixed, toks - 1 - tok)
        return (
            decay[0] * e0 + xb,
            decay[1] * e1 + xb,
            decay[0] * f0 + gb,
            decay[1] * f1 + gb,
        )

    e0, e1, f0, f1 = lax.fori_loop(0, toks, local_body, (zero,) * 4, unroll=16)
    ends = [e0, e1]
    heads = [f0, f1]
    step = 1
    while step < chunks:
        for i in range(2):
            power = jnp.exp(rates[i] * (-1.0 * toks * step))
            moved = jnp.where(chunk_of >= step, pltpu.roll(ends[i], step, 1), 0.0)
            ends[i] = ends[i] + power * moved
            moved = jnp.where(chunk_of < chunks - step, pltpu.roll(heads[i], lanes - step, 1), 0.0)
            heads[i] = heads[i] + power * moved
        step *= 2
    start_h = [jnp.where(chunk_of >= 1, pltpu.roll(e, 1, 1), 0.0) for e in ends]
    start_p = [jnp.where(chunk_of < chunks - 1, pltpu.roll(f, lanes - 1, 1), 0.0) for f in heads]

    def forward_body(tok, carry):
        h0, h1, r0, r1, d0, d1 = carry
        xb = row_of(mixed, tok)
        gb = row_of(gmixed, tok)
        h0 = decay[0] * h0 + xb
        h1 = decay[1] * h1 + xb
        keep(part_y, tok, amp[0] * h0 + amp[1] * h1)
        states[pl.ds(pl.multiple_of(16 * tok, 8), 8), :] = h0
        states[pl.ds(pl.multiple_of(16 * tok + 8, 8), 8), :] = h1
        return (
            h0,
            h1,
            r0 + gb * h0,
            r1 + gb * h1,
            decay[0] * d0 + h0,
            decay[1] * d1 + h1,
        )

    _, _, r0, r1, d0, d1 = lax.fori_loop(
        0, toks, forward_body, (start_h[0], start_h[1]) + (zero,) * 4, unroll=16
    )

    def backward_body(step_index, carry):
        p0, p1, k0, k1, c0, c1 = carry
        tok = toks - 1 - step_index
        gb = row_of(gmixed, tok)
        q0 = decay[0] * p0
        q1 = decay[1] * p1
        k0 = k0 + states[pl.ds(pl.multiple_of(16 * tok, 8), 8), :] * q0
        k1 = k1 + states[pl.ds(pl.multiple_of(16 * tok + 8, 8), 8), :] * q1
        p0 = q0 + gb
        p1 = q1 + gb
        keep(part_z, tok, amp[0] * p0 + amp[1] * p1)
        return (p0, p1, k0, k1, decay[0] * c0 + p0, decay[1] * c1 + p1)

    _, _, k0, k1, c0, c1 = lax.fori_loop(
        0, toks, backward_body, (start_p[0], start_p[1]) + (zero,) * 4, unroll=16
    )

    for start in range(0, toks, block):
        fwd_ref[start : start + block, :] = folded(part_y, 8 * start, block)
        bwd_ref[start : start + block, :] = folded(part_z, 8 * start, block)

    for stream in range(3):
        tap_sums = [zero for _ in range(TAPS)]
        for start in range(0, toks, block):
            conv = (fwd_ref if stream == 0 else bwd_ref)[start : start + block, :]
            own = conv * base[stream, start : start + block, :]
            for tap in range(TAPS):
                lo = PAD - tap + start
                prod = own * xt[stream, lo : lo + block, :]
                for sub in range(0, block, 8):
                    tap_sums[tap] = tap_sums[tap] + prod[sub : sub + 8, :]
        for tap in range(TAPS):
            keep(sums, stream * TAPS + tap, tap_sums[tap])
    for index in range(3 * TAPS, 24):
        keep(sums, index, zero)
    rows[SHORT : SHORT + 24, :] = folded(sums, 0, 24)
    rows[SHORT + 24 : COMPACT, :] = zero

    bf16 = jnp.bfloat16
    rate_line = jnp.exp(rate_ref[...])
    rate_line = jnp.concatenate([rate_line, jnp.zeros((OWNED, toks - MODES), f32)], axis=1)
    rate_line = one_line(rate_line, 0, OWNED, MODES)
    row_lane = lax.broadcasted_iota(jnp.int32, (lanes, toks), 0)
    col_owner = lax.broadcasted_iota(jnp.int32, (lanes, toks), 1) // MODES
    row_chunk = (row_lane % chunks).astype(f32)
    spread = late * (toks * row_chunk - (TAPS - 2.0)) + early * (
        toks * (chunks - 1.0 - row_chunk) + 1.0
    )
    across = jnp.where(row_lane // chunks == col_owner, jnp.exp(-rate_line * spread), 0.0)
    across_hi = across.astype(bf16)
    across_lo = (across - across_hi.astype(f32)).astype(bf16)
    row_tok = lax.broadcasted_iota(jnp.int32, (toks, toks), 0).astype(f32)
    along = jnp.exp(-rate_line * (late * row_tok + early * (toks - 1.0 - row_tok)))

    def respond(slot, stream):
        for tap in range(TAPS):
            for start in range(0, toks, block):
                span = slice(start, start + block)
                lo = PAD - tap + start
                value = base[stream, span, :] * xt[stream, lo : lo + block, :]
                upper = value.astype(bf16)
                upper_w[tap, span, :] = upper
                lower_w[tap, span, :] = (value - upper.astype(f32)).astype(bf16)
            total = (
                jnp.dot(upper_w[tap], across_lo, preferred_element_type=f32)
                + jnp.dot(lower_w[tap], across_hi, preferred_element_type=f32)
                + jnp.dot(upper_w[tap], across_hi, preferred_element_type=f32)
            )
            at = OWNED + slot + tap
            msg_ref[at : at + 1, :] = jnp.sum(total * along, axis=0, keepdims=True)

    span_c = chunk_of.astype(f32)
    msg_ref[OWNED:MESSAGE, :] = jnp.zeros((MESSAGE - OWNED, toks), f32)

    @pl.when(half == 0)
    def _():
        respond(0, 1)
        respond(TAPS, 2)
        for stream in range(4):
            lo = EDGE + 8 * stream
            rows[lo : lo + 8, :] = jnp.where(
                chunk_of == chunks - 1, xt[stream, toks : toks + PAD, :], 0.0
            )
        for i in range(2):
            weight = jnp.exp(-rates[i] * (toks * (chunks - 1.0 - span_c)))
            rows[STATE + 8 * i : STATE + 8 * i + 8, :] = jnp.where(
                chunk_of == chunks - 1, ends[i], 0.0
            )
            rows[DERIV + 8 * i : DERIV + 8 * i + 8, :] = (d0, d1)[i] * weight

    @pl.when(half != 0)
    def _():
        respond(0, 0)
        for stream in range(4):
            lo = EDGE + 8 * stream
            rows[lo : lo + 8, :] = jnp.where(chunk_of == 0, xt[stream, PAD : 2 * PAD, :], 0.0)
        for i in range(2):
            grow = jnp.exp(rates[i] * (TAPS - 1.0))
            weight = jnp.exp(-rates[i] * (toks * span_c))
            first = jnp.where(chunk_of == 0, heads[i], 0.0)
            rows[STATE + 8 * i : STATE + 8 * i + 8, :] = first * grow
            rows[DERIV + 8 * i : DERIV + 8 * i + 8, :] = (
                (c0, c1)[i] * weight - (TAPS - 1.0) * first
            ) * grow

    for i in range(2):
        rows[RSUM + 8 * i : RSUM + 8 * i + 8, :] = (r0, r1)[i]
        rows[KSUM + 8 * i : KSUM + 8 * i + 8, :] = (k0, k1)[i]
    msg_ref[0:OWNED, :] = lane_sums(rows[...], chunks).T[:OWNED, :]


def second_kernel(
    half_ref,
    own_ref,
    other_ref,
    taps_ref,
    modal_ref,
    xt,
    hat_ref,
    conv_ref,
    send_ref,
    sums_ref,
    edge0,
    edge1,
    edges,
    part,
    driven,
    outs,
    grads,
    out_rows,
):
    _, toks, lanes = conv_ref.shape
    fwd_ref, bwd_ref = conv_ref.at[0], conv_ref.at[1]
    chunks = lanes // OWNED
    f32 = jnp.float32
    chunk_of, _ = lane_ids(chunks, 8)
    scale = 1.0 / math.sqrt(2 * chunks * toks)
    half = half_ref[0]
    late = half.astype(f32)
    early = 1.0 - late
    rates, decay, root, amp = modal_rows(modal_ref)
    fringe = TAPS - 1
    zero = jnp.zeros((8, lanes), f32)

    own = own_ref[...]
    other = other_ref[...]
    message0 = own * early + other * late
    message1 = own * late + other * early
    edge0[...] = lane_spread(message0[0:OWNED, :], chunks)
    edge1[...] = lane_spread(message1[0:OWNED, :], chunks)

    def pair(ref, first):
        return [ref[first + 8 * i : first + 8 * i + 8, :] for i in range(2)]

    row_id = lax.broadcasted_iota(jnp.int32, (8, lanes), 0)
    live = jnp.where(row_id < fringe, 1.0, 0.0)
    hats = []
    for stream in range(3):
        edges[stream, 0:8, :] = edge0[EDGE + 8 * stream : EDGE + 8 * stream + 8, :]
        edges[stream, 8:16, :] = edge1[EDGE + 8 * stream : EDGE + 8 * stream + 8, :]
        total = None
        for tap in range(TAPS):
            term = tap_row(taps_ref, stream, tap) * edges[stream, 8 - tap : 16 - tap, :]
            total = term if total is None else total + term
        hats.append(total)
    grad_edge = edge1[EDGE + 24 : EDGE + 32, :]
    x_edge = rounded(hats[1] * hats[2])
    g_edge = rounded(grad_edge * hats[0])

    state = pair(edge0, STATE)
    passed = []
    y_edge = zero
    for tok in range(fringe):
        xb = jnp.broadcast_to(x_edge[tok : tok + 1, :], (8, lanes))
        state = [decay[i] * state[i] + xb for i in range(2)]
        passed.append(state)
        line = jnp.sum(amp[0] * state[0] + amp[1] * state[1], axis=0, keepdims=True)
        y_edge = jnp.where(row_id == tok, line, y_edge)
    after = state
    back = pair(edge1, STATE)
    r_edge = [zero, zero]
    k_edge = [zero, zero]
    z_edge = zero
    adjoint = back
    for tok in range(fringe - 1, -1, -1):
        gb = jnp.broadcast_to(g_edge[tok : tok + 1, :], (8, lanes))
        moved = [decay[i] * adjoint[i] for i in range(2)]
        k_edge = [k_edge[i] + passed[tok][i] * moved[i] for i in range(2)]
        r_edge = [r_edge[i] + gb * passed[tok][i] for i in range(2)]
        adjoint = [moved[i] + gb for i in range(2)]
        line = jnp.sum(amp[0] * adjoint[0] + amp[1] * adjoint[1], axis=0, keepdims=True)
        z_edge = jnp.where(row_id == tok, line, z_edge)

    span_c = chunk_of.astype(f32)
    carry = []
    for i in range(2):
        into_late = after[i] * jnp.exp(-rates[i] * (toks * span_c - (fringe - 1.0)))
        into_early = adjoint[i] * jnp.exp(-rates[i] * (toks * (chunks - 1.0 - span_c) + 1.0))
        carry.append(amp[i] * (early * into_early + late * into_late))

    sub = row_id.astype(f32)[:, :128]
    sub = late * sub + early * (7.0 - sub)
    stride8 = [jnp.exp(-8.0 * r) for r in rates]
    blocks = toks // 8
    for cut in range(lanes // 128):
        cols = slice(cut * 128, (cut + 1) * 128)
        modes = []
        factors = []
        for i in range(2):
            for m in range(8):
                rate = jnp.broadcast_to(rates[i][m : m + 1, cols], (8, 128))
                lead = jnp.broadcast_to(carry[i][m : m + 1, cols], (8, 128))
                modes.append(lead * jnp.exp(-rate * sub))
                factors.append(jnp.broadcast_to(stride8[i][m : m + 1, cols], (8, 128)))

        def reply_body(step_index, values, cols=cols, factors=factors):
            at = half * step_index + (1 - half) * (blocks - 1 - step_index)
            total = list(values)
            while len(total) > 1:
                total = [total[k] + total[k + 1] for k in range(0, len(total), 2)]
            part[pl.ds(pl.multiple_of(8 * at, 8), 8), cols] = total[0]
            return tuple(v * f for v, f in zip(values, factors))

        lax.fori_loop(0, blocks, reply_body, tuple(modes), unroll=4)

    patch = (row_id < fringe) & (chunk_of == 0) & (jnp.broadcast_to(late, (8, lanes)) > 0.5)
    y_edge = rounded(y_edge)
    z_edge = rounded(z_edge)
    for start, count in ((0, 8), (8, 24), (32, 32), (64, 32), (96, 32)):
        span = slice(start, start + count)
        reply = part[span, :]
        conv = rounded(fwd_ref[span, :] + late * reply)
        turn = rounded(bwd_ref[span, :] + early * reply)
        hat = [hat_ref[stream, span, :] for stream in range(3)]
        if start == 0:
            conv = jnp.where(patch, y_edge, conv)
            turn = jnp.where(patch, z_edge, turn)
            hat = [jnp.where(patch, hats[stream], hat[stream]) for stream in range(3)]
        grads[0, span, :] = xt[3, PAD + start : PAD + start + count, :] * conv
        grads[1, span, :] = turn * hat[2]
        grads[2, span, :] = turn * hat[1]
        outs[0, span, :] = hat[0] * conv
    edge_grads = (grad_edge * y_edge, z_edge * hats[2], z_edge * hats[1])
    for stream in range(3):
        head = pltpu.roll(grads[stream, 0:PAD, :], lanes - 1, 1)
        grads[stream, toks : toks + PAD, :] = jnp.where(
            chunk_of < chunks - 1, head, early * edge_grads[stream]
        )
    block = 32
    for stream in range(3):
        for start in range(0, toks, block):
            total = None
            for tap in range(TAPS):
                term = (
                    tap_row(taps_ref, stream, tap)
                    * grads[stream, start + tap : start + tap + block, :]
                )
                total = term if total is None else total + term
            outs[1 + stream, start : start + block, :] = total

    single = jnp.where(chunk_of == 0, scale, 0.0)
    drives = jnp.concatenate(
        [amp[i] * after[i] * single for i in range(2)]
        + [amp[i] * adjoint[i] * single for i in range(2)]
        + [jnp.zeros((toks - 4 * 8, lanes), f32)],
        axis=0,
    )
    drives = lane_sums(drives, chunks).T[:OWNED, :]
    in_first = lax.broadcasted_iota(jnp.int32, (OWNED, toks), 1) < MODES
    forced = one_line(jnp.where(in_first, drives, 0.0), 0, OWNED, MODES)
    turned = pltpu.roll(drives, toks - MODES, 1)
    turned = one_line(jnp.where(in_first, turned, 0.0), 0, OWNED, MODES)
    driven[0:TAPS, :] = message1[OWNED : OWNED + TAPS, :] * forced
    driven[TAPS : 3 * TAPS, :] = message0[OWNED : OWNED + 2 * TAPS, :] * turned
    driven[3 * TAPS : 24, :] = jnp.zeros((24 - 3 * TAPS, toks), f32)
    short = [
        edge0[SHORT + 8 * i : SHORT + 8 * i + 8, :] + edge1[SHORT + 8 * i : SHORT + 8 * i + 8, :]
        for i in range(3)
    ]
    for stream in range(3):
        live_grad = edge_grads[stream] * live
        for tap in range(TAPS):
            index = stream * TAPS + tap
            term = live_grad * edges[stream, 8 - tap : 16 - tap, :]
            line = jnp.sum(term, axis=0, keepdims=True)
            short[index // 8] = short[index // 8] + jnp.where(row_id == index % 8, line, 0.0)
    r_all = []
    k_all = []
    for i in range(2):
        first_r, late_r = pair(edge0, RSUM)[i], pair(edge1, RSUM)[i]
        first_k, late_k = pair(edge0, KSUM)[i], pair(edge1, KSUM)[i]
        lag_early, lag_late = pair(edge0, DERIV)[i], pair(edge1, DERIV)[i]
        r_all.append(first_r + late_r + decay[i] * back[i] * after[i] + r_edge[i])
        k_all.append(
            first_k
            + late_k
            + decay[i] * lag_early * adjoint[i]
            + decay[i] * after[i] * (lag_late - back[i])
            + k_edge[i]
        )
    columns = jnp.concatenate(
        [value * single for value in short]
        + [root[i] * r_all[i] * single for i in range(2)]
        + [amp[i] * (0.5 * r_all[i] - rates[i] * k_all[i]) * single for i in range(2)],
        axis=0,
    )
    columns = lane_sums(columns, chunks)
    replies = lane_sums(driven[...], MODES)
    columns = jnp.concatenate(
        [columns[0:24, :] + replies, columns[24:56, :], jnp.zeros((128 - 56, 128), f32)], axis=0
    )
    totals = columns.T[:OWNED, :]
    sums_ref[...] = totals[:, 24:56]

    per_tile = toks // chunks
    for stream in range(4):
        for group in range(OWNED // per_tile):
            tile = outs[stream, :, group * toks : (group + 1) * toks].T
            for c in range(per_tile):
                out_rows[
                    pl.ds(stream * OWNED + group * per_tile + c, chunks, stride=ROWS_OUT), :
                ] = tile[c * chunks : (c + 1) * chunks]
    wide = jnp.concatenate([totals[:, 0:24], jnp.zeros((8, toks - 24), f32)], axis=1)
    for group in range(2):
        line = one_line(wide, 4 * group, 4, 32)
        upper = rounded(line)
        out_rows[pl.ds(32 + group, chunks, stride=ROWS_OUT), :] = jnp.broadcast_to(
            upper, (chunks, toks)
        )
        out_rows[pl.ds(34 + group, chunks, stride=ROWS_OUT), :] = jnp.broadcast_to(
            line - upper, (chunks, toks)
        )
    send_ref[...] = out_rows[...].astype(jnp.bfloat16)


def run_pack(query_in, key_in, value_in, grad_out):
    chans, toks = query_in.shape
    owners = chans // OWNED
    return pl.pallas_call(
        pack_kernel,
        in_specs=[pl.BlockSpec(memory_space=pltpu.HBM)] * 4,
        out_shape=jax.ShapeDtypeStruct((owners, ROWS_IN, toks), jnp.bfloat16),
        scratch_shapes=[
            pltpu.VMEM((4, chans, toks), jnp.bfloat16),
            pltpu.VMEM((4, chans, toks), jnp.float32),
            pltpu.VMEM((owners * ROWS_IN, toks), jnp.float32),
            pltpu.SemaphoreType.DMA((4,)),
        ],
        compiler_params=pltpu.CompilerParams(vmem_limit_bytes=VMEM_LIMIT),
    )(*[pltpu.with_memory_space_constraint(x, pltpu.HBM) for x in (query_in, key_in, value_in, grad_out)])


def modal_kernel(both_ref, after_ref, out_ref):
    out_ref[...] = both_ref[...]


def run_modal(both, after):
    vmem = pl.BlockSpec(memory_space=pltpu.VMEM)
    return pl.pallas_call(
        modal_kernel,
        in_specs=[vmem, pl.BlockSpec(memory_space=pltpu.HBM)],
        out_specs=vmem,
        out_shape=jax.ShapeDtypeStruct(both.shape, jnp.float32),
        cost_estimate=pl.CostEstimate(flops=2 * 10**10, bytes_accessed=1024, transcendentals=0),
        compiler_params=pltpu.CompilerParams(vmem_limit_bytes=1024 * 1024),
    )(both, pltpu.with_memory_space_constraint(after, pltpu.HBM))


def plane(*shape, dtype=jnp.float32):
    return jax.ShapeDtypeStruct(shape, dtype)


def run_filter(half, recv, taps):
    chunks, _, toks = recv.shape
    lanes = OWNED * chunks
    vmem = pl.BlockSpec(memory_space=pltpu.VMEM)
    return pl.pallas_call(
        filter_kernel,
        in_specs=[pl.BlockSpec(memory_space=pltpu.SMEM), vmem, vmem],
        out_shape=(
            plane(4, PAD + toks, lanes),
            plane(3, toks, lanes),
            plane(5, toks, lanes),
        ),
        scratch_shapes=[pltpu.VMEM((chunks * ROWS_IN, toks), jnp.float32)],
        cost_estimate=pl.CostEstimate(flops=2 * 10**10, bytes_accessed=1024, transcendentals=0),
        compiler_params=pltpu.CompilerParams(vmem_limit_bytes=VMEM_LIMIT),
    )(half, recv, taps)


def run_first(half, modal, log_rate, xt, base):
    _, toks, lanes = base.shape
    f32 = jnp.float32
    vmem = pl.BlockSpec(memory_space=pltpu.VMEM)
    return pl.pallas_call(
        first_kernel,
        in_specs=[pl.BlockSpec(memory_space=pltpu.SMEM)] + [vmem] * 4,
        out_shape=(plane(2, toks, lanes), plane(MESSAGE, toks)),
        scratch_shapes=[
            pltpu.VMEM((2, 8 * toks, lanes // 2), f32),
            pltpu.VMEM((2, 8 * toks, lanes // 2), f32),
            pltpu.VMEM((16 * toks, lanes), f32),
            pltpu.VMEM((TAPS, toks, lanes), jnp.bfloat16),
            pltpu.VMEM((TAPS, toks, lanes), jnp.bfloat16),
            pltpu.VMEM((2, 8 * 24, lanes // 2), f32),
            pltpu.VMEM((COMPACT, lanes), f32),
        ],
        compiler_params=pltpu.CompilerParams(vmem_limit_bytes=VMEM_LIMIT),
    )(half, modal, log_rate, xt, base)


def run_second(half, own, other, taps, modal, xt, hat, conv):
    _, toks, lanes = conv.shape
    chunks = lanes // OWNED
    f32 = jnp.float32
    vmem = pl.BlockSpec(memory_space=pltpu.VMEM)
    return pl.pallas_call(
        second_kernel,
        in_specs=[pl.BlockSpec(memory_space=pltpu.SMEM)] + [vmem] * 7,
        out_shape=(
            plane(chunks * ROWS_OUT, toks, dtype=jnp.bfloat16),
            plane(OWNED, 2 * MODES),
        ),
        scratch_shapes=[
            pltpu.VMEM((COMPACT, lanes), f32),
            pltpu.VMEM((COMPACT, lanes), f32),
            pltpu.VMEM((3, 16, lanes), f32),
            pltpu.VMEM((toks, lanes), f32),
            pltpu.VMEM((24, toks), f32),
            pltpu.VMEM((4, toks, lanes), f32),
            pltpu.VMEM((3, toks + PAD, lanes), f32),
            pltpu.VMEM((chunks * ROWS_OUT, toks), f32),
        ],
        compiler_params=pltpu.CompilerParams(vmem_limit_bytes=VMEM_LIMIT),
    )(half, own, other, taps, modal, xt, hat, conv)


def run_unpack(recv):
    rows, toks = recv.shape
    owners = rows // ROWS_OUT
    chans = OWNED * owners
    whole = jax.ShapeDtypeStruct((chans, toks), jnp.bfloat16)
    return pl.pallas_call(
        unpack_kernel,
        out_shape=(whole,) * 4 + (jax.ShapeDtypeStruct((3, TAPS, chans), jnp.float32),),
        scratch_shapes=[
            pltpu.VMEM((owners * ROWS_OUT, toks), jnp.float32),
            pltpu.VMEM((5, chans, toks), jnp.float32),
        ],
        compiler_params=pltpu.CompilerParams(vmem_limit_bytes=VMEM_LIMIT),
    )(recv)


def tap_rows(weights, chunks):
    rows = jnp.concatenate(
        [weights.reshape(3 * TAPS, OWNED), jnp.zeros((3, OWNED), jnp.float32)], axis=0
    )
    return jnp.repeat(rows, chunks, axis=1)


def local(query_in, key_in, value_in, short_weight, residue, log_rate, grad_out):
    devices = lax.axis_size("seq")
    chunks = devices // 2
    chans = query_in.shape[0]
    me = lax.axis_index("seq")
    half = me // chunks
    index = me % chunks
    groups = [list(range(chunks)), list(range(chunks, devices))]
    across = [(i, (i + chunks) % devices) for i in range(devices)]

    send = run_pack(query_in, key_in, value_in, grad_out)
    mine = run_modal(jnp.concatenate([log_rate, residue], axis=1), send)
    theirs = lax.ppermute(mine, "seq", across)
    weights = jnp.concatenate(
        [
            lax.dynamic_slice(short_weight, (0, 0, 4 * index + at), (3, TAPS, 4))
            for at in (0, chans // 2)
        ],
        axis=2,
    )
    taps = tap_rows(weights, chunks)
    which = half.reshape(1).astype(jnp.int32)

    recv = lax.all_to_all(send, "seq", 0, 0, tiled=True, axis_index_groups=groups)
    xt, hat, *inner = run_filter(which, recv, taps)
    theirs, inner = lax.optimization_barrier((theirs, inner))
    modal_params = jnp.where(
        half == 0, jnp.concatenate([mine, theirs]), jnp.concatenate([theirs, mine])
    )
    modal = jnp.repeat(modal_params.T, chunks, axis=1)
    conv, message = run_first(which, modal, modal_params[:, :MODES], xt, *inner)
    other = lax.ppermute(message, "seq", across)
    back, sums = run_second(which, message, other, taps, modal, xt, hat, conv)
    paired = back.reshape(chunks, ROWS_OUT // 4, 4, back.shape[1])
    final = lax.all_to_all(paired, "seq", 0, 0, tiled=True, axis_index_groups=groups)
    output, grad_query, grad_key, grad_value, grad_short = run_unpack(final.reshape(back.shape))
    own_modal = lax.dynamic_slice(sums, (4 * half, 0), (4, 2 * MODES))
    return (
        output,
        grad_query,
        grad_key,
        grad_value,
        grad_short,
        own_modal[:, :MODES],
        own_modal[:, MODES:],
    )


def solution(mesh):
    return jax.shard_map(
        local,
        mesh=mesh,
        in_specs=(
            P("chan", "seq"),
            P("chan", "seq"),
            P("chan", "seq"),
            P(None, None, "chan"),
            P(("chan", "seq"), None),
            P(("chan", "seq"), None),
            P("chan", "seq"),
        ),
        out_specs=(
            P("chan", "seq"),
            P("chan", "seq"),
            P("chan", "seq"),
            P("chan", "seq"),
            P(None, None, "chan"),
            P(("chan", "seq"), None),
            P(("chan", "seq"), None),
        ),
        check_vma=False,
    )
```

```python
import math

import jax
import jax.numpy as jnp
from jax import lax
from jax.experimental import pallas as pl
from jax.experimental.pallas import tpu as pltpu
from jax.sharding import PartitionSpec as P

TAPS = 7
MODES = 16
PAD = 8
OWNED = 8
ROWS_IN = 4 * OWNED
ROWS_OUT = 36
VMEM_LIMIT = 16 * 1024 * 1024

STATE, DERIV, RSUM, KSUM, EDGE, SHORT, COMPACT = 0, 16, 32, 48, 64, 96, 128
MESSAGE = OWNED + 16


def first_row(chan, chans):
    return chan if chan < 4 else chans // 2 + chan - 4


def pack_kernel(query_ref, key_ref, value_ref, grad_ref, send_ref, held, wide, mixed_rows, sems):
    owners = send_ref.shape[0]
    chans = query_ref.shape[0]
    copies = [
        pltpu.make_async_copy(ref, held.at[stream], sems.at[stream])
        for stream, ref in enumerate((query_ref, key_ref, value_ref, grad_ref))
    ]
    for copy in copies:
        copy.start()
    for stream, copy in enumerate(copies):
        copy.wait()
        wide[stream] = held[stream].astype(jnp.float32)
        for chan in range(OWNED):
            mixed_rows[pl.ds(stream * OWNED + chan, owners, stride=ROWS_IN), :] = wide[
                stream, pl.ds(first_row(chan, chans), owners, stride=4), :
            ]
    send_ref[...] = mixed_rows[...].reshape(send_ref.shape).astype(jnp.bfloat16)


def unpack_kernel(recv_ref, out_ref, gq_ref, gk_ref, gv_ref, short_ref, rows, wide):
    owners = recv_ref.shape[0] // ROWS_OUT
    chans = out_ref.shape[0]
    rows[...] = recv_ref[...].astype(jnp.float32)
    for stream, ref in enumerate((out_ref, gq_ref, gk_ref, gv_ref)):
        for chan in range(OWNED):
            wide[stream, pl.ds(first_row(chan, chans), owners, stride=4), :] = rows[
                pl.ds(stream * OWNED + chan, owners, stride=ROWS_OUT), :
            ]
        ref[...] = wide[stream].astype(jnp.bfloat16)
    for group in range(2):
        short = (
            rows[pl.ds(32 + group, owners, stride=ROWS_OUT), :]
            + rows[pl.ds(34 + group, owners, stride=ROWS_OUT), :]
        )
        for chan in range(4):
            wide[4, pl.ds(first_row(4 * group + chan, chans), owners, stride=4), :] = pltpu.roll(
                short, (128 - 32 * chan) % 128, 1
            )
    turned = wide[4].T
    for stream in range(3):
        short_ref[stream] = turned[stream * TAPS : (stream + 1) * TAPS, :]


def lane_ids(chunks, rows):
    lane = lax.broadcasted_iota(jnp.int32, (rows, OWNED * chunks), 1)
    return lane % chunks, lane // chunks


def owner_pick(chunks):
    owner = lane_ids(chunks, OWNED)[1]
    return (owner == lax.broadcasted_iota(jnp.int32, owner.shape, 0)).astype(jnp.float32)


def three_parts(value):
    upper = rounded(value)
    middle = rounded(value - upper)
    return [upper, middle, value - upper - middle]


def lane_sums(value, chunks):
    shape = (value.shape[1], 128)
    owner = lax.broadcasted_iota(jnp.int32, shape, 0) // chunks
    pick = (owner == lax.broadcasted_iota(jnp.int32, shape, 1)).astype(jnp.float32)
    pick = pick.astype(jnp.bfloat16)
    total = None
    for part in reversed(three_parts(value)):
        term = jnp.dot(part.astype(jnp.bfloat16), pick, preferred_element_type=jnp.float32)
        total = term if total is None else total + term
    return total


def lane_spread(value, chunks):
    pick = owner_pick(chunks)
    return lax.dot_general(
        jnp.concatenate(three_parts(value), axis=0).astype(jnp.bfloat16),
        jnp.concatenate([pick] * 3, axis=0).astype(jnp.bfloat16),
        (((0,), (0,)), ((), ())),
        preferred_element_type=jnp.float32,
    )


def one_line(value, first, count, width):
    line = value[first : first + 1, :]
    for chan in range(1, count):
        at = first + chan
        line = line + pltpu.roll(value, width * chan, 1)[at : at + 1, :]
    return line


def modal_rows(modal_ref):
    rates = [jnp.exp(modal_ref[8 * i : 8 * i + 8, :]) for i in range(2)]
    resid = [modal_ref[16 + 8 * i : 24 + 8 * i, :] for i in range(2)]
    decay = [jnp.exp(-r) for r in rates]
    root = [jnp.sqrt(2.0 * r) for r in rates]
    amp = [resid[i] * root[i] for i in range(2)]
    return rates, decay, root, amp


def keep(ref, tok, value):
    lanes = ref.shape[2]
    for half in range(2):
        ref[half, pl.ds(pl.multiple_of(8 * tok, 8), 8), :] = value[
            :, half * lanes : (half + 1) * lanes
        ]


def folded(ref, first, count):
    halves = []
    for half in range(2):
        total = None
        for sub in range(8):
            term = ref[half, pl.ds(first + sub, count, stride=8), :]
            total = term if total is None else total + term
        halves.append(total)
    return jnp.concatenate(halves, axis=1)


def tap_row(taps_ref, stream, tap):
    index = stream * TAPS + tap
    return taps_ref[index : index + 1, :]


def rounded(value):
    return value.astype(jnp.bfloat16).astype(jnp.float32)


def filter_kernel(
    half_ref,
    recv_ref,
    taps_ref,
    xt,
    hat_ref,
    base,
    raw,
):
    mixed, gmixed = base.at[3], base.at[4]
    chunks = recv_ref.shape[0]
    toks = recv_ref.shape[2]
    lanes = OWNED * chunks
    f32 = jnp.float32
    chunk_of, _ = lane_ids(chunks, 8)
    half = half_ref[0]
    late = half.astype(f32)
    block = 32

    raw[...] = recv_ref[...].reshape(raw.shape).astype(f32)
    per_tile = toks // chunks
    for stream in range(4):
        for group in range(OWNED // per_tile):
            tile = jnp.concatenate(
                [
                    raw[
                        pl.ds(stream * OWNED + group * per_tile + c, chunks, stride=ROWS_IN), :
                    ]
                    for c in range(per_tile)
                ],
                axis=0,
            )
            xt[stream, PAD : PAD + toks, group * toks : (group + 1) * toks] = tile.T
    for stream in range(3):
        tail = pltpu.roll(xt[stream, toks : toks + PAD, :], 1, 1)
        xt[stream, 0:PAD, :] = jnp.where(chunk_of >= 1, tail, 0.0)

    fringe = (lax.broadcasted_iota(jnp.int32, (8, lanes), 0) < TAPS - 1) & (chunk_of == 0)
    kept = 1.0 - jnp.where(fringe, late, 0.0)
    for start in range(0, toks, block):
        filtered = []
        for stream in range(3):
            total = None
            for tap in range(TAPS):
                lo = PAD - tap + start
                term = tap_row(taps_ref, stream, tap) * xt[stream, lo : lo + block, :]
                total = term if total is None else total + term
            filtered.append(total)
            hat_ref[stream, start : start + block, :] = total
        grad = xt[3, PAD + start : PAD + start + block, :]
        mixed[start : start + block, :] = rounded(filtered[1] * filtered[2])
        gmixed[start : start + block, :] = rounded(grad * filtered[0])
        base[0, start : start + block, :] = grad
        base[1, start : start + block, :] = filtered[2]
        base[2, start : start + block, :] = filtered[1]
    mixed[0:8, :] = mixed[0:8, :] * kept
    gmixed[0:8, :] = gmixed[0:8, :] * kept
    for stream in range(3):
        base[stream, 0:8, :] = base[stream, 0:8, :] * kept


def first_kernel(
    half_ref,
    modal_ref,
    rate_ref,
    xt,
    base,
    conv_ref,
    msg_ref,
    part_y,
    part_z,
    states,
    upper_w,
    lower_w,
    sums,
    rows,
):
    _, toks, lanes = base.shape
    mixed, gmixed = base.at[3], base.at[4]
    fwd_ref, bwd_ref = conv_ref.at[0], conv_ref.at[1]
    chunks = lanes // OWNED
    f32 = jnp.float32
    chunk_of, _ = lane_ids(chunks, 8)
    half = half_ref[0]
    late = half.astype(f32)
    early = 1.0 - late
    zero = jnp.zeros((8, lanes), f32)
    block = 32

    rates, decay, _, amp = modal_rows(modal_ref)

    def row_of(ref, tok):
        return jnp.broadcast_to(ref[pl.ds(tok, 1), :], (8, lanes))

    def local_body(tok, carry):
        e0, e1, f0, f1 = carry
        xb = row_of(mixed, tok)
        gb = row_of(gmixed, toks - 1 - tok)
        return (
            decay[0] * e0 + xb,
            decay[1] * e1 + xb,
            decay[0] * f0 + gb,
            decay[1] * f1 + gb,
        )

    e0, e1, f0, f1 = lax.fori_loop(0, toks, local_body, (zero,) * 4, unroll=16)
    ends = [e0, e1]
    heads = [f0, f1]
    step = 1
    while step < chunks:
        for i in range(2):
            power = jnp.exp(rates[i] * (-1.0 * toks * step))
            moved = jnp.where(chunk_of >= step, pltpu.roll(ends[i], step, 1), 0.0)
            ends[i] = ends[i] + power * moved
            moved = jnp.where(chunk_of < chunks - step, pltpu.roll(heads[i], lanes - step, 1), 0.0)
            heads[i] = heads[i] + power * moved
        step *= 2
    start_h = [jnp.where(chunk_of >= 1, pltpu.roll(e, 1, 1), 0.0) for e in ends]
    start_p = [jnp.where(chunk_of < chunks - 1, pltpu.roll(f, lanes - 1, 1), 0.0) for f in heads]

    def forward_body(tok, carry):
        h0, h1, r0, r1, d0, d1 = carry
        xb = row_of(mixed, tok)
        gb = row_of(gmixed, tok)
        h0 = decay[0] * h0 + xb
        h1 = decay[1] * h1 + xb
        keep(part_y, tok, amp[0] * h0 + amp[1] * h1)
        states[pl.ds(pl.multiple_of(16 * tok, 8), 8), :] = h0
        states[pl.ds(pl.multiple_of(16 * tok + 8, 8), 8), :] = h1
        return (
            h0,
            h1,
            r0 + gb * h0,
            r1 + gb * h1,
            decay[0] * d0 + h0,
            decay[1] * d1 + h1,
        )

    def forward(lagged):
        def body(tok, carry):
            out = forward_body(tok, carry)
            return out if lagged else out[:4] + carry[4:]

        first = (start_h[0], start_h[1]) + (zero,) * 4
        return lax.fori_loop(0, toks, body, first, unroll=16)[2:]

    r0, r1, d0, d1 = lax.cond(half == 0, lambda: forward(True), lambda: forward(False))

    def backward_body(step_index, carry):
        p0, p1, k0, k1, c0, c1 = carry
        tok = toks - 1 - step_index
        gb = row_of(gmixed, tok)
        q0 = decay[0] * p0
        q1 = decay[1] * p1
        k0 = k0 + states[pl.ds(pl.multiple_of(16 * tok, 8), 8), :] * q0
        k1 = k1 + states[pl.ds(pl.multiple_of(16 * tok + 8, 8), 8), :] * q1
        p0 = q0 + gb
        p1 = q1 + gb
        keep(part_z, tok, amp[0] * p0 + amp[1] * p1)
        return (p0, p1, k0, k1, decay[0] * c0 + p0, decay[1] * c1 + p1)

    _, _, k0, k1, c0, c1 = lax.fori_loop(
        0, toks, backward_body, (start_p[0], start_p[1]) + (zero,) * 4, unroll=16
    )

    for start in range(0, toks, block):
        fwd_ref[start : start + block, :] = folded(part_y, 8 * start, block)
        bwd_ref[start : start + block, :] = folded(part_z, 8 * start, block)

    for stream in range(3):
        tap_sums = [zero for _ in range(TAPS)]
        for start in range(0, toks, block):
            conv = (fwd_ref if stream == 0 else bwd_ref)[start : start + block, :]
            own = conv * base[stream, start : start + block, :]
            for tap in range(TAPS):
                lo = PAD - tap + start
                prod = own * xt[stream, lo : lo + block, :]
                for sub in range(0, block, 8):
                    tap_sums[tap] = tap_sums[tap] + prod[sub : sub + 8, :]
        for tap in range(TAPS):
            keep(sums, stream * TAPS + tap, tap_sums[tap])
    for index in range(3 * TAPS, 24):
        keep(sums, index, zero)
    rows[SHORT : SHORT + 24, :] = folded(sums, 0, 24)
    rows[SHORT + 24 : COMPACT, :] = zero

    bf16 = jnp.bfloat16
    rate_line = jnp.exp(rate_ref[...])
    rate_line = jnp.concatenate([rate_line, jnp.zeros((OWNED, toks - MODES), f32)], axis=1)
    rate_line = one_line(rate_line, 0, OWNED, MODES)
    row_lane = lax.broadcasted_iota(jnp.int32, (lanes, toks), 0)
    col_owner = lax.broadcasted_iota(jnp.int32, (lanes, toks), 1) // MODES
    row_chunk = (row_lane % chunks).astype(f32)
    spread = late * (toks * row_chunk - (TAPS - 2.0)) + early * (
        toks * (chunks - 1.0 - row_chunk) + 1.0
    )
    across = jnp.where(row_lane // chunks == col_owner, jnp.exp(-rate_line * spread), 0.0)
    across_hi = across.astype(bf16)
    across_lo = (across - across_hi.astype(f32)).astype(bf16)
    row_tok = lax.broadcasted_iota(jnp.int32, (toks, toks), 0).astype(f32)
    along = jnp.exp(-rate_line * (late * row_tok + early * (toks - 1.0 - row_tok)))

    def respond(slot, stream):
        for tap in range(TAPS):
            for start in range(0, toks, block):
                span = slice(start, start + block)
                lo = PAD - tap + start
                value = base[stream, span, :] * xt[stream, lo : lo + block, :]
                upper = value.astype(bf16)
                upper_w[tap, span, :] = upper
                lower_w[tap, span, :] = (value - upper.astype(f32)).astype(bf16)
            total = (
                jnp.dot(upper_w[tap], across_lo, preferred_element_type=f32)
                + jnp.dot(lower_w[tap], across_hi, preferred_element_type=f32)
                + jnp.dot(upper_w[tap], across_hi, preferred_element_type=f32)
            )
            at = OWNED + slot + tap
            msg_ref[at : at + 1, :] = jnp.sum(total * along, axis=0, keepdims=True)

    span_c = chunk_of.astype(f32)
    msg_ref[OWNED:MESSAGE, :] = jnp.zeros((MESSAGE - OWNED, toks), f32)

    @pl.when(half == 0)
    def _():
        respond(0, 1)
        respond(TAPS, 2)
        for stream in range(4):
            lo = EDGE + 8 * stream
            rows[lo : lo + 8, :] = jnp.where(
                chunk_of == chunks - 1, xt[stream, toks : toks + PAD, :], 0.0
            )
        for i in range(2):
            weight = jnp.exp(-rates[i] * (toks * (chunks - 1.0 - span_c)))
            rows[STATE + 8 * i : STATE + 8 * i + 8, :] = jnp.where(
                chunk_of == chunks - 1, ends[i], 0.0
            )
            rows[DERIV + 8 * i : DERIV + 8 * i + 8, :] = (d0, d1)[i] * weight

    @pl.when(half != 0)
    def _():
        respond(0, 0)
        for stream in range(4):
            lo = EDGE + 8 * stream
            rows[lo : lo + 8, :] = jnp.where(chunk_of == 0, xt[stream, PAD : 2 * PAD, :], 0.0)
        for i in range(2):
            grow = jnp.exp(rates[i] * (TAPS - 1.0))
            weight = jnp.exp(-rates[i] * (toks * span_c))
            first = jnp.where(chunk_of == 0, heads[i], 0.0)
            rows[STATE + 8 * i : STATE + 8 * i + 8, :] = first * grow
            rows[DERIV + 8 * i : DERIV + 8 * i + 8, :] = (
                (c0, c1)[i] * weight - (TAPS - 1.0) * first
            ) * grow

    for i in range(2):
        rows[RSUM + 8 * i : RSUM + 8 * i + 8, :] = (r0, r1)[i]
        rows[KSUM + 8 * i : KSUM + 8 * i + 8, :] = (k0, k1)[i]
    msg_ref[0:OWNED, :] = lane_sums(rows[...], chunks).T[:OWNED, :]


def second_kernel(
    half_ref,
    own_ref,
    other_ref,
    taps_ref,
    modal_ref,
    xt,
    hat_ref,
    conv_ref,
    send_ref,
    sums_ref,
    edge0,
    edge1,
    edges,
    part,
    driven,
    outs,
    grads,
    out_rows,
):
    _, toks, lanes = conv_ref.shape
    fwd_ref, bwd_ref = conv_ref.at[0], conv_ref.at[1]
    chunks = lanes // OWNED
    f32 = jnp.float32
    chunk_of, _ = lane_ids(chunks, 8)
    scale = 1.0 / math.sqrt(2 * chunks * toks)
    half = half_ref[0]
    late = half.astype(f32)
    early = 1.0 - late
    rates, decay, root, amp = modal_rows(modal_ref)
    fringe = TAPS - 1
    zero = jnp.zeros((8, lanes), f32)

    own = own_ref[...]
    other = other_ref[...]
    message0 = own * early + other * late
    message1 = own * late + other * early
    edge0[...] = lane_spread(message0[0:OWNED, :], chunks)
    edge1[...] = lane_spread(message1[0:OWNED, :], chunks)

    def pair(ref, first):
        return [ref[first + 8 * i : first + 8 * i + 8, :] for i in range(2)]

    row_id = lax.broadcasted_iota(jnp.int32, (8, lanes), 0)
    live = jnp.where(row_id < fringe, 1.0, 0.0)
    hats = []
    for stream in range(3):
        edges[stream, 0:8, :] = edge0[EDGE + 8 * stream : EDGE + 8 * stream + 8, :]
        edges[stream, 8:16, :] = edge1[EDGE + 8 * stream : EDGE + 8 * stream + 8, :]
        total = None
        for tap in range(TAPS):
            term = tap_row(taps_ref, stream, tap) * edges[stream, 8 - tap : 16 - tap, :]
            total = term if total is None else total + term
        hats.append(total)
    grad_edge = edge1[EDGE + 24 : EDGE + 32, :]
    x_edge = rounded(hats[1] * hats[2])
    g_edge = rounded(grad_edge * hats[0])

    state = pair(edge0, STATE)
    passed = []
    y_edge = zero
    for tok in range(fringe):
        xb = jnp.broadcast_to(x_edge[tok : tok + 1, :], (8, lanes))
        state = [decay[i] * state[i] + xb for i in range(2)]
        passed.append(state)
        line = jnp.sum(amp[0] * state[0] + amp[1] * state[1], axis=0, keepdims=True)
        y_edge = jnp.where(row_id == tok, line, y_edge)
    after = state
    back = pair(edge1, STATE)
    r_edge = [zero, zero]
    k_edge = [zero, zero]
    z_edge = zero
    adjoint = back
    for tok in range(fringe - 1, -1, -1):
        gb = jnp.broadcast_to(g_edge[tok : tok + 1, :], (8, lanes))
        moved = [decay[i] * adjoint[i] for i in range(2)]
        k_edge = [k_edge[i] + passed[tok][i] * moved[i] for i in range(2)]
        r_edge = [r_edge[i] + gb * passed[tok][i] for i in range(2)]
        adjoint = [moved[i] + gb for i in range(2)]
        line = jnp.sum(amp[0] * adjoint[0] + amp[1] * adjoint[1], axis=0, keepdims=True)
        z_edge = jnp.where(row_id == tok, line, z_edge)

    span_c = chunk_of.astype(f32)
    carry = []
    for i in range(2):
        into_late = after[i] * jnp.exp(-rates[i] * (toks * span_c - (fringe - 1.0)))
        into_early = adjoint[i] * jnp.exp(-rates[i] * (toks * (chunks - 1.0 - span_c) + 1.0))
        carry.append(amp[i] * (early * into_early + late * into_late))

    sub = row_id.astype(f32)[:, :128]
    sub = late * sub + early * (7.0 - sub)
    stride8 = [jnp.exp(-8.0 * r) for r in rates]
    blocks = toks // 8
    for cut in range(lanes // 128):
        cols = slice(cut * 128, (cut + 1) * 128)
        modes = []
        factors = []
        for i in range(2):
            for m in range(8):
                rate = jnp.broadcast_to(rates[i][m : m + 1, cols], (8, 128))
                lead = jnp.broadcast_to(carry[i][m : m + 1, cols], (8, 128))
                modes.append(lead * jnp.exp(-rate * sub))
                factors.append(jnp.broadcast_to(stride8[i][m : m + 1, cols], (8, 128)))

        def reply_body(step_index, values, cols=cols, factors=factors):
            at = half * step_index + (1 - half) * (blocks - 1 - step_index)
            total = list(values)
            while len(total) > 1:
                total = [total[k] + total[k + 1] for k in range(0, len(total), 2)]
            part[pl.ds(pl.multiple_of(8 * at, 8), 8), cols] = total[0]
            return tuple(v * f for v, f in zip(values, factors))

        lax.fori_loop(0, blocks, reply_body, tuple(modes), unroll=4)

    patch = (row_id < fringe) & (chunk_of == 0) & (jnp.broadcast_to(late, (8, lanes)) > 0.5)
    y_edge = rounded(y_edge)
    z_edge = rounded(z_edge)
    for start, count in ((0, 8), (8, 24), (32, 32), (64, 32), (96, 32)):
        span = slice(start, start + count)
        reply = part[span, :]
        conv = rounded(fwd_ref[span, :] + late * reply)
        turn = rounded(bwd_ref[span, :] + early * reply)
        hat = [hat_ref[stream, span, :] for stream in range(3)]
        if start == 0:
            conv = jnp.where(patch, y_edge, conv)
            turn = jnp.where(patch, z_edge, turn)
            hat = [jnp.where(patch, hats[stream], hat[stream]) for stream in range(3)]
        grads[0, span, :] = xt[3, PAD + start : PAD + start + count, :] * conv
        grads[1, span, :] = turn * hat[2]
        grads[2, span, :] = turn * hat[1]
        outs[0, span, :] = hat[0] * conv
    edge_grads = (grad_edge * y_edge, z_edge * hats[2], z_edge * hats[1])
    for stream in range(3):
        head = pltpu.roll(grads[stream, 0:PAD, :], lanes - 1, 1)
        grads[stream, toks : toks + PAD, :] = jnp.where(
            chunk_of < chunks - 1, head, early * edge_grads[stream]
        )
    block = 32
    for stream in range(3):
        for start in range(0, toks, block):
            total = None
            for tap in range(TAPS):
                term = (
                    tap_row(taps_ref, stream, tap)
                    * grads[stream, start + tap : start + tap + block, :]
                )
                total = term if total is None else total + term
            outs[1 + stream, start : start + block, :] = total

    single = jnp.where(chunk_of == 0, scale, 0.0)
    drives = jnp.concatenate(
        [amp[i] * after[i] * single for i in range(2)]
        + [amp[i] * adjoint[i] * single for i in range(2)]
        + [jnp.zeros((toks - 4 * 8, lanes), f32)],
        axis=0,
    )
    drives = lane_sums(drives, chunks).T[:OWNED, :]
    in_first = lax.broadcasted_iota(jnp.int32, (OWNED, toks), 1) < MODES
    forced = one_line(jnp.where(in_first, drives, 0.0), 0, OWNED, MODES)
    turned = pltpu.roll(drives, toks - MODES, 1)
    turned = one_line(jnp.where(in_first, turned, 0.0), 0, OWNED, MODES)
    driven[0:TAPS, :] = message1[OWNED : OWNED + TAPS, :] * forced
    driven[TAPS : 3 * TAPS, :] = message0[OWNED : OWNED + 2 * TAPS, :] * turned
    driven[3 * TAPS : 24, :] = jnp.zeros((24 - 3 * TAPS, toks), f32)
    short = [
        edge0[SHORT + 8 * i : SHORT + 8 * i + 8, :] + edge1[SHORT + 8 * i : SHORT + 8 * i + 8, :]
        for i in range(3)
    ]
    for stream in range(3):
        live_grad = edge_grads[stream] * live
        for tap in range(TAPS):
            index = stream * TAPS + tap
            term = live_grad * edges[stream, 8 - tap : 16 - tap, :]
            line = jnp.sum(term, axis=0, keepdims=True)
            short[index // 8] = short[index // 8] + jnp.where(row_id == index % 8, line, 0.0)
    r_all = []
    k_all = []
    for i in range(2):
        first_r, late_r = pair(edge0, RSUM)[i], pair(edge1, RSUM)[i]
        first_k, late_k = pair(edge0, KSUM)[i], pair(edge1, KSUM)[i]
        lag_early, lag_late = pair(edge0, DERIV)[i], pair(edge1, DERIV)[i]
        r_all.append(first_r + late_r + decay[i] * back[i] * after[i] + r_edge[i])
        k_all.append(
            first_k
            + late_k
            + decay[i] * lag_early * adjoint[i]
            + decay[i] * after[i] * (lag_late - back[i])
            + k_edge[i]
        )
    columns = jnp.concatenate(
        [value * single for value in short]
        + [root[i] * r_all[i] * single for i in range(2)]
        + [amp[i] * (0.5 * r_all[i] - rates[i] * k_all[i]) * single for i in range(2)],
        axis=0,
    )
    columns = lane_sums(columns, chunks)
    replies = lane_sums(driven[...], MODES)
    columns = jnp.concatenate(
        [columns[0:24, :] + replies, columns[24:56, :], jnp.zeros((128 - 56, 128), f32)], axis=0
    )
    totals = columns.T[:OWNED, :]
    sums_ref[...] = totals[:, 24:56]

    per_tile = toks // chunks
    for stream in range(4):
        for group in range(OWNED // per_tile):
            tile = outs[stream, :, group * toks : (group + 1) * toks].T
            for c in range(per_tile):
                out_rows[
                    pl.ds(stream * OWNED + group * per_tile + c, chunks, stride=ROWS_OUT), :
                ] = tile[c * chunks : (c + 1) * chunks]
    wide = jnp.concatenate([totals[:, 0:24], jnp.zeros((8, toks - 24), f32)], axis=1)
    for group in range(2):
        line = one_line(wide, 4 * group, 4, 32)
        upper = rounded(line)
        out_rows[pl.ds(32 + group, chunks, stride=ROWS_OUT), :] = jnp.broadcast_to(
            upper, (chunks, toks)
        )
        out_rows[pl.ds(34 + group, chunks, stride=ROWS_OUT), :] = jnp.broadcast_to(
            line - upper, (chunks, toks)
        )
    send_ref[...] = out_rows[...].astype(jnp.bfloat16)


def run_pack(query_in, key_in, value_in, grad_out):
    chans, toks = query_in.shape
    owners = chans // OWNED
    return pl.pallas_call(
        pack_kernel,
        in_specs=[pl.BlockSpec(memory_space=pltpu.HBM)] * 4,
        out_shape=jax.ShapeDtypeStruct((owners, ROWS_IN, toks), jnp.bfloat16),
        scratch_shapes=[
            pltpu.VMEM((4, chans, toks), jnp.bfloat16),
            pltpu.VMEM((4, chans, toks), jnp.float32),
            pltpu.VMEM((owners * ROWS_IN, toks), jnp.float32),
            pltpu.SemaphoreType.DMA((4,)),
        ],
        compiler_params=pltpu.CompilerParams(vmem_limit_bytes=VMEM_LIMIT),
    )(*[pltpu.with_memory_space_constraint(x, pltpu.HBM) for x in (query_in, key_in, value_in, grad_out)])


def modal_kernel(both_ref, after_ref, out_ref):
    out_ref[...] = both_ref[...]


def run_modal(both, after):
    vmem = pl.BlockSpec(memory_space=pltpu.VMEM)
    return pl.pallas_call(
        modal_kernel,
        in_specs=[vmem, pl.BlockSpec(memory_space=pltpu.HBM)],
        out_specs=vmem,
        out_shape=jax.ShapeDtypeStruct(both.shape, jnp.float32),
        cost_estimate=pl.CostEstimate(flops=2 * 10**10, bytes_accessed=1024, transcendentals=0),
        compiler_params=pltpu.CompilerParams(vmem_limit_bytes=1024 * 1024),
    )(both, pltpu.with_memory_space_constraint(after, pltpu.HBM))


def plane(*shape, dtype=jnp.float32):
    return jax.ShapeDtypeStruct(shape, dtype)


def run_filter(half, recv, taps):
    chunks, _, toks = recv.shape
    lanes = OWNED * chunks
    vmem = pl.BlockSpec(memory_space=pltpu.VMEM)
    return pl.pallas_call(
        filter_kernel,
        in_specs=[pl.BlockSpec(memory_space=pltpu.SMEM), vmem, vmem],
        out_shape=(
            plane(4, PAD + toks, lanes),
            plane(3, toks, lanes),
            plane(5, toks, lanes),
        ),
        scratch_shapes=[pltpu.VMEM((chunks * ROWS_IN, toks), jnp.float32)],
        cost_estimate=pl.CostEstimate(flops=2 * 10**10, bytes_accessed=1024, transcendentals=0),
        compiler_params=pltpu.CompilerParams(vmem_limit_bytes=VMEM_LIMIT),
    )(half, recv, taps)


def run_first(half, modal, log_rate, xt, base):
    _, toks, lanes = base.shape
    f32 = jnp.float32
    vmem = pl.BlockSpec(memory_space=pltpu.VMEM)
    return pl.pallas_call(
        first_kernel,
        in_specs=[pl.BlockSpec(memory_space=pltpu.SMEM)] + [vmem] * 4,
        out_shape=(plane(2, toks, lanes), plane(MESSAGE, toks)),
        scratch_shapes=[
            pltpu.VMEM((2, 8 * toks, lanes // 2), f32),
            pltpu.VMEM((2, 8 * toks, lanes // 2), f32),
            pltpu.VMEM((16 * toks, lanes), f32),
            pltpu.VMEM((TAPS, toks, lanes), jnp.bfloat16),
            pltpu.VMEM((TAPS, toks, lanes), jnp.bfloat16),
            pltpu.VMEM((2, 8 * 24, lanes // 2), f32),
            pltpu.VMEM((COMPACT, lanes), f32),
        ],
        compiler_params=pltpu.CompilerParams(vmem_limit_bytes=VMEM_LIMIT),
    )(half, modal, log_rate, xt, base)


def run_second(half, own, other, taps, modal, xt, hat, conv):
    _, toks, lanes = conv.shape
    chunks = lanes // OWNED
    f32 = jnp.float32
    vmem = pl.BlockSpec(memory_space=pltpu.VMEM)
    return pl.pallas_call(
        second_kernel,
        in_specs=[pl.BlockSpec(memory_space=pltpu.SMEM)] + [vmem] * 7,
        out_shape=(
            plane(chunks * ROWS_OUT, toks, dtype=jnp.bfloat16),
            plane(OWNED, 2 * MODES),
        ),
        scratch_shapes=[
            pltpu.VMEM((COMPACT, lanes), f32),
            pltpu.VMEM((COMPACT, lanes), f32),
            pltpu.VMEM((3, 16, lanes), f32),
            pltpu.VMEM((toks, lanes), f32),
            pltpu.VMEM((24, toks), f32),
            pltpu.VMEM((4, toks, lanes), f32),
            pltpu.VMEM((3, toks + PAD, lanes), f32),
            pltpu.VMEM((chunks * ROWS_OUT, toks), f32),
        ],
        compiler_params=pltpu.CompilerParams(vmem_limit_bytes=VMEM_LIMIT),
    )(half, own, other, taps, modal, xt, hat, conv)


def run_unpack(recv):
    rows, toks = recv.shape
    owners = rows // ROWS_OUT
    chans = OWNED * owners
    whole = jax.ShapeDtypeStruct((chans, toks), jnp.bfloat16)
    return pl.pallas_call(
        unpack_kernel,
        out_shape=(whole,) * 4 + (jax.ShapeDtypeStruct((3, TAPS, chans), jnp.float32),),
        scratch_shapes=[
            pltpu.VMEM((owners * ROWS_OUT, toks), jnp.float32),
            pltpu.VMEM((5, chans, toks), jnp.float32),
        ],
        compiler_params=pltpu.CompilerParams(vmem_limit_bytes=VMEM_LIMIT),
    )(recv)


def tap_rows(weights, chunks):
    rows = jnp.concatenate(
        [weights.reshape(3 * TAPS, OWNED), jnp.zeros((3, OWNED), jnp.float32)], axis=0
    )
    return jnp.repeat(rows, chunks, axis=1)


def local(query_in, key_in, value_in, short_weight, residue, log_rate, grad_out):
    devices = lax.axis_size("seq")
    chunks = devices // 2
    chans = query_in.shape[0]
    me = lax.axis_index("seq")
    half = me // chunks
    index = me % chunks
    groups = [list(range(chunks)), list(range(chunks, devices))]
    across = [(i, (i + chunks) % devices) for i in range(devices)]

    send = run_pack(query_in, key_in, value_in, grad_out)
    mine = run_modal(jnp.concatenate([log_rate, residue], axis=1), send)
    theirs = lax.ppermute(mine, "seq", across)
    weights = jnp.concatenate(
        [
            lax.dynamic_slice(short_weight, (0, 0, 4 * index + at), (3, TAPS, 4))
            for at in (0, chans // 2)
        ],
        axis=2,
    )
    taps = tap_rows(weights, chunks)
    which = half.reshape(1).astype(jnp.int32)

    recv = lax.all_to_all(send, "seq", 0, 0, tiled=True, axis_index_groups=groups)
    xt, hat, *inner = run_filter(which, recv, taps)
    theirs, inner = lax.optimization_barrier((theirs, inner))
    modal_params = jnp.where(
        half == 0, jnp.concatenate([mine, theirs]), jnp.concatenate([theirs, mine])
    )
    modal = jnp.repeat(modal_params.T, chunks, axis=1)
    conv, message = run_first(which, modal, modal_params[:, :MODES], xt, *inner)
    other = lax.ppermute(message, "seq", across)
    back, sums = run_second(which, message, other, taps, modal, xt, hat, conv)
    paired = back.reshape(chunks, ROWS_OUT // 4, 4, back.shape[1])
    final = lax.all_to_all(paired, "seq", 0, 0, tiled=True, axis_index_groups=groups)
    output, grad_query, grad_key, grad_value, grad_short = run_unpack(final.reshape(back.shape))
    own_modal = lax.dynamic_slice(sums, (4 * half, 0), (4, 2 * MODES))
    return (
        output,
        grad_query,
        grad_key,
        grad_value,
        grad_short,
        own_modal[:, :MODES],
        own_modal[:, MODES:],
    )


def solution(mesh):
    return jax.shard_map(
        local,
        mesh=mesh,
        in_specs=(
            P("chan", "seq"),
            P("chan", "seq"),
            P("chan", "seq"),
            P(None, None, "chan"),
            P(("chan", "seq"), None),
            P(("chan", "seq"), None),
            P("chan", "seq"),
        ),
        out_specs=(
            P("chan", "seq"),
            P("chan", "seq"),
            P("chan", "seq"),
            P("chan", "seq"),
            P(None, None, "chan"),
            P(("chan", "seq"), None),
            P(("chan", "seq"), None),
        ),
        check_vma=False,
    )
```
